128 devices in a mesh: heads: 4 (over y), tower: 2 (over z_lo), blk: 16 (over z_hi, x, core).
Axes of the slice: x: 4, y: 4, z: 4 (z_hi: 2, z_lo: 2; z = z_hi * 2 + z_lo), core: 2. Of those that a mesh axis runs over, the one named last changes fastest.
Arguments:
- query_input: bfloat16 [6144, 3584], P(('tower', 'blk'), 'heads'), may hold values from -6 to 6
- key_input: bfloat16 [6144, 512], P(('tower', 'blk'), 'heads'), may hold values from -6 to 6
- value_input: bfloat16 [6144, 512], P(('tower', 'blk'), 'heads'), may hold values from -6 to 6
- output_grad: bfloat16 [6144, 3584], P(('tower', 'blk'), 'heads'), may hold values from -6 to 6
- query_gain: float32 [2, 128], P('tower'), may hold values from 0.6 to 5
- key_gain: float32 [2, 128], P('tower'), may hold values from 0.6 to 5
- stripe_order: int32 [96], replicated, may hold values from 0 to 95, each once
- frame_index: int32 [48], replicated, may hold values from 0 to 11, never falling along the last dimension, each value on 1 to 8 neighbouring positions
- cross_blocks: int32 [96, 96], replicated, may hold values 0 or 1
Outputs:
- query_grad: bfloat16 [6144, 3584], P(('tower', 'blk'), 'heads')
- key_grad: bfloat16 [6144, 512], P(('tower', 'blk'), 'heads')
- value_grad: bfloat16 [6144, 512], P(('tower', 'blk'), 'heads')
- gain_grads: float32 [2, 2, 128], P(None, 'tower')
The draws below stay inside these ranges and needn't reach their ends.
All inputs are finite; a program needn't handle non-finite values.
Results may differ from the reference program's by a relative error of at most 0.02.
The reference program's roundings to bfloat16 on the way count: a program that leaves them out, or rounds other values in their place, can miss the bound.
Values may be sent and summed in bfloat16 or wider, within the bound.
A program may use at most 64 MiB of HBM per device.

```python
import math
import jax
import jax.numpy as jnp
import numpy as np
from jax import lax

HEAD_DIM = 128
QUERY_HEADS = 7
KV_HEADS = 4
SEGMENT = 64
LENGTH = 6144
SEGMENTS = 96
FRAMES = 12


def drawn_rows(key):
    base = jax.random.fold_in(key, 7)
    queries = jax.random.normal(jax.random.fold_in(base, 1), (LENGTH, KV_HEADS * QUERY_HEADS * HEAD_DIM), jnp.float32)
    keys = jax.random.normal(jax.random.fold_in(base, 2), (LENGTH, KV_HEADS * HEAD_DIM), jnp.float32)
    return (jnp.clip(queries, -6.0, 6.0), jnp.clip(keys, -6.0, 6.0))


def draw_query_input(key, part):
    return drawn_rows(key)[0].astype(jnp.bfloat16)


def draw_key_input(key, part):
    return drawn_rows(key)[1].astype(jnp.bfloat16)


def draw_query_gain(key, part):
    return jax.random.uniform(jax.random.fold_in(key, 21), (2, HEAD_DIM), jnp.float32, 0.6, 1.6)


def draw_key_gain(key, part):
    return jax.random.uniform(jax.random.fold_in(key, 22), (2, HEAD_DIM), jnp.float32, 0.6, 1.6)


def set_ends(entries, stream_key, least, top_value):
    longest = entries.shape.index(max(entries.shape))
    spots = []
    for shift in (0, 1):
        where = [jax.random.randint(jax.random.fold_in(stream_key, axis), (), 0, length) for axis, length in enumerate(entries.shape)]
        where[longest] = (where[longest] + shift) % entries.shape[longest]
        spots.append(tuple(where))
    return entries.at[spots[0]].set(least).at[spots[1]].set(top_value)


def block_scale(stream_key, dims, split, low, top_value):
    def one(axis_at, blocks):
        heights = jax.random.uniform(jax.random.fold_in(jax.random.fold_in(stream_key, 6), axis_at), (blocks,), jnp.float32, low / len(split), top_value / len(split))
        return jnp.repeat(jnp.exp(heights), dims[axis_at] // blocks).reshape((-1,) + (1,) * (len(dims) - axis_at - 1))

    level = one(*split[0])
    for cut in split[1:]:
        level = level * one(*cut)
    return level


def length_profile(number_of, total, limit, skew):
    loads = [(1 << 20) // math.isqrt(grade ** skew) + 1 for grade in range(2, number_of + 1)]
    spare, holding = total - limit - (number_of - 1), [1] * (number_of - 1)
    while spare > 0:
        movable = [i for i in range(number_of - 1) if holding[i] < limit]
        whole, budget = sum([loads[i] for i in movable]), spare
        for i in movable:
            extra = min(limit - holding[i], max(1, budget * loads[i] // whole), spare)
            holding[i] = holding[i] + extra
            spare = spare - extra
    return np.array([limit] + holding)


def uneven_parts(rng, number_of, total, limit, lean):
    if number_of == 2:
        one = jax.random.randint(rng, (), max(1, total - limit), min(limit, total - 1) + 1)
        return jnp.stack([one, total - one])
    sizes = jnp.asarray(length_profile(number_of, total, limit, lean), jnp.int32)
    twos = (number_of - 1) // 2
    donor, sink = sizes[1:1 + 2 * twos:2], sizes[2:2 + 2 * twos:2]
    margin = jnp.minimum(donor - 1, limit - sink)
    passed = jax.random.randint(jax.random.fold_in(rng, 1), (twos,), 0, 1 << 20) % (margin + 1)
    sizes = sizes.at[1:1 + 2 * twos:2].set(donor - passed).at[2:2 + 2 * twos:2].set(sink + passed)
    return sizes[jax.random.permutation(jax.random.fold_in(rng, 2), number_of)]


def normal_values(own_key, shape, spread, most, pieces=(), held_as=jnp.bfloat16):
    result = jax.random.normal(own_key, shape, jnp.float32) * spread
    if len(pieces) > 0:
        result = block_scale(own_key, shape, pieces, -0.22, 0.18) * result
    return jnp.clip(result, min=-most, max=most).astype(held_as)


def setup_inputs(seed: int = 0) -> dict:
    key_of = jax.random.split(jax.random.key(seed), 10)
    query_input = draw_query_input(jax.random.fold_in(key_of[9], 71), 0)
    key_input = draw_key_input(jax.random.fold_in(key_of[9], 71), 0)
    value_input = normal_values(key_of[2], (LENGTH, KV_HEADS * HEAD_DIM), 1.0, 6.0, ((0, 32), (1, 4)))
    output_grad = normal_values(key_of[3], (LENGTH, KV_HEADS * QUERY_HEADS * HEAD_DIM), 1.0, 6.0, ((0, 32), (1, 4)))
    query_gain = draw_query_gain(jax.random.fold_in(key_of[9], 71), 0)
    key_gain = draw_key_gain(jax.random.fold_in(key_of[9], 71), 0)
    stripe_order = jax.random.permutation(key_of[6], SEGMENTS).astype(jnp.int32)
    frame_index = jnp.searchsorted(jnp.cumsum(uneven_parts(key_of[7], FRAMES, SEGMENTS // 2, 8, 0)), jnp.arange(SEGMENTS // 2), side="right").astype(jnp.int32)
    cross_blocks = set_ends((jax.random.randint(key_of[8], (SEGMENTS, SEGMENTS), 0, 2) < 1).astype(jnp.int32), jax.random.fold_in(key_of[8], 1), 0, 1)
    return {"query_input": query_input, "key_input": key_input, "value_input": value_input, "output_grad": output_grad, "query_gain": query_gain, "key_gain": key_gain, "stripe_order": stripe_order, "frame_index": frame_index, "cross_blocks": cross_blocks}


EPSILON = 1e-06
NEGATIVE = -1e+30

def row_order(stripe_order, first, count, seg_len):
    slots = lax.dynamic_slice_in_dim(stripe_order, first, count)
    return (slots[:, None] * seg_len + jnp.arange(seg_len, dtype=jnp.int32)[None, :]).reshape(-1)

def allowed_pairs(query_first, query_segs, key_first, key_segs, stripe_order, frame_all, cross_blocks, seg_len):
    half_segs = stripe_order.shape[0] // 2
    query_first = jnp.asarray(query_first, jnp.int32)
    key_first = jnp.asarray(key_first, jnp.int32)
    query_place = row_order(stripe_order, query_first, query_segs, seg_len).reshape(query_segs, seg_len, 1, 1)
    key_place = row_order(stripe_order, key_first, key_segs, seg_len).reshape(1, 1, key_segs, seg_len)
    query_frame = lax.dynamic_slice_in_dim(frame_all, query_first, query_segs)
    key_frame = lax.dynamic_slice_in_dim(frame_all, key_first, key_segs)
    same_frame = (query_frame[:, None] == key_frame[None, :]) & (query_frame[:, None] >= 0)
    query_image = query_first + jnp.arange(query_segs, dtype=jnp.int32) >= half_segs
    key_image = key_first + jnp.arange(key_segs, dtype=jnp.int32) >= half_segs
    opened = lax.dynamic_slice(cross_blocks, (query_first, key_first), (query_segs, key_segs)) == 1
    segment_open = (query_image[:, None] == key_image[None, :]) | opened
    allowed = ((key_place <= query_place) | same_frame[:, None, :, None]) & segment_open[:, None, :, None]
    return allowed.reshape(query_segs * seg_len, key_segs * seg_len)

def rounded(values):
    return lax.optimization_barrier(values.astype(jnp.bfloat16)).astype(jnp.float32)

def unit_rows(raw, gain):
    values = raw.astype(jnp.float32)
    inverse = lax.rsqrt(lax.optimization_barrier(jnp.mean(values * values, axis=-1, keepdims=True)) + EPSILON)
    unit = values * inverse
    return (unit, inverse, (unit * gain).astype(jnp.bfloat16))

def unit_grad(grad, unit, inverse, gain):
    scaled = grad * gain
    return inverse * (scaled - unit * lax.optimization_barrier(jnp.mean(scaled * unit, axis=-1, keepdims=True)))

def reference(query_input, key_input, value_input, output_grad, query_gain, key_gain, stripe_order, frame_index, cross_blocks):
    length = query_input.shape[0]
    half = length // 2
    scale = 1.0 / math.sqrt(HEAD_DIM)
    second = jnp.arange(length, dtype=jnp.int32) >= half
    query_rows = jnp.where(second[:, None], query_gain[1][None, :], query_gain[0][None, :])
    key_rows = jnp.where(second[:, None], key_gain[1][None, :], key_gain[0][None, :])
    q_unit, q_inverse, q_normed = unit_rows(query_input.reshape(length, KV_HEADS, QUERY_HEADS, HEAD_DIM), query_rows[:, None, None, :])
    k_unit, k_inverse, k_normed = unit_rows(key_input.reshape(length, KV_HEADS, HEAD_DIM), key_rows[:, None, :])
    value_rows = value_input.reshape(length, KV_HEADS, HEAD_DIM)
    grad_rows = output_grad.reshape(length, KV_HEADS, QUERY_HEADS, HEAD_DIM)
    frame_all = jnp.concatenate([jnp.full((SEGMENTS // 2,), -1, jnp.int32), frame_index.astype(jnp.int32)])
    query_block = math.gcd(length, 512)
    block_segs = query_block // SEGMENT
    grads_q = []
    grads_k = []
    grads_v = []
    for group in range(KV_HEADS):
        keys = k_normed[:, group].astype(jnp.float32)
        values = value_rows[:, group].astype(jnp.float32)
        queries_all = q_normed[:, group]
        douts_all = grad_rows[:, group]

        def block_step(carry, index):
            grad_k, grad_v = carry
            begin = index * query_block
            queries = lax.dynamic_slice_in_dim(queries_all, begin, query_block).astype(jnp.float32)
            douts = lax.dynamic_slice_in_dim(douts_all, begin, query_block).astype(jnp.float32)
            allowed = allowed_pairs(begin // SEGMENT, block_segs, 0, SEGMENTS, stripe_order, frame_all, cross_blocks, SEGMENT)[:, None, :]
            logits = jnp.where(allowed, jnp.einsum('rhd,kd->rhk', queries, keys) * scale, NEGATIVE)
            top = lax.optimization_barrier(jnp.max(logits, axis=-1))
            weights = jnp.exp(logits - top[..., None])
            total = lax.optimization_barrier(jnp.sum(weights, axis=-1))
            output = rounded(jnp.einsum('rhk,kd->rhd', rounded(weights), values) / total[..., None])
            lse = top + jnp.log(total)
            delta = lax.optimization_barrier(jnp.sum(douts * output, axis=-1))
            probs = jnp.exp(logits - lse[..., None])
            pushes = jnp.einsum('rhd,kd->rhk', douts, values)
            slopes = rounded(probs * (pushes - delta[..., None]))
            grad_q = jnp.einsum('rhk,kd->rhd', slopes, keys) * scale
            grad_k = grad_k + jnp.einsum('rhk,rhd->kd', slopes, queries) * scale
            grad_v = grad_v + jnp.einsum('rhk,rhd->kd', rounded(probs), douts)
            return ((grad_k, grad_v), grad_q)
        zeros = jnp.zeros((length, HEAD_DIM), jnp.float32)
        (grad_k, grad_v), grad_q = lax.scan(block_step, (zeros, zeros), jnp.arange(length // query_block, dtype=jnp.int32))
        grads_q.append(grad_q.reshape(length, QUERY_HEADS, HEAD_DIM))
        grads_k.append(grad_k)
        grads_v.append(grad_v)
    grad_qn = jnp.stack(grads_q, axis=1)
    grad_kn = jnp.stack(grads_k, axis=1)
    grad_value = jnp.stack(grads_v, axis=1)
    query_grad = unit_grad(grad_qn, q_unit, q_inverse, query_rows[:, None, None, :])
    key_grad = unit_grad(grad_kn, k_unit, k_inverse, key_rows[:, None, :])
    q_terms = lax.optimization_barrier(jnp.sum(grad_qn * q_unit, axis=(1, 2))).reshape(2, half, HEAD_DIM).sum(axis=1)
    k_terms = lax.optimization_barrier(jnp.sum(grad_kn * k_unit, axis=1)).reshape(2, half, HEAD_DIM).sum(axis=1)
    gain_grads = jnp.stack([q_terms, k_terms])
    return (query_grad.reshape(length, -1).astype(jnp.bfloat16), key_grad.reshape(length, -1).astype(jnp.bfloat16), grad_value.reshape(length, -1).astype(jnp.bfloat16), gain_grads)
```

```python
import functools
import math

import jax
import jax.numpy as jnp
from jax import lax
from jax.experimental import pallas as pl
from jax.experimental.pallas import tpu as pltpu
from jax.sharding import Mesh
from jax.sharding import PartitionSpec as P

SEGMENT = 64
AXES = ("heads", "tower", "blk_0", "blk_1", "blk_2")
TOWER_BLK = ("tower", "blk_0", "blk_1", "blk_2")
EPSILON = 1e-06
NEGATIVE = -1e30
LOG2E = 1.4426950408889634
MESH = pl.DeviceIdType.MESH
VMEM = pltpu.VMEM
DMA = pltpu.SemaphoreType.DMA
F32, BF16, I32 = jnp.float32, jnp.bfloat16, jnp.int32


def dot(a, b, left, right):
    return lax.dot_general(a, b, (((left,), (right,)), ((), ())), preferred_element_type=F32)


def position():
    z = lax.axis_index("blk_0") * 2 + lax.axis_index("tower")
    return lax.axis_index("heads"), lax.axis_index("blk_1"), z, lax.axis_index("blk_2")


def device(y, x, z, core):
    return (y, lax.rem(z, 2), lax.div(z, 2), x, core)


def place_of(x, z, core):
    return lax.rem(z, 2) * 16 + lax.div(z, 2) * 8 + x * 2 + core


def shifted(x, z, core, first, second):
    nx = lax.rem(x + (1 - core) * first + core * second, 4)
    nz = lax.rem(z + core * first + (1 - core) * second, 4)
    return nx, nz


def remote(src, dst, send, recv, target):
    return pltpu.make_async_remote_copy(
        src_ref=src, dst_ref=dst, send_sem=send, recv_sem=recv, device_id=target, device_id_type=MESH
    )


def meet(targets):
    barrier = pltpu.get_barrier_semaphore()
    for target in targets:
        pl.semaphore_signal(barrier, inc=1, device_id=target, device_id_type=MESH)
    return lambda: pl.semaphore_wait(barrier, len(targets))


def gather_kernel(
    key_ref, value_ref, gain_ref, order_ref, frame_ref, cross_ref, all_ref, list_ref,
    mine, own_sem, send_a, recv_a, send_b, recv_b, send_s, recv_s,
):
    y, x, z, core = position()

    def target(first, second):
        nx, nz = shifted(x, z, core, first, second)
        return device(y, nx, nz, core)

    def chunk(first, second):
        nx, nz = shifted(x, z, core, first, second)
        return place_of(nx, nz, core)

    sibling = device(y, x, z, 1 - core)
    ring_a = (target(1, 0), target(3, 0))
    ring_b = (target(0, 1), target(0, 3))
    wait_all = meet((*ring_a, *ring_b, sibling))
    keys = key_ref[...].astype(F32)
    inverse = lax.rsqrt(jnp.mean(keys * keys, axis=-1, keepdims=True) + EPSILON)
    mine[0] = (keys * inverse * gain_ref[...]).astype(BF16)
    mine[1] = value_ref[...]
    me = place_of(x, z, core)
    own = pltpu.make_async_copy(mine, all_ref.at[me], own_sem)
    started = []

    def send(src, dst, send_sem, recv_sem, to):
        copy = remote(src, dst, send_sem, recv_sem, to)
        copy.start()
        started.append(copy)

    def arrived(dst, recv_sem):
        remote(dst, dst, send_s.at[0], recv_sem, sibling).wait_recv()

    def spread(first, src):
        at = all_ref.at[chunk(first, 0)]
        send(src, at, send_b.at[first, 0], recv_b.at[first, 1], ring_b[0])
        send(src, at, send_b.at[first, 1], recv_b.at[first, 0], ring_b[1])

    def share(first, second, src):
        n = first * 4 + second
        send(src, all_ref.at[chunk(first, second)], send_s.at[n], recv_s.at[n], sibling)

    wait_all()
    own.start()
    send(mine, all_ref.at[me], send_a.at[0], recv_a.at[1], ring_a[0])
    send(mine, all_ref.at[me], send_a.at[1], recv_a.at[0], ring_a[1])
    spread(0, mine)
    share(0, 0, mine)

    lane = lax.broadcasted_iota(I32, (1, 128), 1)
    down = lax.broadcasted_iota(I32, (128, 128), 0)
    across = lax.broadcasted_iota(I32, (128, 128), 1)
    order, frame = order_ref[...], frame_ref[...]
    below = (across < down).astype(F32)
    start_of = (lax.shift_right_logical(down * 171, 9) * 384 + (down - 3 * lax.shift_right_logical(down * 171, 9)) * 64)
    image = me >= 16
    list_ref[...] = jnp.zeros_like(list_ref)
    counts = jnp.where(lane == 3, jnp.where(image, 0, 1), 0)
    for b in range(3):
        block = me * 3 + b
        here = lane == block
        slot = jnp.sum(jnp.where(here, order, 0), axis=-1, keepdims=True)
        seen = jnp.sum(jnp.where(here, frame, 0), axis=-1, keepdims=True)
        same = (lane >= 48) == image
        near = (order <= slot) | ((frame == seen) & (seen >= 0))
        opened = same | (cross_ref[pl.ds(block, 1), :] == 1)
        others = (near & opened & (lane < 96) & (lane != block)).astype(F32)
        column = jnp.broadcast_to(others, (128, 128)).T
        at = dot(below, column, 1, 0).astype(I32) + 1
        chosen = (column > 0.5) & (at == across)
        listed = jnp.sum(jnp.where(chosen, start_of, 0), axis=0, keepdims=True)
        first_start = me * 384 + b * 64
        list_ref[b : b + 1, :] = jnp.where(lane == 0, first_start, listed)
        count = 1 + jnp.sum(others, axis=-1, keepdims=True).astype(I32)
        counts = jnp.where(lane == b, count, counts)
    list_ref[3:4, :] = counts

    def from_a(slot, first, half, to, forward_recv):
        at = all_ref.at[chunk(first, 0)]
        arrived(at, recv_a.at[slot])
        send(at.at[half], at.at[half], send_a.at[2 + half], recv_a.at[forward_recv], to)
        spread(first, at)
        share(first, 0, at)

    def from_b(first, slot, second, half, to):
        at = all_ref.at[chunk(first, second)]
        arrived(at, recv_b.at[first, slot])
        send(at.at[half], at.at[half], send_b.at[first, 2 + half], recv_b.at[first, 2 + half], to)
        share(first, second, at)

    def both_b(first):
        from_b(first, 0, 1, 0, ring_b[1])
        from_b(first, 1, 3, 1, ring_b[0])

    from_a(0, 1, 0, ring_a[1], 2)
    from_a(1, 3, 1, ring_a[0], 3)
    both_b(0)
    at = all_ref.at[chunk(2, 0)]
    arrived(at.at[0], recv_a.at[2])
    arrived(at.at[1], recv_a.at[3])
    spread(2, at)
    share(2, 0, at)
    both_b(1)
    both_b(3)
    both_b(2)
    for first in (0, 1, 3, 2):
        at = all_ref.at[chunk(first, 2)]
        arrived(at.at[0], recv_b.at[first, 2])
        arrived(at.at[1], recv_b.at[first, 3])
        share(first, 2, at)
    own.wait()
    for copy in started:
        copy.wait_send()
    for n in range(16):
        nx, nz = shifted(x, z, 1 - core, n // 4, n % 4)
        arrived(all_ref.at[place_of(nx, nz, 1 - core)], recv_s.at[n])


def gathered(key_input, value_input, key_gain, order, frame, cross):
    rows, dim = key_input.shape
    whole = pl.BlockSpec(memory_space=VMEM)
    return pl.pallas_call(
        gather_kernel,
        out_shape=(jax.ShapeDtypeStruct((32, 2, rows, dim), BF16), jax.ShapeDtypeStruct((8, 128), I32)),
        in_specs=[whole] * 6,
        out_specs=(pl.BlockSpec(memory_space=pl.ANY), whole),
        scratch_shapes=[
            VMEM((2, rows, dim), BF16), DMA, DMA((4,)), DMA((4,)), DMA((4, 4)), DMA((4, 4)), DMA((16,)), DMA((16,)),
        ],
        compiler_params=pltpu.CompilerParams(collective_id=0, has_side_effects=True),
        name="gather_keys",
    )(key_input, value_input, key_gain, order, frame, cross)


def attention_kernel(
    per_group, blocks, width, list_ref, query_ref, grad_ref, gain_ref, kv_ref,
    out_ref, gain_out, part_ref,
    qn, dop, s_ref, w_ref, m_ref, l_ref, o_ref, dq_ref, acc,
):
    dim = 128
    rows = SEGMENT * per_group
    per = width // SEGMENT
    log_scale = LOG2E / math.sqrt(dim)
    scale = 1.0 / math.sqrt(dim)
    places = kv_ref.shape[0] // 384
    is_text = list_ref[3, 3] == 1
    gain = gain_ref[...]

    def zero(i, _):
        acc[pl.ds(pl.multiple_of(i * 128, 128), 128), :] = jnp.zeros((128, dim), F32)
        return 0

    lax.fori_loop(0, places * 3, zero, 0)
    query_part = jnp.zeros((8, dim), F32)

    for b in range(blocks):
        count = list_ref[3, b]
        rest = lax.rem(count - 1, per)
        groups = lax.div(count - 1, per)
        for h in range(per_group):
            q = query_ref[b * SEGMENT : (b + 1) * SEGMENT, h * dim : (h + 1) * dim].astype(F32)
            inverse = lax.rsqrt(jnp.mean(q * q, axis=-1, keepdims=True) + EPSILON)
            qn[h * SEGMENT : (h + 1) * SEGMENT, :] = (q * inverse * gain).astype(BF16)
        m_ref[...] = jnp.full_like(m_ref, NEGATIVE)
        l_ref[...] = jnp.zeros_like(l_ref)
        o_ref[...] = jnp.zeros_like(o_ref)
        dq_ref[...] = jnp.zeros_like(dq_ref)

        def starts(g):
            out = []
            for j in range(per):
                if isinstance(g, int):
                    p = 0 if j == 0 else jnp.where(j <= rest, j, 0)
                else:
                    p = 1 + rest + (g - 1) * per + j
                out.append(pl.multiple_of(list_ref[b, p], SEGMENT))
            return out

        def tile(at, offset):
            return jnp.concatenate([kv_ref[pl.ds(s + offset, SEGMENT), :] for s in at], axis=0)

        def logits(g, at, masked):
            s = dot(qn[...], tile(at, 0), 1, 1)
            if masked:
                lane = lax.broadcasted_iota(I32, (rows, width), 1)
                row = lax.broadcasted_iota(I32, (rows, width), 0)
                limit = lax.rem(row, SEGMENT) + jnp.where(is_text, 0, SEGMENT)
                ok = (lane < (rest + 1) * SEGMENT) & ((lane >= SEGMENT) | (lane <= limit))
                s = jnp.where(ok, s, NEGATIVE)
            s_ref[g] = s
            top = m_ref[...]
            for t in range(width // 128):
                top = jnp.maximum(top, s[:, t * 128 : (t + 1) * 128])
            m_ref[...] = top

        def weights(g, at):
            top = m_ref[...]
            total = l_ref[...]
            parts = []
            for t in range(width // 128):
                w = jnp.exp2((s_ref[g, :, t * 128 : (t + 1) * 128] - top) * log_scale)
                total = total + w
                parts.append(w.astype(BF16))
            l_ref[...] = total
            w = jnp.concatenate(parts, axis=1)
            w_ref[g] = w
            o_ref[...] += dot(w, tile(at, 192), 1, 0)

        def slopes(g, at):
            keys = tile(at, 0)
            pushes = dot(dop[...], tile(at, 192), 1, 1)
            delta = m_ref[...]
            w = w_ref[g]
            parts = []
            for t in range(width // 128):
                sl = slice(t * 128, (t + 1) * 128)
                parts.append((w[:, sl].astype(F32) * (pushes[:, sl] - delta)).astype(BF16))
            ds = jnp.concatenate(parts, axis=1)
            dq_ref[...] += dot(ds, keys, 1, 0)
            dk = dot(ds, qn[...], 0, 0)
            dv = dot(w, dop[...], 0, 0)
            for j in range(per):
                sl = slice(j * SEGMENT, (j + 1) * SEGMENT)
                acc[pl.ds(at[j], SEGMENT), :] += dk[sl]
                acc[pl.ds(at[j] + 192, SEGMENT), :] += dv[sl]

        def over(step):
            def body(g, _):
                step(g, starts(g))
                return 0

            lax.fori_loop(1, groups + 1, body, 0)

        logits(0, starts(0), True)
        over(lambda g, at: logits(g, at, False))
        m_ref[...] = jnp.broadcast_to(jnp.max(m_ref[...], axis=-1, keepdims=True), m_ref.shape)
        weights(0, starts(0))
        over(weights)
        total = jnp.sum(l_ref[...], axis=-1, keepdims=True)
        over_total = 1.0 / total
        output = (o_ref[...] / total).astype(BF16).astype(F32)
        for h in range(per_group):
            sl = slice(h * SEGMENT, (h + 1) * SEGMENT)
            g = grad_ref[b * SEGMENT : (b + 1) * SEGMENT, h * dim : (h + 1) * dim].astype(F32)
            g = (g * over_total[sl]).astype(BF16)
            dop[sl, :] = g
            delta = jnp.sum(g.astype(F32) * output[sl], axis=-1, keepdims=True)
            m_ref[sl, :] = jnp.broadcast_to(delta, (SEGMENT, 128))
        slopes(0, starts(0))
        over(slopes)
        for h in range(per_group):
            sl = slice(h * SEGMENT, (h + 1) * SEGMENT)
            q = query_ref[b * SEGMENT : (b + 1) * SEGMENT, h * dim : (h + 1) * dim].astype(F32)
            inverse = lax.rsqrt(jnp.mean(q * q, axis=-1, keepdims=True) + EPSILON)
            unit = q * inverse
            grad = dq_ref[sl, :] * scale
            e = grad * gain
            dq = inverse * (e - unit * jnp.mean(e * unit, axis=-1, keepdims=True))
            out_ref[b * SEGMENT : (b + 1) * SEGMENT, h * dim : (h + 1) * dim] = dq.astype(BF16)
            query_part = query_part + jnp.sum((grad * unit).reshape(SEGMENT // 8, 8, dim), axis=0)

    def finish(i, part):
        at = pl.multiple_of(i * 384, 384)
        mine = acc[pl.ds(at, 384), :]
        part_ref[i, 0] = mine[:192].astype(BF16)
        part_ref[i, 1] = mine[192:].astype(BF16)
        terms = mine[:192] * kv_ref[pl.ds(at, 192), :].astype(F32)
        return part + jnp.sum(terms.reshape(24, 8, dim), axis=0)

    text = lax.fori_loop(0, places // 2, finish, jnp.zeros((8, dim), F32))
    image = lax.fori_loop(places // 2, places, finish, jnp.zeros((8, dim), F32))
    query_sum = jnp.sum(query_part, axis=0, keepdims=True)
    row = lax.broadcasted_iota(I32, (8, dim), 0)
    filled = jnp.where(row == jnp.where(is_text, 0, 1), query_sum, 0.0)
    filled = jnp.where(row == 2, jnp.sum(text, axis=0, keepdims=True), filled)
    gain_out[...] = jnp.where(row == 3, jnp.sum(image, axis=0, keepdims=True), filled)


def attention(lists, query_input, output_grad, query_gain, kv, width):
    rows, columns = query_input.shape
    per_group = columns // 128
    stacked = SEGMENT * per_group
    segments = kv.shape[0] * 3
    per = width // SEGMENT
    groups = (segments + per - 1) // per + 1
    flat = kv.shape[0] * 384
    whole = pl.BlockSpec(memory_space=VMEM)
    return pl.pallas_call(
        functools.partial(attention_kernel, per_group, rows // SEGMENT, width),
        out_shape=(
            jax.ShapeDtypeStruct((rows, columns), BF16),
            jax.ShapeDtypeStruct((8, 128), F32),
            jax.ShapeDtypeStruct(kv.shape, BF16),
        ),
        in_specs=[pl.BlockSpec(memory_space=pltpu.SMEM)] + [whole] * 4,
        out_specs=(whole,) * 3,
        scratch_shapes=[
            VMEM((stacked, 128), BF16), VMEM((stacked, 128), BF16),
            VMEM((groups, stacked, width), F32), VMEM((groups, stacked, width), BF16),
            VMEM((stacked, 128), F32), VMEM((stacked, 128), F32), VMEM((stacked, 128), F32), VMEM((stacked, 128), F32),
            VMEM((flat, 128), F32),
        ],
        compiler_params=pltpu.CompilerParams(vmem_limit_bytes=60 * 1024 * 1024),
        name="attention",
    )(lists, query_input, output_grad, query_gain, kv.reshape(flat, 128))


def reduce_kernel(
    part_ref, gain_part, key_ref, gain_ref, key_out, value_out, gain_out,
    sib, work, half_b, full_b, half_a, full_a, sums,
    send_s, recv_s, send_hb, recv_hb, send_fb, recv_fb, send_a, recv_a, send_g, recv_g,
):
    y, x, z, core = position()
    scale = 1.0 / math.sqrt(128)

    def target(first, second):
        nx, nz = shifted(x, z, core, first, second)
        return device(y, nx, nz, core)

    sibling = device(y, x, z, 1 - core)
    ring_a = (target(1, 0), target(3, 0))
    ring_b = (target(0, 1), target(0, 3))
    lines = (
        (y, 4, lambda n: device(n, x, z, core)),
        (core, 2, lambda n: device(y, x, z, n)),
        (x, 4, lambda n: device(y, n, z, core)),
        (z, 4, lambda n: device(y, x, n, core)),
    )
    peers = [sibling]
    for at, size, of in lines[:1] + lines[2:]:
        peers += [of(lax.rem(at + o, size)) for o in range(1, size)]
    meet(peers)()
    started = []

    def send(src, dst, send_sem, recv_sem, to):
        copy = remote(src, dst, send_sem, recv_sem, to)
        copy.start()
        started.append(copy)

    def arrived(dst, recv_sem):
        remote(dst, dst, send_s.at[0], recv_sem, sibling).wait_recv()

    def gain_send(stage, value):
        at, size, of = lines[stage]
        sums[stage, at] = value
        for o in range(1, size):
            send(sums.at[stage, at], sums.at[stage, at], send_g.at[stage, o], recv_g.at[stage, at], of(lax.rem(at + o, size)))

    def gain_sum(stage):
        at, size, of = lines[stage]
        for o in range(1, size):
            n = lax.rem(at + o, size)
            arrived(sums.at[stage, n], recv_g.at[stage, n])
        total = sums[stage, 0]
        for n in range(1, size):
            total = total + sums[stage, n]
        return total

    visit = [(first, second) for second in (2, 1, 3, 0) for first in (2, 1, 3, 0)]
    for first, second in visit:
        nx, nz = shifted(x, z, 1 - core, first, second)
        n = first * 4 + second
        send(part_ref.at[place_of(nx, nz, 1 - core)], sib.at[first, second], send_s.at[n], recv_s.at[n], sibling)
    gain_send(0, gain_part[...])

    def combine(first, second):
        n = first * 4 + second
        arrived(sib.at[first, second], recv_s.at[n])
        nx, nz = shifted(x, z, core, first, second)
        return part_ref[place_of(nx, nz, core)].astype(F32) + sib[first, second].astype(F32)

    for first in (2, 1, 3, 0):
        work[first, 2] = combine(first, 2).astype(BF16)
        for half in (0, 1):
            send(work.at[first, 2, half], half_b.at[first, half], send_hb.at[first, half], recv_hb.at[first, half], ring_b[half])
    gain_send(1, gain_sum(0))
    for first in (2, 1, 3, 0):
        for half, second in ((0, 1), (1, 3)):
            mine = combine(first, second)
            arrived(half_b.at[first, half], recv_hb.at[first, half])
            work[first, second] = mine.astype(BF16)
            work[first, second, half] = (mine[half] + half_b[first, half].astype(F32)).astype(BF16)
            send(work.at[first, second], full_b.at[first, half], send_fb.at[first, half], recv_fb.at[first, half], ring_b[half])
    gain_send(2, gain_sum(1))

    def settled(first):
        mine = combine(first, 0)
        for half in (0, 1):
            arrived(full_b.at[first, half], recv_fb.at[first, half])
            mine = mine + full_b[first, half].astype(F32)
        return mine

    work[2, 0] = settled(2).astype(BF16)
    for half in (0, 1):
        send(work.at[2, 0, half], half_a.at[half], send_a.at[half], recv_a.at[half], ring_a[half])
    gain_send(3, gain_sum(2))
    for half, first in ((0, 1), (1, 3)):
        mine = settled(first)
        arrived(half_a.at[half], recv_a.at[half])
        work[first, 0] = mine.astype(BF16)
        work[first, 0, half] = (mine[half] + half_a[half].astype(F32)).astype(BF16)
        send(work.at[first, 0], full_a.at[half], send_a.at[2 + half], recv_a.at[2 + half], ring_a[half])
    mine = settled(0)
    totals = gain_sum(3)
    gain = gain_ref[...]
    tower = lax.rem(z, 2)
    row = lax.broadcasted_iota(I32, (8, 128), 0)
    query_sum = jnp.sum(jnp.where(row == tower, totals, 0.0), axis=0, keepdims=True)
    key_sum = jnp.sum(jnp.where(row == 2 + tower, totals, 0.0), axis=0, keepdims=True)
    gain_out[0:1, :] = query_sum
    gain_out[1:2, :] = key_sum * scale / gain
    for half in (0, 1):
        arrived(full_a.at[half], recv_a.at[2 + half])
        mine = mine + full_a[half].astype(F32)
    value_out[...] = mine[1].astype(BF16)
    keys = key_ref[...].astype(F32)
    inverse = lax.rsqrt(jnp.mean(keys * keys, axis=-1, keepdims=True) + EPSILON)
    unit = keys * inverse
    e = mine[0] * scale * gain
    key_out[...] = (inverse * (e - unit * jnp.mean(e * unit, axis=-1, keepdims=True))).astype(BF16)
    for copy in started:
        copy.wait_send()


def reduced(part, gain_part, key_input, key_gain):
    rows, dim = key_input.shape
    whole = pl.BlockSpec(memory_space=VMEM)
    one = (2, rows, dim)
    return pl.pallas_call(
        reduce_kernel,
        out_shape=(
            jax.ShapeDtypeStruct((rows, dim), BF16),
            jax.ShapeDtypeStruct((rows, dim), BF16),
            jax.ShapeDtypeStruct((2, dim), F32),
        ),
        in_specs=[whole] * 4,
        out_specs=(whole,) * 3,
        scratch_shapes=[
            VMEM((4, 4, *one), BF16), VMEM((4, 4, *one), BF16), VMEM((4, *one), BF16), VMEM((4, 2, *one), BF16),
            VMEM(one, BF16), VMEM((2, *one), BF16), VMEM((4, 4, 8, dim), F32),
            DMA((16,)), DMA((16,)), DMA((4, 2)), DMA((4, 2)), DMA((4, 2)), DMA((4, 2)), DMA((4,)), DMA((4,)),
            DMA((4, 4)), DMA((4, 4)),
        ],
        compiler_params=pltpu.CompilerParams(collective_id=1, has_side_effects=True),
        name="reduce_keys",
    )(part, gain_part, key_input, key_gain)


def shards(
    query_input, key_input, value_input, output_grad, query_gain, key_gain, stripe_order, frame_index, cross_blocks
):
    order = jnp.pad(stripe_order, (0, 32))[None]
    frame = jnp.pad(frame_index, (48, 32), constant_values=-1)[None]
    cross = jnp.pad(cross_blocks, ((0, 0), (0, 32)))
    kv, lists = gathered(key_input, value_input, key_gain, order, frame, cross)
    query_grad, gain_part, part = attention(lists, query_input, output_grad, query_gain, kv, 768)
    key_grad, value_grad, gain_grads = reduced(part, gain_part, key_input, key_gain)
    return query_grad, key_grad, value_grad, gain_grads[:, None, :]


def solution(mesh):
    split = Mesh(mesh.devices.reshape(mesh.shape["heads"], mesh.shape["tower"], 2, 4, 2), AXES)
    in_specs = (
        P(TOWER_BLK, "heads"),
        P(TOWER_BLK, "heads"),
        P(TOWER_BLK, "heads"),
        P(TOWER_BLK, "heads"),
        P("tower", None),
        P("tower", None),
        P(),
        P(),
        P(),
    )
    out_specs = (
        P(TOWER_BLK, "heads"),
        P(TOWER_BLK, "heads"),
        P(TOWER_BLK, "heads"),
        P(None, "tower", None),
    )
    return jax.shard_map(shards, mesh=split, in_specs=in_specs, out_specs=out_specs, check_vma=False)
```

```python
import functools
import math

import jax
import jax.numpy as jnp
from jax import lax
from jax.experimental import pallas as pl
from jax.experimental.pallas import tpu as pltpu
from jax.sharding import Mesh
from jax.sharding import PartitionSpec as P

SEGMENT = 64
AXES = ("heads", "tower", "blk_0", "blk_1", "blk_2")
TOWER_BLK = ("tower", "blk_0", "blk_1", "blk_2")
EPSILON = 1e-06
NEGATIVE = -1e30
LOG2E = 1.4426950408889634
MESH = pl.DeviceIdType.MESH
HBM = pl.BlockSpec(memory_space=pltpu.HBM)
MIB = 1024 * 1024
DIRECT_A, DIRECT_B, LATE = True, (2,), False
SUM_A, SUM_B = True, ()
MOST, CHUNKS, ROWS = 67_043_328, 32 * 2 * 192 * 128 * 2, 2 * 192 * 896 * 2
VMEM = pltpu.VMEM
DMA = pltpu.SemaphoreType.DMA
F32, BF16, I32 = jnp.float32, jnp.bfloat16, jnp.int32


def dot(a, b, left, right):
    return lax.dot_general(a, b, (((left,), (right,)), ((), ())), preferred_element_type=F32)


def position():
    z = lax.axis_index("blk_0") * 2 + lax.axis_index("tower")
    return lax.axis_index("heads"), lax.axis_index("blk_1"), z, lax.axis_index("blk_2")


def device(y, x, z, core):
    return (y, lax.rem(z, 2), lax.div(z, 2), x, core)


def place_of(x, z, core):
    return lax.rem(z, 2) * 16 + lax.div(z, 2) * 8 + x * 2 + core


def shifted(x, z, core, first, second):
    nx = lax.rem(x + (1 - core) * first + core * second, 4)
    nz = lax.rem(z + core * first + (1 - core) * second, 4)
    return nx, nz


def remote(src, dst, send, recv, target):
    return pltpu.make_async_remote_copy(
        src_ref=src, dst_ref=dst, send_sem=send, recv_sem=recv, device_id=target, device_id_type=MESH
    )


def meet(targets):
    barrier = pltpu.get_barrier_semaphore()
    for target in targets:
        pl.semaphore_signal(barrier, inc=1, device_id=target, device_id_type=MESH)
    return lambda: pl.semaphore_wait(barrier, len(targets))


def gather_kernel(
    key_hbm, value_hbm, gain_hbm, order_hbm, frame_hbm, cross_hbm, query_hbm, grad_hbm, query_gain_hbm,
    all_ref, list_ref, query_out, grad_out, query_gain_out,
    key_ref, gain_ref, order_ref, frame_ref, cross_ref, mine, load_sem, own_sem, send_a, recv_a, send_b, recv_b, send_s, recv_s,
):
    y, x, z, core = position()

    def target(first, second):
        nx, nz = shifted(x, z, core, first, second)
        return device(y, nx, nz, core)

    def chunk(first, second):
        nx, nz = shifted(x, z, core, first, second)
        return place_of(nx, nz, core)

    loads = [
        pltpu.make_async_copy(src, dst, load_sem.at[n])
        for n, (src, dst) in enumerate((
            (key_hbm, key_ref),
            (gain_hbm, gain_ref),
            (value_hbm, mine.at[1]),
            (order_hbm, order_ref),
            (frame_hbm, frame_ref),
            (cross_hbm, cross_ref),
            (query_hbm, query_out),
            (grad_hbm, grad_out),
            (query_gain_hbm, query_gain_out),
        ))
    ]
    for load in loads:
        load.start()
    sibling = device(y, x, z, 1 - core)
    ring_a = (target(1, 0), target(3, 0))
    ring_b = (target(0, 1), target(0, 3))
    far_a, far_b = target(2, 0), target(0, 2)
    wait_all = meet((*ring_a, *ring_b, far_a, far_b, sibling))
    loads[0].wait()
    loads[1].wait()
    keys = key_ref[...].astype(F32)
    inverse = lax.rsqrt(jnp.mean(keys * keys, axis=-1, keepdims=True) + EPSILON)
    mine[0] = (keys * inverse * gain_ref[...]).astype(BF16)
    me = place_of(x, z, core)
    own = pltpu.make_async_copy(mine, all_ref.at[me], own_sem)
    started = []

    def send(src, dst, send_sem, recv_sem, to):
        copy = remote(src, dst, send_sem, recv_sem, to)
        copy.start()
        started.append(copy)

    def arrived(dst, recv_sem):
        remote(dst, dst, send_s.at[0], recv_sem, sibling).wait_recv()

    def spread(first, src):
        at = all_ref.at[chunk(first, 0)]
        send(src, at, send_b.at[first, 0], recv_b.at[first, 1], ring_b[0])
        send(src, at, send_b.at[first, 1], recv_b.at[first, 0], ring_b[1])
        if first in DIRECT_B:
            send(src, at, send_b.at[first, 2], recv_b.at[first, 2], far_b)

    def share(first, second, src):
        n = first * 4 + second
        send(src, all_ref.at[chunk(first, second)], send_s.at[n], recv_s.at[n], sibling)

    loads[2].wait()
    wait_all()
    own.start()
    send(mine, all_ref.at[me], send_a.at[0], recv_a.at[1], ring_a[0])
    send(mine, all_ref.at[me], send_a.at[1], recv_a.at[0], ring_a[1])
    if DIRECT_A:
        send(mine, all_ref.at[me], send_a.at[2], recv_a.at[2], far_a)
    if not LATE:
        spread(0, mine)
    share(0, 0, mine)

    lane = lax.broadcasted_iota(I32, (1, 128), 1)
    down = lax.broadcasted_iota(I32, (128, 128), 0)
    across = lax.broadcasted_iota(I32, (128, 128), 1)
    for load in loads[3:6]:
        load.wait()
    order = jnp.concatenate([order_ref[...], jnp.zeros((1, 32), I32)], axis=1)
    frame = jnp.concatenate([frame_ref[...], jnp.zeros((1, 80), I32)], axis=1)
    frame = jnp.where((lane >= 48) & (lane < 96), pltpu.roll(frame, 48, 1), -1)
    below = (across < down).astype(F32)
    start_of = (lax.shift_right_logical(down * 171, 9) * 384 + (down - 3 * lax.shift_right_logical(down * 171, 9)) * 64)
    image = me >= 16
    list_ref[...] = jnp.zeros_like(list_ref)
    counts = jnp.where(lane == 3, jnp.where(image, 0, 1), 0)
    for b in range(3):
        block = me * 3 + b
        here = lane == block
        slot = jnp.sum(jnp.where(here, order, 0), axis=-1, keepdims=True)
        seen = jnp.sum(jnp.where(here, frame, 0), axis=-1, keepdims=True)
        same = (lane >= 48) == image
        near = (order <= slot) | ((frame == seen) & (seen >= 0))
        crossing = jnp.concatenate([cross_ref[pl.ds(block, 1), :], jnp.zeros((1, 32), I32)], axis=1)
        opened = same | (crossing == 1)
        others = (near & opened & (lane < 96) & (lane != block)).astype(F32)
        column = jnp.broadcast_to(others, (128, 128)).T
        at = dot(below, column, 1, 0).astype(I32) + 1
        chosen = (column > 0.5) & (at == across)
        listed = jnp.sum(jnp.where(chosen, start_of, 0), axis=0, keepdims=True)
        first_start = me * 384 + b * 64
        list_ref[b : b + 1, :] = jnp.where(lane == 0, first_start, listed)
        count = 1 + jnp.sum(others, axis=-1, keepdims=True).astype(I32)
        counts = jnp.where(lane == b, count, counts)
    list_ref[3:4, :] = counts

    def from_a(slot, first, half, to, forward_recv):
        at = all_ref.at[chunk(first, 0)]
        arrived(at, recv_a.at[slot])
        if not DIRECT_A:
            send(at.at[half], at.at[half], send_a.at[2 + half], recv_a.at[forward_recv], to)
        spread(first, at)
        share(first, 0, at)

    def from_b(first, slot, second, half, to):
        at = all_ref.at[chunk(first, second)]
        arrived(at, recv_b.at[first, slot])
        if first not in DIRECT_B:
            send(at.at[half], at.at[half], send_b.at[first, 2 + half], recv_b.at[first, 2 + half], to)
        share(first, second, at)

    def both_b(first):
        from_b(first, 0, 1, 0, ring_b[1])
        from_b(first, 1, 3, 1, ring_b[0])

    from_a(0, 1, 0, ring_a[1], 2)
    from_a(1, 3, 1, ring_a[0], 3)
    if LATE:
        spread(0, mine)
    if not DIRECT_A:
        both_b(0)
    at = all_ref.at[chunk(2, 0)]
    if DIRECT_A:
        arrived(at, recv_a.at[2])
    else:
        arrived(at.at[0], recv_a.at[2])
        arrived(at.at[1], recv_a.at[3])
    spread(2, at)
    share(2, 0, at)
    if DIRECT_A:
        both_b(0)
    both_b(1)
    both_b(3)
    both_b(2)
    for first in (0, 1, 3, 2):
        at = all_ref.at[chunk(first, 2)]
        if first in DIRECT_B:
            arrived(at, recv_b.at[first, 2])
        else:
            arrived(at.at[0], recv_b.at[first, 2])
            arrived(at.at[1], recv_b.at[first, 3])
        share(first, 2, at)
    own.wait()
    for load in loads[6:]:
        load.wait()
    for copy in started:
        copy.wait_send()
    for n in range(16):
        nx, nz = shifted(x, z, 1 - core, n // 4, n % 4)
        arrived(all_ref.at[place_of(nx, nz, 1 - core)], recv_s.at[n])


def gathered(key_input, value_input, key_gain, order, frame, cross, query_input, output_grad, query_gain):
    rows, dim = key_input.shape
    whole = pl.BlockSpec(memory_space=VMEM)
    return pl.pallas_call(
        gather_kernel,
        out_shape=(
            VMEM((32, 2, rows, dim), BF16), VMEM((8, 128), I32), VMEM(query_input.shape, BF16), VMEM(query_input.shape, BF16),
            VMEM((1, dim), F32),
        ),
        in_specs=[HBM] * 9,
        out_specs=(pl.BlockSpec(memory_space=pl.ANY), whole, *(pl.BlockSpec(memory_space=pl.ANY),) * 3),
        scratch_shapes=[
            VMEM((rows, dim), BF16), VMEM((1, dim), F32), VMEM(order.shape, I32), VMEM(frame.shape, I32),
            VMEM(cross.shape, I32), VMEM((2, rows, dim), BF16), DMA((9,)), DMA, DMA((4,)), DMA((4,)), DMA((4, 4)), DMA((4, 4)), DMA((16,)), DMA((16,)),
        ],
        compiler_params=pltpu.CompilerParams(collective_id=0, has_side_effects=True, vmem_limit_bytes=MOST - CHUNKS - ROWS - 16 * 1024),
        cost_estimate=pl.CostEstimate(flops=0, bytes_accessed=60_000_000, transcendentals=0),
        name="gather_keys",
    )(key_input, value_input, key_gain, order, frame, cross, query_input, output_grad, query_gain)


def attention_kernel(
    per_group, blocks, width, list_ref, query_ref, grad_ref, gain_ref, kv_ref,
    out_ref, gain_out, part_ref,
    qn, dop, s_ref, w_ref, m_ref, l_ref, o_ref, dq_ref, acc,
):
    dim = 128
    rows = SEGMENT * per_group
    per = width // SEGMENT
    log_scale = LOG2E / math.sqrt(dim)
    scale = 1.0 / math.sqrt(dim)
    places = kv_ref.shape[0] // 384
    is_text = list_ref[3, 3] == 1
    def zero(i, _):
        acc[pl.ds(pl.multiple_of(i * 128, 128), 128), :] = jnp.zeros((128, dim), F32)
        return 0

    lax.fori_loop(0, places * 3, zero, 0)
    gain = gain_ref[...]
    query_part = jnp.zeros((8, dim), F32)

    for b in range(blocks):
        count = list_ref[3, b]
        rest = lax.rem(count - 1, per)
        groups = lax.div(count - 1, per)
        for h in range(per_group):
            q = query_ref[b * SEGMENT : (b + 1) * SEGMENT, h * dim : (h + 1) * dim].astype(F32)
            inverse = lax.rsqrt(jnp.mean(q * q, axis=-1, keepdims=True) + EPSILON)
            qn[h * SEGMENT : (h + 1) * SEGMENT, :] = (q * inverse * gain).astype(BF16)
        m_ref[...] = jnp.full_like(m_ref, NEGATIVE)
        l_ref[...] = jnp.zeros_like(l_ref)
        o_ref[...] = jnp.zeros_like(o_ref)
        dq_ref[...] = jnp.zeros_like(dq_ref)

        def starts(g):
            out = []
            for j in range(per):
                if isinstance(g, int):
                    p = 0 if j == 0 else jnp.where(j <= rest, j, 0)
                else:
                    p = 1 + rest + (g - 1) * per + j
                out.append(pl.multiple_of(list_ref[b, p], SEGMENT))
            return out

        def tile(at, offset):
            return jnp.concatenate([kv_ref[pl.ds(s + offset, SEGMENT), :] for s in at], axis=0)

        def logits(g, at, masked):
            s = dot(qn[...], tile(at, 0), 1, 1)
            if masked:
                lane = lax.broadcasted_iota(I32, (rows, width), 1)
                row = lax.broadcasted_iota(I32, (rows, width), 0)
                limit = lax.rem(row, SEGMENT) + jnp.where(is_text, 0, SEGMENT)
                ok = (lane < (rest + 1) * SEGMENT) & ((lane >= SEGMENT) | (lane <= limit))
                s = jnp.where(ok, s, NEGATIVE)
            s_ref[g] = s
            top = m_ref[...]
            for t in range(width // 128):
                top = jnp.maximum(top, s[:, t * 128 : (t + 1) * 128])
            m_ref[...] = top

        def weights(g, at):
            top = m_ref[...]
            total = l_ref[...]
            parts = []
            for t in range(width // 128):
                w = jnp.exp2((s_ref[g, :, t * 128 : (t + 1) * 128] - top) * log_scale)
                total = total + w
                parts.append(w.astype(BF16))
            l_ref[...] = total
            w = jnp.concatenate(parts, axis=1)
            w_ref[g] = w
            o_ref[...] += dot(w, tile(at, 192), 1, 0)

        def slopes(g, at):
            keys = tile(at, 0)
            pushes = dot(dop[...], tile(at, 192), 1, 1)
            delta = m_ref[...]
            w = w_ref[g]
            parts = []
            for t in range(width // 128):
                sl = slice(t * 128, (t + 1) * 128)
                parts.append((w[:, sl].astype(F32) * (pushes[:, sl] - delta)).astype(BF16))
            ds = jnp.concatenate(parts, axis=1)
            dq_ref[...] += dot(ds, keys, 1, 0)
            dk = dot(ds, qn[...], 0, 0)
            dv = dot(w, dop[...], 0, 0)
            for j in range(per):
                sl = slice(j * SEGMENT, (j + 1) * SEGMENT)
                acc[pl.ds(at[j], SEGMENT), :] += dk[sl]
                acc[pl.ds(at[j] + 192, SEGMENT), :] += dv[sl]

        def over(step):
            def body(g, _):
                step(g, starts(g))
                return 0

            lax.fori_loop(1, groups + 1, body, 0)

        logits(0, starts(0), True)
        over(lambda g, at: logits(g, at, False))
        m_ref[...] = jnp.broadcast_to(jnp.max(m_ref[...], axis=-1, keepdims=True), m_ref.shape)
        weights(0, starts(0))
        over(weights)
        total = jnp.sum(l_ref[...], axis=-1, keepdims=True)
        over_total = 1.0 / total
        output = (o_ref[...] / total).astype(BF16).astype(F32)
        for h in range(per_group):
            sl = slice(h * SEGMENT, (h + 1) * SEGMENT)
            g = grad_ref[b * SEGMENT : (b + 1) * SEGMENT, h * dim : (h + 1) * dim].astype(F32)
            g = (g * over_total[sl]).astype(BF16)
            dop[sl, :] = g
            delta = jnp.sum(g.astype(F32) * output[sl], axis=-1, keepdims=True)
            m_ref[sl, :] = jnp.broadcast_to(delta, (SEGMENT, 128))
        slopes(0, starts(0))
        over(slopes)
        for h in range(per_group):
            sl = slice(h * SEGMENT, (h + 1) * SEGMENT)
            q = query_ref[b * SEGMENT : (b + 1) * SEGMENT, h * dim : (h + 1) * dim].astype(F32)
            inverse = lax.rsqrt(jnp.mean(q * q, axis=-1, keepdims=True) + EPSILON)
            unit = q * inverse
            grad = dq_ref[sl, :] * scale
            e = grad * gain
            dq = inverse * (e - unit * jnp.mean(e * unit, axis=-1, keepdims=True))
            out_ref[b * SEGMENT : (b + 1) * SEGMENT, h * dim : (h + 1) * dim] = dq.astype(BF16)
            query_part = query_part + jnp.sum((grad * unit).reshape(SEGMENT // 8, 8, dim), axis=0)

    def finish(i, part):
        at = pl.multiple_of(i * 384, 384)
        mine = acc[pl.ds(at, 384), :]
        part_ref[i, 0] = mine[:192].astype(BF16)
        part_ref[i, 1] = mine[192:].astype(BF16)
        terms = mine[:192] * kv_ref[pl.ds(at, 192), :].astype(F32)
        return part + jnp.sum(terms.reshape(24, 8, dim), axis=0)

    text = lax.fori_loop(0, places // 2, finish, jnp.zeros((8, dim), F32))
    image = lax.fori_loop(places // 2, places, finish, jnp.zeros((8, dim), F32))
    query_sum = jnp.sum(query_part, axis=0, keepdims=True)
    row = lax.broadcasted_iota(I32, (8, dim), 0)
    filled = jnp.where(row == jnp.where(is_text, 0, 1), query_sum, 0.0)
    filled = jnp.where(row == 2, jnp.sum(text, axis=0, keepdims=True), filled)
    gain_out[...] = jnp.where(row == 3, jnp.sum(image, axis=0, keepdims=True), filled)


def attention(lists, query_input, output_grad, query_gain, kv, width):
    rows, columns = query_input.shape
    per_group = columns // 128
    stacked = SEGMENT * per_group
    segments = kv.shape[0] * 3
    per = width // SEGMENT
    groups = (segments + per - 1) // per + 1
    flat = kv.shape[0] * 384
    whole = pl.BlockSpec(memory_space=VMEM)
    return pl.pallas_call(
        functools.partial(attention_kernel, per_group, rows // SEGMENT, width),
        out_shape=(
            jax.ShapeDtypeStruct((rows, columns), BF16),
            VMEM((8, 128), F32),
            VMEM(kv.shape, BF16),
        ),
        in_specs=[pl.BlockSpec(memory_space=pltpu.SMEM)] + [whole] * 4,
        out_specs=(whole,) * 3,
        scratch_shapes=[
            VMEM((stacked, 128), BF16), VMEM((stacked, 128), BF16),
            VMEM((groups, stacked, width), F32), VMEM((groups, stacked, width), BF16),
            VMEM((stacked, 128), F32), VMEM((stacked, 128), F32), VMEM((stacked, 128), F32), VMEM((stacked, 128), F32),
            VMEM((flat, 128), F32),
        ],
        compiler_params=pltpu.CompilerParams(vmem_limit_bytes=36 * MIB),
        cost_estimate=pl.CostEstimate(flops=20_000_000_000, bytes_accessed=60_000_000, transcendentals=0),
        name="attention",
    )(lists, query_input, output_grad, query_gain, kv.reshape(flat, 128))


def reduce_kernel(
    part_ref, gain_part, key_hbm, gain_hbm, key_out, value_out, gain_out,
    key_ref, gain_ref, load_sem, sib, work, half_b, full_b, half_a, full_a, sums,
    send_s, recv_s, send_hb, recv_hb, send_fb, recv_fb, send_a, recv_a, send_g, recv_g,
):
    y, x, z, core = position()
    scale = 1.0 / math.sqrt(128)

    def target(first, second):
        nx, nz = shifted(x, z, core, first, second)
        return device(y, nx, nz, core)

    sibling = device(y, x, z, 1 - core)
    ring_a = (target(1, 0), target(3, 0))
    ring_b = (target(0, 1), target(0, 3))
    lines = (
        (y * 2 + core, 8, lambda n: device(lax.div(n, 2), x, z, lax.rem(n, 2))),
        (x * 4 + z, 16, lambda n: device(y, lax.div(n, 4), lax.rem(n, 4), core)),
    )
    far_a, far_b = target(2, 0), target(0, 2)
    peers = [of(lax.rem(at + o, size)) for at, size, of in lines for o in range(1, size)]
    loads = [
        pltpu.make_async_copy(key_hbm, key_ref, load_sem.at[0]), pltpu.make_async_copy(gain_hbm, gain_ref, load_sem.at[1])
    ]
    for load in loads:
        load.start()
    meet(peers)()
    started = []

    def send(src, dst, send_sem, recv_sem, to):
        copy = remote(src, dst, send_sem, recv_sem, to)
        copy.start()
        started.append(copy)

    def arrived(dst, recv_sem):
        remote(dst, dst, send_s.at[0], recv_sem, sibling).wait_recv()

    def gain_send(stage, value):
        at, size, of = lines[stage]
        sums[stage, at] = value
        for o in range(1, size):
            send(sums.at[stage, at], sums.at[stage, at], send_g.at[stage, o], recv_g.at[stage, at], of(lax.rem(at + o, size)))

    def gain_sum(stage):
        at, size, of = lines[stage]
        for o in range(1, size):
            n = lax.rem(at + o, size)
            arrived(sums.at[stage, n], recv_g.at[stage, n])
        total = sums[stage, 0]
        for n in range(1, size):
            total = total + sums[stage, n]
        return total

    visit = [(first, second) for second in (2, 1, 3, 0) for first in (2, 1, 3, 0)]
    for first, second in visit:
        nx, nz = shifted(x, z, 1 - core, first, second)
        n = first * 4 + second
        send(part_ref.at[place_of(nx, nz, 1 - core)], sib.at[first, second], send_s.at[n], recv_s.at[n], sibling)
    gain_send(0, gain_part[...])

    def combine(first, second):
        n = first * 4 + second
        arrived(sib.at[first, second], recv_s.at[n])
        nx, nz = shifted(x, z, core, first, second)
        return part_ref[place_of(nx, nz, core)].astype(F32) + sib[first, second].astype(F32)

    for first in (2, 1, 3, 0):
        work[first, 2] = combine(first, 2).astype(BF16)
        if first in SUM_B:
            send(work.at[first, 2], half_b.at[first], send_hb.at[first, 0], recv_hb.at[first, 0], far_b)
        else:
            for half in (0, 1):
                send(work.at[first, 2, half], half_b.at[first, half], send_hb.at[first, half], recv_hb.at[first, half], ring_b[half])
    for first in (2, 1, 3, 0):
        for half, second in ((0, 1), (1, 3)):
            mine = combine(first, second)
            work[first, second] = mine.astype(BF16)
            if first not in SUM_B:
                arrived(half_b.at[first, half], recv_hb.at[first, half])
                work[first, second, half] = (mine[half] + half_b[first, half].astype(F32)).astype(BF16)
            send(work.at[first, second], full_b.at[first, half], send_fb.at[first, half], recv_fb.at[first, half], ring_b[half])

    def settled(first):
        mine = combine(first, 0)
        if first in SUM_B:
            arrived(half_b.at[first], recv_hb.at[first, 0])
            mine = mine + half_b[first].astype(F32)
        for half in (0, 1):
            arrived(full_b.at[first, half], recv_fb.at[first, half])
            mine = mine + full_b[first, half].astype(F32)
        return mine

    gain_send(1, gain_sum(0))
    work[2, 0] = settled(2).astype(BF16)
    if SUM_A:
        send(work.at[2, 0], half_a, send_a.at[0], recv_a.at[0], far_a)
    else:
        for half in (0, 1):
            send(work.at[2, 0, half], half_a.at[half], send_a.at[half], recv_a.at[half], ring_a[half])
    for half, first in ((0, 1), (1, 3)):
        mine = settled(first)
        work[first, 0] = mine.astype(BF16)
        if not SUM_A:
            arrived(half_a.at[half], recv_a.at[half])
            work[first, 0, half] = (mine[half] + half_a[half].astype(F32)).astype(BF16)
        send(work.at[first, 0], full_a.at[half], send_a.at[2 + half], recv_a.at[2 + half], ring_a[half])
    mine = settled(0)
    totals = gain_sum(1)
    for load in loads:
        load.wait()
    gain = gain_ref[...]
    tower = lax.rem(z, 2)
    row = lax.broadcasted_iota(I32, (8, 128), 0)
    query_sum = jnp.sum(jnp.where(row == tower, totals, 0.0), axis=0, keepdims=True)
    key_sum = jnp.sum(jnp.where(row == 2 + tower, totals, 0.0), axis=0, keepdims=True)
    gain_out[0:1, :] = query_sum
    gain_out[1:2, :] = key_sum * scale / gain
    if SUM_A:
        arrived(half_a, recv_a.at[0])
        mine = mine + half_a[...].astype(F32)
    for half in (0, 1):
        arrived(full_a.at[half], recv_a.at[2 + half])
        mine = mine + full_a[half].astype(F32)
    value_out[...] = mine[1].astype(BF16)
    keys = key_ref[...].astype(F32)
    inverse = lax.rsqrt(jnp.mean(keys * keys, axis=-1, keepdims=True) + EPSILON)
    unit = keys * inverse
    e = mine[0] * scale * gain
    key_out[...] = (inverse * (e - unit * jnp.mean(e * unit, axis=-1, keepdims=True))).astype(BF16)
    for copy in started:
        copy.wait_send()


def reduced(part, gain_part, key_input, key_gain):
    rows, dim = key_input.shape
    whole = pl.BlockSpec(memory_space=VMEM)
    one = (2, rows, dim)
    return pl.pallas_call(
        reduce_kernel,
        out_shape=(
            VMEM((rows, dim), BF16),
            VMEM((rows, dim), BF16),
            VMEM((2, dim), F32),
        ),
        in_specs=[whole, whole, HBM, HBM],
        out_specs=(whole,) * 3,
        scratch_shapes=[
            VMEM((rows, dim), BF16), VMEM((1, dim), F32), DMA((2,)),
            VMEM((4, 4, *one), BF16), VMEM((4, 4, *one), BF16), VMEM((4, *one), BF16), VMEM((4, 2, *one), BF16),
            VMEM(one, BF16), VMEM((2, *one), BF16), VMEM((2, 16, 8, dim), F32),
            DMA((16,)), DMA((16,)), DMA((4, 2)), DMA((4, 2)), DMA((4, 2)), DMA((4, 2)), DMA((4,)), DMA((4,)),
            DMA((2, 16)), DMA((2, 16)),
        ],
        compiler_params=pltpu.CompilerParams(collective_id=1, has_side_effects=True, vmem_limit_bytes=16 * MIB),
        name="reduce_keys",
    )(part, gain_part, key_input, key_gain)


def shards(
    query_input, key_input, value_input, output_grad, query_gain, key_gain, stripe_order, frame_index, cross_blocks
):
    kv, lists, queries, grads, gain = gathered(
        key_input, value_input, key_gain, stripe_order[None], frame_index[None], cross_blocks,
        query_input, output_grad, query_gain,
    )
    query_grad, gain_part, part = attention(lists, queries, grads, gain, kv, 768)
    key_grad, value_grad, gain_grads = reduced(part, gain_part, key_input, key_gain)
    return query_grad, key_grad, value_grad, gain_grads[:, None, :]


def solution(mesh):
    split = Mesh(mesh.devices.reshape(mesh.shape["heads"], mesh.shape["tower"], 2, 4, 2), AXES)
    in_specs = (
        P(TOWER_BLK, "heads"),
        P(TOWER_BLK, "heads"),
        P(TOWER_BLK, "heads"),
        P(TOWER_BLK, "heads"),
        P("tower", None),
        P("tower", None),
        P(),
        P(),
        P(),
    )
    out_specs = (
        P(TOWER_BLK, "heads"),
        P(TOWER_BLK, "heads"),
        P(TOWER_BLK, "heads"),
        P(None, "tower", None),
    )
    return jax.shard_map(shards, mesh=split, in_specs=in_specs, out_specs=out_specs, check_vma=False)
```

```python
import functools
import math

import jax
import jax.numpy as jnp
from jax import lax
from jax.experimental import pallas as pl
from jax.experimental.pallas import tpu as pltpu
from jax.sharding import Mesh
from jax.sharding import PartitionSpec as P

SEGMENT = 64
AXES = ("heads", "tower", "blk_0", "blk_1", "blk_2")
TOWER_BLK = ("tower", "blk_0", "blk_1", "blk_2")
EPSILON = 1e-06
NEGATIVE = -1e30
LOG2E = 1.4426950408889634
WIDE, NARROW, LANES = 24, 12, 256
MESH = pl.DeviceIdType.MESH
HBM = pl.BlockSpec(memory_space=pltpu.HBM)
MIB = 1024 * 1024
DIRECT_A, DIRECT_B, LATE = True, (2,), False
SUM_A, SUM_B = True, ()
MOST, CHUNKS, ROWS = 67_043_328, 32 * 2 * 192 * 128 * 2, 2 * 192 * 896 * 2
VMEM = pltpu.VMEM
DMA = pltpu.SemaphoreType.DMA
F32, BF16, I32 = jnp.float32, jnp.bfloat16, jnp.int32


def dot(a, b, left, right):
    return lax.dot_general(a, b, (((left,), (right,)), ((), ())), preferred_element_type=F32)


def position():
    z = lax.axis_index("blk_0") * 2 + lax.axis_index("tower")
    return lax.axis_index("heads"), lax.axis_index("blk_1"), z, lax.axis_index("blk_2")


def device(y, x, z, core):
    return (y, lax.rem(z, 2), lax.div(z, 2), x, core)


def place_of(x, z, core):
    return lax.rem(z, 2) * 16 + lax.div(z, 2) * 8 + x * 2 + core


def shifted(x, z, core, first, second):
    nx = lax.rem(x + (1 - core) * first + core * second, 4)
    nz = lax.rem(z + core * first + (1 - core) * second, 4)
    return nx, nz


def remote(src, dst, send, recv, target):
    return pltpu.make_async_remote_copy(
        src_ref=src, dst_ref=dst, send_sem=send, recv_sem=recv, device_id=target, device_id_type=MESH
    )


def meet(targets):
    barrier = pltpu.get_barrier_semaphore()
    for target in targets:
        pl.semaphore_signal(barrier, inc=1, device_id=target, device_id_type=MESH)
    return lambda: pl.semaphore_wait(barrier, len(targets))


def gather_kernel(
    key_hbm, value_hbm, gain_hbm, order_hbm, frame_hbm, cross_hbm, query_hbm, grad_hbm, query_gain_hbm,
    all_ref, list_ref, query_out, grad_out, query_gain_out,
    key_ref, gain_ref, order_ref, frame_ref, cross_ref, mine, load_sem, own_sem, send_a, recv_a, send_b, recv_b, send_s, recv_s,
):
    y, x, z, core = position()

    def target(first, second):
        nx, nz = shifted(x, z, core, first, second)
        return device(y, nx, nz, core)

    def chunk(first, second):
        nx, nz = shifted(x, z, core, first, second)
        return place_of(nx, nz, core)

    loads = [
        pltpu.make_async_copy(src, dst, load_sem.at[n])
        for n, (src, dst) in enumerate((
            (key_hbm, key_ref),
            (gain_hbm, gain_ref),
            (value_hbm, mine.at[1]),
            (order_hbm, order_ref),
            (frame_hbm, frame_ref),
            (cross_hbm, cross_ref),
            (query_hbm, query_out),
            (grad_hbm, grad_out),
            (query_gain_hbm, query_gain_out),
        ))
    ]
    for load in loads:
        load.start()
    sibling = device(y, x, z, 1 - core)
    ring_a = (target(1, 0), target(3, 0))
    ring_b = (target(0, 1), target(0, 3))
    far_a, far_b = target(2, 0), target(0, 2)
    wait_all = meet((*ring_a, *ring_b, far_a, far_b, sibling))
    loads[0].wait()
    loads[1].wait()
    keys = key_ref[...].astype(F32)
    inverse = lax.rsqrt(jnp.mean(keys * keys, axis=-1, keepdims=True) + EPSILON)
    mine[0] = (keys * inverse * gain_ref[...]).astype(BF16)
    me = place_of(x, z, core)
    own = pltpu.make_async_copy(mine, all_ref.at[me], own_sem)
    started = []

    def send(src, dst, send_sem, recv_sem, to):
        copy = remote(src, dst, send_sem, recv_sem, to)
        copy.start()
        started.append(copy)

    def arrived(dst, recv_sem):
        remote(dst, dst, send_s.at[0], recv_sem, sibling).wait_recv()

    def spread(first, src):
        at = all_ref.at[chunk(first, 0)]
        send(src, at, send_b.at[first, 0], recv_b.at[first, 1], ring_b[0])
        send(src, at, send_b.at[first, 1], recv_b.at[first, 0], ring_b[1])
        if first in DIRECT_B:
            send(src, at, send_b.at[first, 2], recv_b.at[first, 2], far_b)

    def share(first, second, src):
        n = first * 4 + second
        send(src, all_ref.at[chunk(first, second)], send_s.at[n], recv_s.at[n], sibling)

    loads[2].wait()
    wait_all()
    own.start()
    send(mine, all_ref.at[me], send_a.at[0], recv_a.at[1], ring_a[0])
    send(mine, all_ref.at[me], send_a.at[1], recv_a.at[0], ring_a[1])
    if DIRECT_A:
        send(mine, all_ref.at[me], send_a.at[2], recv_a.at[2], far_a)
    if not LATE:
        spread(0, mine)
    share(0, 0, mine)

    lane = lax.broadcasted_iota(I32, (1, 128), 1)
    down = lax.broadcasted_iota(I32, (128, 128), 0)
    across = lax.broadcasted_iota(I32, (128, 128), 1)
    for load in loads[3:6]:
        load.wait()
    order = jnp.concatenate([order_ref[...], jnp.zeros((1, 32), I32)], axis=1)
    frame = jnp.concatenate([frame_ref[...], jnp.zeros((1, 80), I32)], axis=1)
    frame = jnp.where((lane >= 48) & (lane < 96), pltpu.roll(frame, 48, 1), -1)
    below = (across < down).astype(F32)
    start_of = (lax.shift_right_logical(down * 171, 9) * 384 + (down - 3 * lax.shift_right_logical(down * 171, 9)) * 64)
    image = me >= 16
    list_ref[...] = jnp.zeros_like(list_ref)
    counts = jnp.where(lane == 3, jnp.where(image, 0, 1), 0)
    for b in range(3):
        block = me * 3 + b
        here = lane == block
        slot = jnp.sum(jnp.where(here, order, 0), axis=-1, keepdims=True)
        seen = jnp.sum(jnp.where(here, frame, 0), axis=-1, keepdims=True)
        same = (lane >= 48) == image
        near = (order <= slot) | ((frame == seen) & (seen >= 0))
        crossing = jnp.concatenate([cross_ref[pl.ds(block, 1), :], jnp.zeros((1, 32), I32)], axis=1)
        opened = same | (crossing == 1)
        others = (near & opened & (lane < 96) & (lane != block)).astype(F32)
        column = jnp.broadcast_to(others, (128, 128)).T
        at = dot(below, column, 1, 0).astype(I32) + 1
        chosen = (column > 0.5) & (at == across)
        listed = jnp.sum(jnp.where(chosen, start_of, 0), axis=0, keepdims=True)
        first_start = me * 384 + b * 64
        list_ref[b : b + 1, :] = jnp.where(lane == 0, first_start, listed)
        count = 1 + jnp.sum(others, axis=-1, keepdims=True).astype(I32)
        counts = jnp.where(lane == b, count, counts)
    list_ref[3:4, :] = counts

    def from_a(slot, first, half, to, forward_recv):
        at = all_ref.at[chunk(first, 0)]
        arrived(at, recv_a.at[slot])
        if not DIRECT_A:
            send(at.at[half], at.at[half], send_a.at[2 + half], recv_a.at[forward_recv], to)
        spread(first, at)
        share(first, 0, at)

    def from_b(first, slot, second, half, to):
        at = all_ref.at[chunk(first, second)]
        arrived(at, recv_b.at[first, slot])
        if first not in DIRECT_B:
            send(at.at[half], at.at[half], send_b.at[first, 2 + half], recv_b.at[first, 2 + half], to)
        share(first, second, at)

    def both_b(first):
        from_b(first, 0, 1, 0, ring_b[1])
        from_b(first, 1, 3, 1, ring_b[0])

    from_a(0, 1, 0, ring_a[1], 2)
    from_a(1, 3, 1, ring_a[0], 3)
    if LATE:
        spread(0, mine)
    if not DIRECT_A:
        both_b(0)
    at = all_ref.at[chunk(2, 0)]
    if DIRECT_A:
        arrived(at, recv_a.at[2])
    else:
        arrived(at.at[0], recv_a.at[2])
        arrived(at.at[1], recv_a.at[3])
    spread(2, at)
    share(2, 0, at)
    if DIRECT_A:
        both_b(0)
    both_b(1)
    both_b(3)
    both_b(2)
    for first in (0, 1, 3, 2):
        at = all_ref.at[chunk(first, 2)]
        if first in DIRECT_B:
            arrived(at, recv_b.at[first, 2])
        else:
            arrived(at.at[0], recv_b.at[first, 2])
            arrived(at.at[1], recv_b.at[first, 3])
        share(first, 2, at)
    own.wait()
    for load in loads[6:]:
        load.wait()
    for copy in started:
        copy.wait_send()
    for n in range(16):
        nx, nz = shifted(x, z, 1 - core, n // 4, n % 4)
        arrived(all_ref.at[place_of(nx, nz, 1 - core)], recv_s.at[n])


def gathered(key_input, value_input, key_gain, order, frame, cross, query_input, output_grad, query_gain):
    rows, dim = key_input.shape
    whole = pl.BlockSpec(memory_space=VMEM)
    return pl.pallas_call(
        gather_kernel,
        out_shape=(
            VMEM((32, 2, rows, dim), BF16), VMEM((8, 128), I32), VMEM(query_input.shape, BF16), VMEM(query_input.shape, BF16),
            VMEM((1, dim), F32),
        ),
        in_specs=[HBM] * 9,
        out_specs=(pl.BlockSpec(memory_space=pl.ANY), whole, *(pl.BlockSpec(memory_space=pl.ANY),) * 3),
        scratch_shapes=[
            VMEM((rows, dim), BF16), VMEM((1, dim), F32), VMEM(order.shape, I32), VMEM(frame.shape, I32),
            VMEM(cross.shape, I32), VMEM((2, rows, dim), BF16), DMA((9,)), DMA, DMA((4,)), DMA((4,)), DMA((4, 4)), DMA((4, 4)), DMA((16,)), DMA((16,)),
        ],
        compiler_params=pltpu.CompilerParams(collective_id=0, has_side_effects=True, vmem_limit_bytes=MOST - CHUNKS - ROWS - 16 * 1024),
        cost_estimate=pl.CostEstimate(flops=0, bytes_accessed=60_000_000, transcendentals=0),
        name="gather_keys",
    )(key_input, value_input, key_gain, order, frame, cross, query_input, output_grad, query_gain)


def attention_kernel(
    per_group, blocks, list_ref, query_ref, grad_ref, gain_ref, kv_ref,
    out_ref, gain_out, part_ref,
    qn, qt, dop, dot_t, s_ref, w_ref, m_ref, l_ref, o_ref, acc,
):
    dim = 128
    rows = SEGMENT * per_group
    log_scale = LOG2E / math.sqrt(dim)
    scale = 1.0 / math.sqrt(dim)
    places = kv_ref.shape[0] // 384
    is_text = list_ref[3, 3] == 1
    gain = gain_ref[...]

    def zero(i, _):
        acc[i] = jnp.zeros((dim, 128), F32)
        return 0

    lax.fori_loop(0, places * 3, zero, 0)

    def one_block(b, parts):
        query_part, all_part = parts
        base = pl.multiple_of(b * SEGMENT, SEGMENT)
        count = list_ref[3, b] - 1
        wide = lax.div(count, WIDE)
        small = lax.div(lax.rem(count, WIDE), NARROW)
        rest = lax.rem(count, NARROW)
        for h in range(per_group):
            q = query_ref[pl.ds(base, SEGMENT), h * dim : (h + 1) * dim].astype(F32)
            inverse = lax.rsqrt(jnp.mean(q * q, axis=-1, keepdims=True) + EPSILON)
            qn[h * SEGMENT : (h + 1) * SEGMENT, :] = (q * inverse * gain).astype(BF16)
        qt[...] = qn[...].astype(F32).T.astype(BF16)
        m_ref[...] = jnp.full_like(m_ref, NEGATIVE)
        l_ref[...] = jnp.zeros_like(l_ref)
        o_ref[...] = jnp.zeros_like(o_ref)

        def starts(first, size):
            return [pl.multiple_of(list_ref[b, first + j], SEGMENT) for j in range(size)]

        def first_starts():
            ps = [0] + [jnp.where(j <= rest, j, 0) for j in range(1, NARROW)]
            return [pl.multiple_of(list_ref[b, p], SEGMENT) for p in ps]

        def tile(at, offset):
            return jnp.concatenate([kv_ref[pl.ds(s + offset, SEGMENT), :] for s in at], axis=0)

        def number(start):
            return lax.div(start, 384) * 3 + lax.div(lax.rem(start, 384), SEGMENT)

        def logits(slot, at, masked):
            width = len(at) * SEGMENT
            s = dot(qn[...], tile(at, 0), 1, 1) * log_scale
            if masked:
                lane = lax.broadcasted_iota(I32, (rows, width), 1)
                row = lax.broadcasted_iota(I32, (rows, width), 0)
                limit = lax.rem(row, SEGMENT) + jnp.where(is_text, 0, SEGMENT)
                ok = (lane < (rest + 1) * SEGMENT) & ((lane >= SEGMENT) | (lane <= limit))
                s = jnp.where(ok, s, NEGATIVE)
            top = m_ref[...]
            for t in range(width // 128):
                top = jnp.maximum(top, s[:, t * 128 : (t + 1) * 128])
            m_ref[...] = top
            for t in range(width // LANES):
                s_ref[slot + t] = s[:, t * LANES : (t + 1) * LANES]

        def weights(slot, at):
            top = m_ref[...]
            total = l_ref[...]
            out = o_ref[...]
            tiles = len(at) * SEGMENT // LANES
            each = LANES // SEGMENT
            values = [tile(at[u * each : (u + 1) * each], 192).T for u in range(tiles)]
            ready = []
            for u in range(tiles + 1):
                if u < tiles:
                    parts = []
                    for t in range(LANES // 128):
                        w = jnp.exp2(s_ref[slot + u, :, t * 128 : (t + 1) * 128] - top)
                        total = total + w
                        parts.append(w.astype(BF16))
                    w = jnp.concatenate(parts, axis=1)
                    w_ref[slot + u] = w
                    ready.append(w)
                if u > 0:
                    out = out + dot(values[u - 1], ready[u - 1], 1, 1)
            l_ref[...] = total
            o_ref[...] = out

        def slopes(slot, at):
            delta = m_ref[...]
            low = lax.broadcasted_iota(I32, (dim, 128), 1) < SEGMENT
            tiles = len(at) * SEGMENT // LANES
            each = LANES // SEGMENT
            here = [at[u * each : (u + 1) * each] for u in range(tiles)]
            keys = [tile(h, 0).T for h in here]
            pushes, ds, done = {}, {}, {}
            grad_q = o_ref[...]
            for step in range(tiles + 2):
                if step < tiles:
                    pushes[step] = dot(dop[...], tile(here[step], 192), 1, 1)
                u = step - 1
                if 0 <= u < tiles:
                    w = w_ref[slot + u]
                    parts = []
                    for t in range(LANES // 128):
                        sl = slice(t * 128, (t + 1) * 128)
                        parts.append((w[:, sl].astype(F32) * (pushes[u][:, sl] - delta)).astype(BF16))
                    d = jnp.concatenate(parts, axis=1)
                    grad_q = grad_q + dot(keys[u], d, 1, 1)
                    done[u] = dot(qt[...], d, 1, 0), dot(dot_t[...], w, 1, 0)
                u = step - 2
                if 0 <= u < tiles:
                    dk, dv = done[u]
                    for t in range(LANES // 128):
                        sl = slice(t * 128, (t + 1) * 128)
                        k2, v2 = dk[:, sl], dv[:, sl]
                        acc[number(here[u][2 * t])] += jnp.where(low, k2, pltpu.roll(v2, SEGMENT, 1))
                        acc[number(here[u][2 * t + 1])] += jnp.where(low, pltpu.roll(k2, SEGMENT, 1), v2)
            o_ref[...] = grad_q

        def over(step):
            def narrow(g, _):
                step((1 + g) * (NARROW * SEGMENT // LANES), starts(1 + rest + g * NARROW, NARROW))
                return 0

            def broad(g, _):
                step(
                    (1 + small) * (NARROW * SEGMENT // LANES) + g * (WIDE * SEGMENT // LANES),
                    starts(1 + rest + small * NARROW + g * WIDE, WIDE),
                )
                return 0

            lax.fori_loop(0, small, narrow, 0)
            lax.fori_loop(0, wide, broad, 0)

        logits(0, first_starts(), True)
        over(lambda slot, at: logits(slot, at, False))
        m_ref[...] = jnp.broadcast_to(jnp.max(m_ref[...], axis=-1, keepdims=True), m_ref.shape)
        weights(0, first_starts())
        over(weights)
        total = jnp.sum(l_ref[...], axis=-1, keepdims=True)
        over_total = 1.0 / total
        output = (o_ref[...].T / total).astype(BF16).astype(F32)
        o_ref[...] = jnp.zeros_like(o_ref)
        for h in range(per_group):
            sl = slice(h * SEGMENT, (h + 1) * SEGMENT)
            g = grad_ref[pl.ds(base, SEGMENT), h * dim : (h + 1) * dim].astype(F32)
            g = (g * over_total[sl]).astype(BF16)
            dop[sl, :] = g
            delta = jnp.sum(g.astype(F32) * output[sl], axis=-1, keepdims=True)
            m_ref[sl, :] = jnp.broadcast_to(delta, (SEGMENT, 128))
        dot_t[...] = dop[...].astype(F32).T.astype(BF16)
        slopes(0, first_starts())
        over(slopes)
        raw = o_ref[...].T
        for h in range(per_group):
            sl = slice(h * SEGMENT, (h + 1) * SEGMENT)
            q = query_ref[pl.ds(base, SEGMENT), h * dim : (h + 1) * dim].astype(F32)
            inverse = lax.rsqrt(jnp.mean(q * q, axis=-1, keepdims=True) + EPSILON)
            unit = q * inverse
            grad = raw[sl] * scale
            e = grad * gain
            dq = inverse * (e - unit * jnp.mean(e * unit, axis=-1, keepdims=True))
            out_ref[pl.ds(base, SEGMENT), h * dim : (h + 1) * dim] = dq.astype(BF16)
            query_part = query_part + jnp.sum((grad * unit).reshape(SEGMENT // 8, 8, dim), axis=0)
            terms = raw[sl] * qn[sl, :].astype(F32)
            all_part = all_part + jnp.sum(terms.reshape(SEGMENT // 8, 8, dim), axis=0)
        return query_part, all_part

    none = jnp.zeros((8, dim), F32)
    query_part, all_part = lax.fori_loop(0, blocks, one_block, (none, none))

    def finish(i, part):
        at = pl.multiple_of(i * 384, 384)
        mine = [acc[i * 3 + j].astype(BF16) for j in range(3)]
        keys = []
        for j in range(3):
            part_ref[i, j * dim : (j + 1) * dim, :] = mine[j]
            keys.append(kv_ref[pl.ds(at + j * SEGMENT, SEGMENT), :])
            keys.append(jnp.zeros_like(keys[-1]))
        part = part + dot(jnp.concatenate(mine, axis=1), jnp.concatenate(keys, axis=0), 1, 0)
        return part

    text = lax.fori_loop(0, places // 2, finish, jnp.zeros((dim, dim), F32), unroll=4)

    def store(i, _):
        for j in range(3):
            part_ref[i, j * dim : (j + 1) * dim, :] = acc[i * 3 + j].astype(BF16)
        return 0

    lax.fori_loop(places // 2, places, store, 0)
    diagonal = lax.broadcasted_iota(I32, (dim, dim), 0) == lax.broadcasted_iota(I32, (dim, dim), 1)
    text_sum = jnp.sum(jnp.where(diagonal, text, 0.0), axis=0, keepdims=True)
    image_sum = jnp.sum(all_part, axis=0, keepdims=True) - text_sum
    query_sum = jnp.sum(query_part, axis=0, keepdims=True)
    row = lax.broadcasted_iota(I32, (8, dim), 0)
    filled = jnp.where(row == jnp.where(is_text, 0, 1), query_sum, 0.0)
    filled = jnp.where(row == 2, text_sum, filled)
    gain_out[...] = jnp.where(row == 3, image_sum, filled)


def attention(lists, query_input, output_grad, query_gain, kv):
    rows, columns = query_input.shape
    per_group = columns // 128
    stacked = SEGMENT * per_group
    segments = kv.shape[0] * 3
    slots = (segments + NARROW) * SEGMENT // LANES
    flat = kv.shape[0] * 384
    whole = pl.BlockSpec(memory_space=VMEM)
    return pl.pallas_call(
        functools.partial(attention_kernel, per_group, rows // SEGMENT),
        out_shape=(
            jax.ShapeDtypeStruct((rows, columns), BF16),
            VMEM((8, 128), F32),
            VMEM((kv.shape[0], 384, 128), BF16),
        ),
        in_specs=[pl.BlockSpec(memory_space=pltpu.SMEM)] + [whole] * 4,
        out_specs=(whole,) * 3,
        scratch_shapes=[
            VMEM((stacked, 128), BF16), VMEM((128, stacked), BF16), VMEM((stacked, 128), BF16), VMEM((128, stacked), BF16),
            VMEM((slots, stacked, LANES), F32), VMEM((slots, stacked, LANES), BF16),
            VMEM((stacked, 128), F32), VMEM((stacked, 128), F32), VMEM((128, stacked), F32),
            VMEM((segments, 128, 128), F32),
        ],
        compiler_params=pltpu.CompilerParams(vmem_limit_bytes=40 * MIB),
        name="attention",
    )(lists, query_input, output_grad, query_gain, kv.reshape(flat, 128))


def reduce_kernel(
    part_ref, gain_part, key_hbm, gain_hbm, key_out, value_out, gain_out,
    key_ref, gain_ref, load_sem, sib, work, half_b, full_b, half_a, full_a, sums,
    send_s, recv_s, send_hb, recv_hb, send_fb, recv_fb, send_a, recv_a, send_g, recv_g,
):
    y, x, z, core = position()
    scale = 1.0 / math.sqrt(128)

    def target(first, second):
        nx, nz = shifted(x, z, core, first, second)
        return device(y, nx, nz, core)

    sibling = device(y, x, z, 1 - core)
    ring_a = (target(1, 0), target(3, 0))
    ring_b = (target(0, 1), target(0, 3))
    lines = (
        (y * 2 + core, 8, lambda n: device(lax.div(n, 2), x, z, lax.rem(n, 2))),
        (x * 4 + z, 16, lambda n: device(y, lax.div(n, 4), lax.rem(n, 4), core)),
    )
    far_a, far_b = target(2, 0), target(0, 2)
    peers = [of(lax.rem(at + o, size)) for at, size, of in lines for o in range(1, size)]
    loads = [
        pltpu.make_async_copy(key_hbm, key_ref, load_sem.at[0]), pltpu.make_async_copy(gain_hbm, gain_ref, load_sem.at[1])
    ]
    for load in loads:
        load.start()
    meet(peers)()
    started = []

    def send(src, dst, send_sem, recv_sem, to):
        copy = remote(src, dst, send_sem, recv_sem, to)
        copy.start()
        started.append(copy)

    def arrived(dst, recv_sem):
        remote(dst, dst, send_s.at[0], recv_sem, sibling).wait_recv()

    def gain_send(stage, value):
        at, size, of = lines[stage]
        sums[stage, at] = value
        for o in range(1, size):
            send(sums.at[stage, at], sums.at[stage, at], send_g.at[stage, o], recv_g.at[stage, at], of(lax.rem(at + o, size)))

    def gain_sum(stage):
        at, size, of = lines[stage]
        for o in range(1, size):
            n = lax.rem(at + o, size)
            arrived(sums.at[stage, n], recv_g.at[stage, n])
        total = sums[stage, 0]
        for n in range(1, size):
            total = total + sums[stage, n]
        return total

    visit = [(first, second) for second in (2, 1, 3, 0) for first in (2, 1, 3, 0)]
    for first, second in visit:
        nx, nz = shifted(x, z, 1 - core, first, second)
        n = first * 4 + second
        send(part_ref.at[place_of(nx, nz, 1 - core)], sib.at[first, second], send_s.at[n], recv_s.at[n], sibling)
    gain_send(0, gain_part[...])

    def combine(first, second):
        n = first * 4 + second
        arrived(sib.at[first, second], recv_s.at[n])
        nx, nz = shifted(x, z, core, first, second)
        return part_ref[place_of(nx, nz, core)].astype(F32) + sib[first, second].astype(F32)

    for first in (2, 1, 3, 0):
        work[first, 2] = combine(first, 2).astype(BF16)
        if first in SUM_B:
            send(work.at[first, 2], half_b.at[first], send_hb.at[first, 0], recv_hb.at[first, 0], far_b)
        else:
            for half in (0, 1):
                send(work.at[first, 2, half], half_b.at[first, half], send_hb.at[first, half], recv_hb.at[first, half], ring_b[half])
    for first in (2, 1, 3, 0):
        for half, second in ((0, 1), (1, 3)):
            mine = combine(first, second)
            work[first, second] = mine.astype(BF16)
            if first not in SUM_B:
                arrived(half_b.at[first, half], recv_hb.at[first, half])
                work[first, second, half] = (mine[half] + half_b[first, half].astype(F32)).astype(BF16)
            send(work.at[first, second], full_b.at[first, half], send_fb.at[first, half], recv_fb.at[first, half], ring_b[half])

    def settled(first):
        mine = combine(first, 0)
        if first in SUM_B:
            arrived(half_b.at[first], recv_hb.at[first, 0])
            mine = mine + half_b[first].astype(F32)
        for half in (0, 1):
            arrived(full_b.at[first, half], recv_fb.at[first, half])
            mine = mine + full_b[first, half].astype(F32)
        return mine

    gain_send(1, gain_sum(0))
    work[2, 0] = settled(2).astype(BF16)
    if SUM_A:
        send(work.at[2, 0], half_a, send_a.at[0], recv_a.at[0], far_a)
    else:
        for half in (0, 1):
            send(work.at[2, 0, half], half_a.at[half], send_a.at[half], recv_a.at[half], ring_a[half])
    for half, first in ((0, 1), (1, 3)):
        mine = settled(first)
        work[first, 0] = mine.astype(BF16)
        if not SUM_A:
            arrived(half_a.at[half], recv_a.at[half])
            work[first, 0, half] = (mine[half] + half_a[half].astype(F32)).astype(BF16)
        send(work.at[first, 0], full_a.at[half], send_a.at[2 + half], recv_a.at[2 + half], ring_a[half])
    mine = settled(0)
    totals = gain_sum(1)
    for load in loads:
        load.wait()
    gain = gain_ref[...]
    tower = lax.rem(z, 2)
    row = lax.broadcasted_iota(I32, (8, 128), 0)
    query_sum = jnp.sum(jnp.where(row == tower, totals, 0.0), axis=0, keepdims=True)
    key_sum = jnp.sum(jnp.where(row == 2 + tower, totals, 0.0), axis=0, keepdims=True)
    gain_out[0:1, :] = query_sum
    gain_out[1:2, :] = key_sum * scale / gain
    if SUM_A:
        arrived(half_a, recv_a.at[0])
        mine = mine + half_a[...].astype(F32)
    for half in (0, 1):
        arrived(full_a.at[half], recv_a.at[2 + half])
        mine = mine + full_a[half].astype(F32)
    blocks = jnp.concatenate([mine[0], mine[1]], axis=0)
    blocks = [blocks[j * 128 : (j + 1) * 128].T for j in range(3)]
    grad_keys = jnp.concatenate([block[:SEGMENT] for block in blocks], axis=0)
    grad_values = jnp.concatenate([block[SEGMENT:] for block in blocks], axis=0)
    value_out[...] = grad_values.astype(BF16)
    keys = key_ref[...].astype(F32)
    inverse = lax.rsqrt(jnp.mean(keys * keys, axis=-1, keepdims=True) + EPSILON)
    unit = keys * inverse
    e = grad_keys * scale * gain
    key_out[...] = (inverse * (e - unit * jnp.mean(e * unit, axis=-1, keepdims=True))).astype(BF16)
    for copy in started:
        copy.wait_send()


def reduced(part, gain_part, key_input, key_gain):
    rows, dim = key_input.shape
    whole = pl.BlockSpec(memory_space=VMEM)
    one = (2, rows, dim)
    return pl.pallas_call(
        reduce_kernel,
        out_shape=(
            VMEM((rows, dim), BF16),
            VMEM((rows, dim), BF16),
            VMEM((2, dim), F32),
        ),
        in_specs=[whole, whole, HBM, HBM],
        out_specs=(whole,) * 3,
        scratch_shapes=[
            VMEM((rows, dim), BF16), VMEM((1, dim), F32), DMA((2,)),
            VMEM((4, 4, *one), BF16), VMEM((4, 4, *one), BF16), VMEM((4, *one), BF16), VMEM((4, 2, *one), BF16),
            VMEM(one, BF16), VMEM((2, *one), BF16), VMEM((2, 16, 8, dim), F32),
            DMA((16,)), DMA((16,)), DMA((4, 2)), DMA((4, 2)), DMA((4, 2)), DMA((4, 2)), DMA((4,)), DMA((4,)),
            DMA((2, 16)), DMA((2, 16)),
        ],
        compiler_params=pltpu.CompilerParams(collective_id=1, has_side_effects=True, vmem_limit_bytes=16 * MIB),
        name="reduce_keys",
    )(part, gain_part, key_input, key_gain)


def shards(
    query_input, key_input, value_input, output_grad, query_gain, key_gain, stripe_order, frame_index, cross_blocks
):
    kv, lists, queries, grads, gain = gathered(
        key_input, value_input, key_gain, stripe_order[None], frame_index[None], cross_blocks,
        query_input, output_grad, query_gain,
    )
    query_grad, gain_part, part = attention(lists, queries, grads, gain, kv)
    key_grad, value_grad, gain_grads = reduced(part.reshape(kv.shape), gain_part, key_input, key_gain)
    return query_grad, key_grad, value_grad, gain_grads[:, None, :]


def solution(mesh):
    split = Mesh(mesh.devices.reshape(mesh.shape["heads"], mesh.shape["tower"], 2, 4, 2), AXES)
    in_specs = (
        P(TOWER_BLK, "heads"),
        P(TOWER_BLK, "heads"),
        P(TOWER_BLK, "heads"),
        P(TOWER_BLK, "heads"),
        P("tower", None),
        P("tower", None),
        P(),
        P(),
        P(),
    )
    out_specs = (
        P(TOWER_BLK, "heads"),
        P(TOWER_BLK, "heads"),
        P(TOWER_BLK, "heads"),
        P(None, "tower", None),
    )
    return jax.shard_map(shards, mesh=split, in_specs=in_specs, out_specs=out_specs, check_vma=False)
```

```python
import functools
import math

import jax
import jax.numpy as jnp
from jax import lax
from jax.experimental import pallas as pl
from jax.experimental.pallas import tpu as pltpu
from jax.sharding import Mesh
from jax.sharding import PartitionSpec as P

SEGMENT = 64
AXES = ("heads", "tower", "blk_0", "blk_1", "blk_2")
TOWER_BLK = ("tower", "blk_0", "blk_1", "blk_2")
EPSILON = 1e-06
NEGATIVE = -1e30
LOG2E = 1.4426950408889634
WIDE, NARROW, SMALL, LANES = 24, 12, 4, 256
MESH = pl.DeviceIdType.MESH
HBM = pl.BlockSpec(memory_space=pltpu.HBM)
MIB = 1024 * 1024
DIRECT_A, DIRECT_B, LATE = True, (2,), False
SUM_A, SUM_B = True, ()
STACKED = 448
MOST, CHUNKS, ROWS, SUMS = 67_043_328, 32 * 2 * 192 * 128 * 2, 3 * 192 * 896 * 2 + 3 * 128 * 512 * 2, 96 * 128 * 128 * 4
VMEM = pltpu.VMEM
DMA = pltpu.SemaphoreType.DMA
F32, BF16, I32 = jnp.float32, jnp.bfloat16, jnp.int32


def dot(a, b, left, right):
    return lax.dot_general(a, b, (((left,), (right,)), ((), ())), preferred_element_type=F32)


def position():
    z = lax.axis_index("blk_0") * 2 + lax.axis_index("tower")
    return lax.axis_index("heads"), lax.axis_index("blk_1"), z, lax.axis_index("blk_2")


def device(y, x, z, core):
    return (y, lax.rem(z, 2), lax.div(z, 2), x, core)


def place_of(x, z, core):
    return lax.rem(z, 2) * 16 + lax.div(z, 2) * 8 + x * 2 + core


def shifted(x, z, core, first, second):
    nx = lax.rem(x + (1 - core) * first + core * second, 4)
    nz = lax.rem(z + core * first + (1 - core) * second, 4)
    return nx, nz


def remote(src, dst, send, recv, target):
    return pltpu.make_async_remote_copy(
        src_ref=src, dst_ref=dst, send_sem=send, recv_sem=recv, device_id=target, device_id_type=MESH
    )


def meet(targets):
    barrier = pltpu.get_barrier_semaphore()
    for target in targets:
        pl.semaphore_signal(barrier, inc=1, device_id=target, device_id_type=MESH)
    return lambda: pl.semaphore_wait(barrier, len(targets))


def gather_kernel(
    key_hbm, value_hbm, gain_hbm, order_hbm, frame_hbm, cross_hbm, query_hbm, grad_hbm, query_gain_hbm,
    all_ref, list_ref, query_out, grad_out, query_gain_out, qn_out, qt_out, acc_out,
    key_ref, gain_ref, order_ref, frame_ref, cross_ref, mine, load_sem, own_sem, send_a, recv_a, send_b, recv_b, send_s, recv_s,
):
    y, x, z, core = position()

    def target(first, second):
        nx, nz = shifted(x, z, core, first, second)
        return device(y, nx, nz, core)

    def chunk(first, second):
        nx, nz = shifted(x, z, core, first, second)
        return place_of(nx, nz, core)

    loads = [
        pltpu.make_async_copy(src, dst, load_sem.at[n])
        for n, (src, dst) in enumerate((
            (key_hbm, key_ref),
            (gain_hbm, gain_ref),
            (value_hbm, mine.at[1]),
            (order_hbm, order_ref),
            (frame_hbm, frame_ref),
            (cross_hbm, cross_ref),
            (query_hbm, query_out),
            (grad_hbm, grad_out),
            (query_gain_hbm, query_gain_out),
        ))
    ]
    for load in loads:
        load.start()
    sibling = device(y, x, z, 1 - core)
    ring_a = (target(1, 0), target(3, 0))
    ring_b = (target(0, 1), target(0, 3))
    far_a, far_b = target(2, 0), target(0, 2)
    wait_all = meet((*ring_a, *ring_b, far_a, far_b, sibling))
    loads[0].wait()
    loads[1].wait()
    keys = key_ref[...].astype(F32)
    inverse = lax.rsqrt(jnp.mean(keys * keys, axis=-1, keepdims=True) + EPSILON)
    mine[0] = (keys * inverse * gain_ref[...]).astype(BF16)
    me = place_of(x, z, core)
    own = pltpu.make_async_copy(mine, all_ref.at[me], own_sem)
    started = []

    def send(src, dst, send_sem, recv_sem, to):
        copy = remote(src, dst, send_sem, recv_sem, to)
        copy.start()
        started.append(copy)

    def arrived(dst, recv_sem):
        remote(dst, dst, send_s.at[0], recv_sem, sibling).wait_recv()

    def spread(first, src):
        at = all_ref.at[chunk(first, 0)]
        send(src, at, send_b.at[first, 0], recv_b.at[first, 1], ring_b[0])
        send(src, at, send_b.at[first, 1], recv_b.at[first, 0], ring_b[1])
        if first in DIRECT_B:
            send(src, at, send_b.at[first, 2], recv_b.at[first, 2], far_b)

    def share(first, second, src):
        n = first * 4 + second
        send(src, all_ref.at[chunk(first, second)], send_s.at[n], recv_s.at[n], sibling)

    loads[2].wait()
    wait_all()
    own.start()
    send(mine, all_ref.at[me], send_a.at[0], recv_a.at[1], ring_a[0])
    send(mine, all_ref.at[me], send_a.at[1], recv_a.at[0], ring_a[1])
    if DIRECT_A:
        send(mine, all_ref.at[me], send_a.at[2], recv_a.at[2], far_a)
    if not LATE:
        spread(0, mine)
    share(0, 0, mine)

    lane = lax.broadcasted_iota(I32, (1, 128), 1)
    down = lax.broadcasted_iota(I32, (128, 128), 0)
    across = lax.broadcasted_iota(I32, (128, 128), 1)
    for load in loads[3:6]:
        load.wait()
    order = jnp.concatenate([order_ref[...], jnp.zeros((1, 32), I32)], axis=1)
    frame = jnp.concatenate([frame_ref[...], jnp.zeros((1, 80), I32)], axis=1)
    frame = jnp.where((lane >= 48) & (lane < 96), pltpu.roll(frame, 48, 1), -1)
    below = (across < down).astype(F32)
    start_of = (lax.shift_right_logical(down * 171, 9) * 384 + (down - 3 * lax.shift_right_logical(down * 171, 9)) * 64)
    image = me >= 16
    list_ref[...] = jnp.zeros_like(list_ref)
    counts = jnp.where(lane == 3, jnp.where(image, 0, 1), 0)
    for b in range(3):
        block = me * 3 + b
        here = lane == block
        slot = jnp.sum(jnp.where(here, order, 0), axis=-1, keepdims=True)
        seen = jnp.sum(jnp.where(here, frame, 0), axis=-1, keepdims=True)
        same = (lane >= 48) == image
        near = (order <= slot) | ((frame == seen) & (seen >= 0))
        crossing = jnp.concatenate([cross_ref[pl.ds(block, 1), :], jnp.zeros((1, 32), I32)], axis=1)
        opened = same | (crossing == 1)
        others = (near & opened & (lane < 96) & (lane != block)).astype(F32)
        column = jnp.broadcast_to(others, (128, 128)).T
        at = dot(below, column, 1, 0).astype(I32) + 1
        chosen = (column > 0.5) & (at == across)
        listed = jnp.sum(jnp.where(chosen, start_of, 0), axis=0, keepdims=True)
        first_start = me * 384 + b * 64
        list_ref[b : b + 1, :] = jnp.where(lane == 0, first_start, listed)
        count = 1 + jnp.sum(others, axis=-1, keepdims=True).astype(I32)
        counts = jnp.where(lane == b, count, counts)
    list_ref[3:4, :] = counts

    for load in loads[6:]:
        load.wait()
    query_gain = query_gain_out[...]
    per_group = query_out.shape[1] // 128
    for b in range(3):
        for h in range(per_group):
            q = query_out[b * SEGMENT : (b + 1) * SEGMENT, h * 128 : (h + 1) * 128].astype(F32)
            inverse = lax.rsqrt(jnp.mean(q * q, axis=-1, keepdims=True) + EPSILON)
            qn_out[b, h * SEGMENT : (h + 1) * SEGMENT, :] = (q * inverse * query_gain).astype(BF16)
        qt_out[b] = qn_out[b].astype(F32).T.astype(BF16)

    def clear(i, _):
        acc_out[i] = jnp.zeros((128, 128), F32)
        return 0

    lax.fori_loop(0, acc_out.shape[0], clear, 0)

    def from_a(slot, first, half, to, forward_recv):
        at = all_ref.at[chunk(first, 0)]
        arrived(at, recv_a.at[slot])
        if not DIRECT_A:
            send(at.at[half], at.at[half], send_a.at[2 + half], recv_a.at[forward_recv], to)
        spread(first, at)
        share(first, 0, at)

    def from_b(first, slot, second, half, to):
        at = all_ref.at[chunk(first, second)]
        arrived(at, recv_b.at[first, slot])
        if first not in DIRECT_B:
            send(at.at[half], at.at[half], send_b.at[first, 2 + half], recv_b.at[first, 2 + half], to)
        share(first, second, at)

    def both_b(first):
        from_b(first, 0, 1, 0, ring_b[1])
        from_b(first, 1, 3, 1, ring_b[0])

    from_a(0, 1, 0, ring_a[1], 2)
    from_a(1, 3, 1, ring_a[0], 3)
    if LATE:
        spread(0, mine)
    if not DIRECT_A:
        both_b(0)
    at = all_ref.at[chunk(2, 0)]
    if DIRECT_A:
        arrived(at, recv_a.at[2])
    else:
        arrived(at.at[0], recv_a.at[2])
        arrived(at.at[1], recv_a.at[3])
    spread(2, at)
    share(2, 0, at)
    if DIRECT_A:
        both_b(0)
    both_b(1)
    both_b(3)
    both_b(2)
    for first in (0, 1, 3, 2):
        at = all_ref.at[chunk(first, 2)]
        if first in DIRECT_B:
            arrived(at, recv_b.at[first, 2])
        else:
            arrived(at.at[0], recv_b.at[first, 2])
            arrived(at.at[1], recv_b.at[first, 3])
        share(first, 2, at)
    own.wait()
    for copy in started:
        copy.wait_send()
    for n in range(16):
        nx, nz = shifted(x, z, 1 - core, n // 4, n % 4)
        arrived(all_ref.at[place_of(nx, nz, 1 - core)], recv_s.at[n])


def gathered(key_input, value_input, key_gain, order, frame, cross, query_input, output_grad, query_gain):
    rows, dim = key_input.shape
    whole = pl.BlockSpec(memory_space=VMEM)
    return pl.pallas_call(
        gather_kernel,
        out_shape=(
            VMEM((32, 2, rows, dim), BF16), VMEM((8, 128), I32), VMEM(query_input.shape, BF16), VMEM(query_input.shape, BF16),
            VMEM((1, dim), F32), VMEM((3, STACKED, dim), BF16), VMEM((3, dim, STACKED), BF16), VMEM((96, dim, 128), F32),
        ),
        in_specs=[HBM] * 9,
        out_specs=(pl.BlockSpec(memory_space=pl.ANY), whole, *(whole,) * 6),
        scratch_shapes=[
            VMEM((rows, dim), BF16), VMEM((1, dim), F32), VMEM(order.shape, I32), VMEM(frame.shape, I32),
            VMEM(cross.shape, I32), VMEM((2, rows, dim), BF16), DMA((9,)), DMA, DMA((4,)), DMA((4,)), DMA((4, 4)), DMA((4, 4)), DMA((16,)), DMA((16,)),
        ],
        compiler_params=pltpu.CompilerParams(collective_id=0, has_side_effects=True, vmem_limit_bytes=MOST - CHUNKS - ROWS - SUMS - 24 * 1024),
        cost_estimate=pl.CostEstimate(flops=0, bytes_accessed=60_000_000, transcendentals=0),
        name="gather_keys",
    )(key_input, value_input, key_gain, order, frame, cross, query_input, output_grad, query_gain)


def attention_kernel(
    per_group, blocks, list_ref, query_ref, grad_ref, gain_ref, kv_ref, qn_ref, qt_ref, clear_ref,
    out_ref, gain_out, part_ref, acc,
    dop, dot_t, s_ref, w_ref, m_ref, l_ref, o_ref,
):
    dim = 128
    rows = SEGMENT * per_group
    log_scale = LOG2E / math.sqrt(dim)
    scale = 1.0 / math.sqrt(dim)
    places = kv_ref.shape[0] // 384
    is_text = list_ref[3, 3] == 1
    gain = gain_ref[...]

    def one_block(b, parts):
        query_part, all_part = parts
        base = pl.multiple_of(b * SEGMENT, SEGMENT)
        count = list_ref[3, b] - 1
        wide = lax.div(count, WIDE)
        small = lax.div(lax.rem(count, WIDE), NARROW)
        rest = lax.rem(count, NARROW)
        qn, qt = qn_ref.at[b], qt_ref.at[b]
        m_ref[...] = jnp.full_like(m_ref, NEGATIVE)
        l_ref[...] = jnp.zeros_like(l_ref)
        o_ref[...] = jnp.zeros_like(o_ref)

        def starts(first, size):
            return [pl.multiple_of(list_ref[b, first + j], SEGMENT) for j in range(size)]

        def first(step):
            def at(size):
                ps = [0] + [jnp.where(j <= rest, j, 0) for j in range(1, size)]
                return [pl.multiple_of(list_ref[b, p], SEGMENT) for p in ps]

            @pl.when(rest < SMALL)
            def _():
                step(0, at(SMALL))

            @pl.when(rest >= SMALL)
            def _():
                step(0, at(NARROW))

        def tile(at, offset):
            return jnp.concatenate([kv_ref[pl.ds(s + offset, SEGMENT), :] for s in at], axis=0)

        def number(start):
            return lax.div(start, 384) * 3 + lax.div(lax.rem(start, 384), SEGMENT)

        def logits(slot, at, masked):
            width = len(at) * SEGMENT
            s = dot(qn[...], tile(at, 0), 1, 1) * log_scale
            if masked:
                lane = lax.broadcasted_iota(I32, (rows, width), 1)
                row = lax.broadcasted_iota(I32, (rows, width), 0)
                limit = lax.rem(row, SEGMENT) + jnp.where(is_text, 0, SEGMENT)
                ok = (lane < (rest + 1) * SEGMENT) & ((lane >= SEGMENT) | (lane <= limit))
                s = jnp.where(ok, s, NEGATIVE)
            top = m_ref[...]
            for t in range(width // 128):
                top = jnp.maximum(top, s[:, t * 128 : (t + 1) * 128])
            m_ref[...] = top
            for t in range(width // LANES):
                s_ref[slot + t] = s[:, t * LANES : (t + 1) * LANES]

        def weights(slot, at):
            top = m_ref[...]
            total = l_ref[...]
            out = o_ref[...]
            tiles = len(at) * SEGMENT // LANES
            each = LANES // SEGMENT
            values = [tile(at[u * each : (u + 1) * each], 192).T for u in range(tiles)]
            ready = []
            for u in range(tiles + 1):
                if u < tiles:
                    parts = []
                    for t in range(LANES // 128):
                        w = jnp.exp2(s_ref[slot + u, :, t * 128 : (t + 1) * 128] - top)
                        total = total + w
                        parts.append(w.astype(BF16))
                    w = jnp.concatenate(parts, axis=1)
                    w_ref[slot + u] = w
                    ready.append(w)
                if u > 0:
                    out = out + dot(values[u - 1], ready[u - 1], 1, 1)
            l_ref[...] = total
            o_ref[...] = out

        def slopes(slot, at):
            delta = m_ref[...]
            low = lax.broadcasted_iota(I32, (dim, 128), 1) < SEGMENT
            tiles = len(at) * SEGMENT // LANES
            each = LANES // SEGMENT
            here = [at[u * each : (u + 1) * each] for u in range(tiles)]
            keys = [tile(h, 0).T for h in here]
            pushes, ds, done = {}, {}, {}
            grad_q = o_ref[...]
            for step in range(tiles + 2):
                if step < tiles:
                    pushes[step] = dot(dop[...], tile(here[step], 192), 1, 1)
                u = step - 1
                if 0 <= u < tiles:
                    w = w_ref[slot + u]
                    parts = []
                    for t in range(LANES // 128):
                        sl = slice(t * 128, (t + 1) * 128)
                        parts.append((w[:, sl].astype(F32) * (pushes[u][:, sl] - delta)).astype(BF16))
                    d = jnp.concatenate(parts, axis=1)
                    grad_q = grad_q + dot(keys[u], d, 1, 1)
                    done[u] = dot(qt[...], d, 1, 0), dot(dot_t[...], w, 1, 0)
                u = step - 2
                if 0 <= u < tiles:
                    dk, dv = done[u]
                    for t in range(LANES // 128):
                        sl = slice(t * 128, (t + 1) * 128)
                        k2, v2 = dk[:, sl], dv[:, sl]
                        acc[number(here[u][2 * t])] += jnp.where(low, k2, pltpu.roll(v2, SEGMENT, 1))
                        acc[number(here[u][2 * t + 1])] += jnp.where(low, pltpu.roll(k2, SEGMENT, 1), v2)
            o_ref[...] = grad_q

        def over(step):
            def narrow(g, _):
                step((1 + g) * (NARROW * SEGMENT // LANES), starts(1 + rest + g * NARROW, NARROW))
                return 0

            def broad(g, _):
                step(
                    (1 + small) * (NARROW * SEGMENT // LANES) + g * (WIDE * SEGMENT // LANES),
                    starts(1 + rest + small * NARROW + g * WIDE, WIDE),
                )
                return 0

            lax.fori_loop(0, small, narrow, 0)
            lax.fori_loop(0, wide, broad, 0)

        first(lambda slot, at: logits(slot, at, True))
        over(lambda slot, at: logits(slot, at, False))
        m_ref[...] = jnp.broadcast_to(jnp.max(m_ref[...], axis=-1, keepdims=True), m_ref.shape)
        first(weights)
        over(weights)
        total = jnp.sum(l_ref[...], axis=-1, keepdims=True)
        over_total = 1.0 / total
        output = (o_ref[...].T / total).astype(BF16).astype(F32)
        o_ref[...] = jnp.zeros_like(o_ref)
        for h in range(per_group):
            sl = slice(h * SEGMENT, (h + 1) * SEGMENT)
            g = grad_ref[pl.ds(base, SEGMENT), h * dim : (h + 1) * dim].astype(F32)
            g = (g * over_total[sl]).astype(BF16)
            dop[sl, :] = g
            delta = jnp.sum(g.astype(F32) * output[sl], axis=-1, keepdims=True)
            m_ref[sl, :] = jnp.broadcast_to(delta, (SEGMENT, 128))
        dot_t[...] = dop[...].astype(F32).T.astype(BF16)
        first(slopes)
        over(slopes)
        raw = o_ref[...].T
        for h in range(per_group):
            sl = slice(h * SEGMENT, (h + 1) * SEGMENT)
            q = query_ref[pl.ds(base, SEGMENT), h * dim : (h + 1) * dim].astype(F32)
            inverse = lax.rsqrt(jnp.mean(q * q, axis=-1, keepdims=True) + EPSILON)
            unit = q * inverse
            grad = raw[sl] * scale
            e = grad * gain
            dq = inverse * (e - unit * jnp.mean(e * unit, axis=-1, keepdims=True))
            out_ref[pl.ds(base, SEGMENT), h * dim : (h + 1) * dim] = dq.astype(BF16)
            query_part = query_part + jnp.sum((grad * unit).reshape(SEGMENT // 8, 8, dim), axis=0)
            terms = raw[sl] * qn[sl, :].astype(F32)
            all_part = all_part + jnp.sum(terms.reshape(SEGMENT // 8, 8, dim), axis=0)
        return query_part, all_part

    none = jnp.zeros((8, dim), F32)
    query_part, all_part = lax.fori_loop(0, blocks, one_block, (none, none))

    def finish(i, part):
        at = pl.multiple_of(i * 384, 384)
        mine = [acc[i * 3 + j].astype(BF16) for j in range(3)]
        keys = []
        for j in range(3):
            part_ref[i, j * dim : (j + 1) * dim, :] = mine[j]
            keys.append(kv_ref[pl.ds(at + j * SEGMENT, SEGMENT), :])
            keys.append(jnp.zeros_like(keys[-1]))
        part = part + dot(jnp.concatenate(mine, axis=1), jnp.concatenate(keys, axis=0), 1, 0)
        return part

    text = lax.fori_loop(0, places // 2, finish, jnp.zeros((dim, dim), F32), unroll=4)

    def store(i, _):
        for j in range(3):
            part_ref[i, j * dim : (j + 1) * dim, :] = acc[i * 3 + j].astype(BF16)
        return 0

    lax.fori_loop(places // 2, places, store, 0)
    diagonal = lax.broadcasted_iota(I32, (dim, dim), 0) == lax.broadcasted_iota(I32, (dim, dim), 1)
    text_sum = jnp.sum(jnp.where(diagonal, text, 0.0), axis=0, keepdims=True)
    image_sum = jnp.sum(all_part, axis=0, keepdims=True) - text_sum
    query_sum = jnp.sum(query_part, axis=0, keepdims=True)
    row = lax.broadcasted_iota(I32, (8, dim), 0)
    filled = jnp.where(row == jnp.where(is_text, 0, 1), query_sum, 0.0)
    filled = jnp.where(row == 2, text_sum, filled)
    gain_out[...] = jnp.where(row == 3, image_sum, filled)


def attention(lists, query_input, output_grad, query_gain, kv, qn, qt, sums):
    rows, columns = query_input.shape
    per_group = columns // 128
    stacked = SEGMENT * per_group
    segments = kv.shape[0] * 3
    slots = (segments + NARROW) * SEGMENT // LANES
    flat = kv.shape[0] * 384
    whole = pl.BlockSpec(memory_space=VMEM)
    return pl.pallas_call(
        functools.partial(attention_kernel, per_group, rows // SEGMENT),
        out_shape=(
            jax.ShapeDtypeStruct((rows, columns), BF16),
            VMEM((8, 128), F32),
            VMEM((kv.shape[0], 384, 128), BF16),
            VMEM(sums.shape, F32),
        ),
        in_specs=[pl.BlockSpec(memory_space=pltpu.SMEM)] + [whole] * 7,
        out_specs=(whole,) * 4,
        input_output_aliases={7: 3},
        scratch_shapes=[
            VMEM((stacked, 128), BF16), VMEM((128, stacked), BF16),
            VMEM((slots, stacked, LANES), F32), VMEM((slots, stacked, LANES), BF16),
            VMEM((stacked, 128), F32), VMEM((stacked, 128), F32), VMEM((128, stacked), F32),
        ],
        compiler_params=pltpu.CompilerParams(vmem_limit_bytes=40 * MIB),
        name="attention",
    )(lists, query_input, output_grad, query_gain, kv.reshape(flat, 128), qn, qt, sums)


def reduce_kernel(
    part_ref, gain_part, key_hbm, gain_hbm, key_out, value_out, gain_out,
    key_ref, gain_ref, load_sem, sib, work, half_b, full_b, half_a, full_a, sums,
    send_s, recv_s, send_hb, recv_hb, send_fb, recv_fb, send_a, recv_a, send_g, recv_g,
):
    y, x, z, core = position()
    scale = 1.0 / math.sqrt(128)

    def target(first, second):
        nx, nz = shifted(x, z, core, first, second)
        return device(y, nx, nz, core)

    sibling = device(y, x, z, 1 - core)
    ring_a = (target(1, 0), target(3, 0))
    ring_b = (target(0, 1), target(0, 3))
    lines = (
        (y * 2 + core, 8, lambda n: device(lax.div(n, 2), x, z, lax.rem(n, 2))),
        (x * 4 + z, 16, lambda n: device(y, lax.div(n, 4), lax.rem(n, 4), core)),
    )
    far_a, far_b = target(2, 0), target(0, 2)
    peers = [of(lax.rem(at + o, size)) for at, size, of in lines for o in range(1, size)]
    loads = [
        pltpu.make_async_copy(key_hbm, key_ref, load_sem.at[0]), pltpu.make_async_copy(gain_hbm, gain_ref, load_sem.at[1])
    ]
    for load in loads:
        load.start()
    meet(peers)()
    started = []

    def send(src, dst, send_sem, recv_sem, to):
        copy = remote(src, dst, send_sem, recv_sem, to)
        copy.start()
        started.append(copy)

    def arrived(dst, recv_sem):
        remote(dst, dst, send_s.at[0], recv_sem, sibling).wait_recv()

    def gain_send(stage, value):
        at, size, of = lines[stage]
        sums[stage, at] = value
        for o in range(1, size):
            send(sums.at[stage, at], sums.at[stage, at], send_g.at[stage, o], recv_g.at[stage, at], of(lax.rem(at + o, size)))

    def gain_sum(stage):
        at, size, of = lines[stage]
        for o in range(1, size):
            n = lax.rem(at + o, size)
            arrived(sums.at[stage, n], recv_g.at[stage, n])
        total = sums[stage, 0]
        for n in range(1, size):
            total = total + sums[stage, n]
        return total

    visit = [(first, second) for second in (2, 1, 3, 0) for first in (2, 1, 3, 0)]
    for first, second in visit:
        nx, nz = shifted(x, z, 1 - core, first, second)
        n = first * 4 + second
        send(part_ref.at[place_of(nx, nz, 1 - core)], sib.at[first, second], send_s.at[n], recv_s.at[n], sibling)
    gain_send(0, gain_part[...])

    def combine(first, second):
        n = first * 4 + second
        arrived(sib.at[first, second], recv_s.at[n])
        nx, nz = shifted(x, z, core, first, second)
        return part_ref[place_of(nx, nz, core)].astype(F32) + sib[first, second].astype(F32)

    for first in (2, 1, 3, 0):
        work[first, 2] = combine(first, 2).astype(BF16)
        if first in SUM_B:
            send(work.at[first, 2], half_b.at[first], send_hb.at[first, 0], recv_hb.at[first, 0], far_b)
        else:
            for half in (0, 1):
                send(work.at[first, 2, half], half_b.at[first, half], send_hb.at[first, half], recv_hb.at[first, half], ring_b[half])
    for first in (2, 1, 3, 0):
        for half, second in ((0, 1), (1, 3)):
            mine = combine(first, second)
            work[first, second] = mine.astype(BF16)
            if first not in SUM_B:
                arrived(half_b.at[first, half], recv_hb.at[first, half])
                work[first, second, half] = (mine[half] + half_b[first, half].astype(F32)).astype(BF16)
            send(work.at[first, second], full_b.at[first, half], send_fb.at[first, half], recv_fb.at[first, half], ring_b[half])

    def settled(first):
        mine = combine(first, 0)
        if first in SUM_B:
            arrived(half_b.at[first], recv_hb.at[first, 0])
            mine = mine + half_b[first].astype(F32)
        for half in (0, 1):
            arrived(full_b.at[first, half], recv_fb.at[first, half])
            mine = mine + full_b[first, half].astype(F32)
        return mine

    gain_send(1, gain_sum(0))
    work[2, 0] = settled(2).astype(BF16)
    if SUM_A:
        send(work.at[2, 0], half_a, send_a.at[0], recv_a.at[0], far_a)
    else:
        for half in (0, 1):
            send(work.at[2, 0, half], half_a.at[half], send_a.at[half], recv_a.at[half], ring_a[half])
    for half, first in ((0, 1), (1, 3)):
        mine = settled(first)
        work[first, 0] = mine.astype(BF16)
        if not SUM_A:
            arrived(half_a.at[half], recv_a.at[half])
            work[first, 0, half] = (mine[half] + half_a[half].astype(F32)).astype(BF16)
        send(work.at[first, 0], full_a.at[half], send_a.at[2 + half], recv_a.at[2 + half], ring_a[half])
    mine = settled(0)
    totals = gain_sum(1)
    for load in loads:
        load.wait()
    gain = gain_ref[...]
    tower = lax.rem(z, 2)
    row = lax.broadcasted_iota(I32, (8, 128), 0)
    query_sum = jnp.sum(jnp.where(row == tower, totals, 0.0), axis=0, keepdims=True)
    key_sum = jnp.sum(jnp.where(row == 2 + tower, totals, 0.0), axis=0, keepdims=True)
    gain_out[0:1, :] = query_sum
    gain_out[1:2, :] = key_sum * scale / gain
    if SUM_A:
        arrived(half_a, recv_a.at[0])
        mine = mine + half_a[...].astype(F32)
    for half in (0, 1):
        arrived(full_a.at[half], recv_a.at[2 + half])
        mine = mine + full_a[half].astype(F32)
    blocks = jnp.concatenate([mine[0], mine[1]], axis=0)
    blocks = [blocks[j * 128 : (j + 1) * 128].T for j in range(3)]
    grad_keys = jnp.concatenate([block[:SEGMENT] for block in blocks], axis=0)
    grad_values = jnp.concatenate([block[SEGMENT:] for block in blocks], axis=0)
    value_out[...] = grad_values.astype(BF16)
    keys = key_ref[...].astype(F32)
    inverse = lax.rsqrt(jnp.mean(keys * keys, axis=-1, keepdims=True) + EPSILON)
    unit = keys * inverse
    e = grad_keys * scale * gain
    key_out[...] = (inverse * (e - unit * jnp.mean(e * unit, axis=-1, keepdims=True))).astype(BF16)
    for copy in started:
        copy.wait_send()


def reduced(part, gain_part, key_input, key_gain):
    rows, dim = key_input.shape
    whole = pl.BlockSpec(memory_space=VMEM)
    one = (2, rows, dim)
    return pl.pallas_call(
        reduce_kernel,
        out_shape=(
            VMEM((rows, dim), BF16),
            VMEM((rows, dim), BF16),
            VMEM((2, dim), F32),
        ),
        in_specs=[whole, whole, HBM, HBM],
        out_specs=(whole,) * 3,
        scratch_shapes=[
            VMEM((rows, dim), BF16), VMEM((1, dim), F32), DMA((2,)),
            VMEM((4, 4, *one), BF16), VMEM((4, 4, *one), BF16), VMEM((4, *one), BF16), VMEM((4, 2, *one), BF16),
            VMEM(one, BF16), VMEM((2, *one), BF16), VMEM((2, 16, 8, dim), F32),
            DMA((16,)), DMA((16,)), DMA((4, 2)), DMA((4, 2)), DMA((4, 2)), DMA((4, 2)), DMA((4,)), DMA((4,)),
            DMA((2, 16)), DMA((2, 16)),
        ],
        compiler_params=pltpu.CompilerParams(collective_id=1, has_side_effects=True, vmem_limit_bytes=16 * MIB),
        name="reduce_keys",
    )(part, gain_part, key_input, key_gain)


def shards(
    query_input, key_input, value_input, output_grad, query_gain, key_gain, stripe_order, frame_index, cross_blocks
):
    kv, lists, queries, grads, gain, qn, qt, sums = gathered(
        key_input, value_input, key_gain, stripe_order[None], frame_index[None], cross_blocks,
        query_input, output_grad, query_gain,
    )
    query_grad, gain_part, part, _ = attention(lists, queries, grads, gain, kv, qn, qt, sums)
    key_grad, value_grad, gain_grads = reduced(part.reshape(kv.shape), gain_part, key_input, key_gain)
    return query_grad, key_grad, value_grad, gain_grads[:, None, :]


def solution(mesh):
    split = Mesh(mesh.devices.reshape(mesh.shape["heads"], mesh.shape["tower"], 2, 4, 2), AXES)
    in_specs = (
        P(TOWER_BLK, "heads"),
        P(TOWER_BLK, "heads"),
        P(TOWER_BLK, "heads"),
        P(TOWER_BLK, "heads"),
        P("tower", None),
        P("tower", None),
        P(),
        P(),
        P(),
    )
    out_specs = (
        P(TOWER_BLK, "heads"),
        P(TOWER_BLK, "heads"),
        P(TOWER_BLK, "heads"),
        P(None, "tower", None),
    )
    return jax.shard_map(shards, mesh=split, in_specs=in_specs, out_specs=out_specs, check_vma=False)
```

```python
import functools
import math

import jax
import jax.numpy as jnp
from jax import lax
from jax.experimental import pallas as pl
from jax.experimental.pallas import tpu as pltpu
from jax.sharding import Mesh
from jax.sharding import PartitionSpec as P

SEGMENT = 64
AXES = ("heads", "tower", "blk_0", "blk_1", "blk_2")
TOWER_BLK = ("tower", "blk_0", "blk_1", "blk_2")
EPSILON = 1e-06
NEGATIVE = -1e30
LOG2E = 1.4426950408889634
WIDE, NARROW, SMALL, LANES = 24, 12, 4, 256
MESH = pl.DeviceIdType.MESH
HBM = pl.BlockSpec(memory_space=pltpu.HBM)
MIB = 1024 * 1024
DIRECT_A, DIRECT_B, LATE = True, (2,), False
SUM_A, SUM_B = True, ()
STACKED = 448
MOST, CHUNKS, ROWS, SUMS = 67_043_328, 32 * 2 * 192 * 128 * 2, 3 * 192 * 896 * 2 + 3 * 128 * 512 * 2, 96 * 128 * 128 * 4
VMEM = pltpu.VMEM
DMA = pltpu.SemaphoreType.DMA
F32, BF16, I32 = jnp.float32, jnp.bfloat16, jnp.int32


def dot(a, b, left, right):
    return lax.dot_general(a, b, (((left,), (right,)), ((), ())), preferred_element_type=F32)


def position():
    z = lax.axis_index("blk_0") * 2 + lax.axis_index("tower")
    return lax.axis_index("heads"), lax.axis_index("blk_1"), z, lax.axis_index("blk_2")


def device(y, x, z, core):
    return (y, lax.rem(z, 2), lax.div(z, 2), x, core)


def place_of(x, z, core):
    return lax.rem(z, 2) * 16 + lax.div(z, 2) * 8 + x * 2 + core


def shifted(x, z, core, first, second):
    nx = lax.rem(x + (1 - core) * first + core * second, 4)
    nz = lax.rem(z + core * first + (1 - core) * second, 4)
    return nx, nz


def remote(src, dst, send, recv, target):
    return pltpu.make_async_remote_copy(
        src_ref=src, dst_ref=dst, send_sem=send, recv_sem=recv, device_id=target, device_id_type=MESH
    )


def meet(targets):
    barrier = pltpu.get_barrier_semaphore()
    for target in targets:
        pl.semaphore_signal(barrier, inc=1, device_id=target, device_id_type=MESH)
    return lambda: pl.semaphore_wait(barrier, len(targets))


def gather_kernel(
    key_hbm, value_hbm, gain_hbm, order_hbm, frame_hbm, cross_hbm, query_hbm, grad_hbm, query_gain_hbm,
    all_ref, list_ref, query_out, grad_out, query_gain_out, qn_out, qt_out, acc_out,
    key_ref, gain_ref, order_ref, frame_ref, cross_ref, mine, load_sem, own_sem, send_a, recv_a, send_b, recv_b, send_s, recv_s,
):
    y, x, z, core = position()

    def target(first, second):
        nx, nz = shifted(x, z, core, first, second)
        return device(y, nx, nz, core)

    def chunk(first, second):
        nx, nz = shifted(x, z, core, first, second)
        return place_of(nx, nz, core)

    loads = [
        pltpu.make_async_copy(src, dst, load_sem.at[n])
        for n, (src, dst) in enumerate((
            (key_hbm, key_ref),
            (gain_hbm, gain_ref),
            (value_hbm, mine.at[1]),
            (order_hbm, order_ref),
            (frame_hbm, frame_ref),
            (cross_hbm, cross_ref),
            (query_hbm, query_out),
            (grad_hbm, grad_out),
            (query_gain_hbm, query_gain_out),
        ))
    ]
    for load in loads:
        load.start()
    sibling = device(y, x, z, 1 - core)
    ring_a = (target(1, 0), target(3, 0))
    ring_b = (target(0, 1), target(0, 3))
    far_a, far_b = target(2, 0), target(0, 2)
    wait_all = meet((*ring_a, *ring_b, far_a, far_b, sibling))
    loads[0].wait()
    loads[1].wait()
    keys = key_ref[...].astype(F32)
    inverse = lax.rsqrt(jnp.mean(keys * keys, axis=-1, keepdims=True) + EPSILON)
    mine[0] = (keys * inverse * gain_ref[...]).astype(BF16)
    me = place_of(x, z, core)
    own = pltpu.make_async_copy(mine, all_ref.at[me], own_sem)
    started = []

    def send(src, dst, send_sem, recv_sem, to):
        copy = remote(src, dst, send_sem, recv_sem, to)
        copy.start()
        started.append(copy)

    def arrived(dst, recv_sem):
        remote(dst, dst, send_s.at[0], recv_sem, sibling).wait_recv()

    def spread(first, src):
        at = all_ref.at[chunk(first, 0)]
        send(src, at, send_b.at[first, 0], recv_b.at[first, 1], ring_b[0])
        send(src, at, send_b.at[first, 1], recv_b.at[first, 0], ring_b[1])
        if first in DIRECT_B:
            send(src, at, send_b.at[first, 2], recv_b.at[first, 2], far_b)

    def share(first, second, src):
        n = first * 4 + second
        send(src, all_ref.at[chunk(first, second)], send_s.at[n], recv_s.at[n], sibling)

    loads[2].wait()
    wait_all()
    own.start()
    send(mine, all_ref.at[me], send_a.at[0], recv_a.at[1], ring_a[0])
    send(mine, all_ref.at[me], send_a.at[1], recv_a.at[0], ring_a[1])
    if DIRECT_A:
        send(mine, all_ref.at[me], send_a.at[2], recv_a.at[2], far_a)
    if not LATE:
        spread(0, mine)
    share(0, 0, mine)

    lane = lax.broadcasted_iota(I32, (1, 128), 1)
    down = lax.broadcasted_iota(I32, (128, 128), 0)
    across = lax.broadcasted_iota(I32, (128, 128), 1)
    for load in loads[3:6]:
        load.wait()
    order = jnp.concatenate([order_ref[...], jnp.zeros((1, 32), I32)], axis=1)
    frame = jnp.concatenate([frame_ref[...], jnp.zeros((1, 80), I32)], axis=1)
    frame = jnp.where((lane >= 48) & (lane < 96), pltpu.roll(frame, 48, 1), -1)
    below = (across < down).astype(F32)
    start_of = (lax.shift_right_logical(down * 171, 9) * 384 + (down - 3 * lax.shift_right_logical(down * 171, 9)) * 64)
    image = me >= 16
    list_ref[...] = jnp.zeros_like(list_ref)
    counts = jnp.where(lane == 3, jnp.where(image, 0, 1), 0)
    for b in range(3):
        block = me * 3 + b
        here = lane == block
        slot = jnp.sum(jnp.where(here, order, 0), axis=-1, keepdims=True)
        seen = jnp.sum(jnp.where(here, frame, 0), axis=-1, keepdims=True)
        same = (lane >= 48) == image
        near = (order <= slot) | ((frame == seen) & (seen >= 0))
        crossing = jnp.concatenate([cross_ref[pl.ds(block, 1), :], jnp.zeros((1, 32), I32)], axis=1)
        opened = same | (crossing == 1)
        others = (near & opened & (lane < 96) & (lane != block)).astype(F32)
        column = jnp.broadcast_to(others, (128, 128)).T
        at = dot(below, column, 1, 0).astype(I32) + 1
        chosen = (column > 0.5) & (at == across)
        listed = jnp.sum(jnp.where(chosen, start_of, 0), axis=0, keepdims=True)
        first_start = me * 384 + b * 64
        list_ref[b : b + 1, :] = jnp.where(lane == 0, first_start, listed)
        count = 1 + jnp.sum(others, axis=-1, keepdims=True).astype(I32)
        counts = jnp.where(lane == b, count, counts)
    list_ref[3:4, :] = counts

    for load in loads[6:]:
        load.wait()
    query_gain = query_gain_out[...]
    per_group = query_out.shape[1] // 128
    for b in range(3):
        for h in range(per_group):
            q = query_out[b * SEGMENT : (b + 1) * SEGMENT, h * 128 : (h + 1) * 128].astype(F32)
            inverse = lax.rsqrt(jnp.mean(q * q, axis=-1, keepdims=True) + EPSILON)
            qn_out[b, h * SEGMENT : (h + 1) * SEGMENT, :] = (q * inverse * query_gain).astype(BF16)
        qt_out[b] = qn_out[b].astype(F32).T.astype(BF16)

    def clear(i, _):
        acc_out[i] = jnp.zeros((128, 128), F32)
        return 0

    lax.fori_loop(0, acc_out.shape[0], clear, 0)

    def from_a(slot, first, half, to, forward_recv):
        at = all_ref.at[chunk(first, 0)]
        arrived(at, recv_a.at[slot])
        if not DIRECT_A:
            send(at.at[half], at.at[half], send_a.at[2 + half], recv_a.at[forward_recv], to)
        spread(first, at)
        share(first, 0, at)

    def from_b(first, slot, second, half, to):
        at = all_ref.at[chunk(first, second)]
        arrived(at, recv_b.at[first, slot])
        if first not in DIRECT_B:
            send(at.at[half], at.at[half], send_b.at[first, 2 + half], recv_b.at[first, 2 + half], to)
        share(first, second, at)

    def both_b(first):
        from_b(first, 0, 1, 0, ring_b[1])
        from_b(first, 1, 3, 1, ring_b[0])

    from_a(0, 1, 0, ring_a[1], 2)
    from_a(1, 3, 1, ring_a[0], 3)
    if LATE:
        spread(0, mine)
    if not DIRECT_A:
        both_b(0)
    at = all_ref.at[chunk(2, 0)]
    if DIRECT_A:
        arrived(at, recv_a.at[2])
    else:
        arrived(at.at[0], recv_a.at[2])
        arrived(at.at[1], recv_a.at[3])
    spread(2, at)
    share(2, 0, at)
    if DIRECT_A:
        both_b(0)
    both_b(1)
    both_b(3)
    both_b(2)
    for first in (0, 1, 3, 2):
        at = all_ref.at[chunk(first, 2)]
        if first in DIRECT_B:
            arrived(at, recv_b.at[first, 2])
        else:
            arrived(at.at[0], recv_b.at[first, 2])
            arrived(at.at[1], recv_b.at[first, 3])
        share(first, 2, at)
    own.wait()
    for copy in started:
        copy.wait_send()
    for n in range(16):
        nx, nz = shifted(x, z, 1 - core, n // 4, n % 4)
        arrived(all_ref.at[place_of(nx, nz, 1 - core)], recv_s.at[n])


def gathered(key_input, value_input, key_gain, order, frame, cross, query_input, output_grad, query_gain):
    rows, dim = key_input.shape
    whole = pl.BlockSpec(memory_space=VMEM)
    return pl.pallas_call(
        gather_kernel,
        out_shape=(
            VMEM((32, 2, rows, dim), BF16), VMEM((8, 128), I32), VMEM(query_input.shape, BF16), VMEM(query_input.shape, BF16),
            VMEM((1, dim), F32), VMEM((3, STACKED, dim), BF16), VMEM((3, dim, STACKED), BF16), VMEM((96, dim, 128), F32),
        ),
        in_specs=[HBM] * 9,
        out_specs=(pl.BlockSpec(memory_space=pl.ANY), whole, *(whole,) * 6),
        scratch_shapes=[
            VMEM((rows, dim), BF16), VMEM((1, dim), F32), VMEM(order.shape, I32), VMEM(frame.shape, I32),
            VMEM(cross.shape, I32), VMEM((2, rows, dim), BF16), DMA((9,)), DMA, DMA((4,)), DMA((4,)), DMA((4, 4)), DMA((4, 4)), DMA((16,)), DMA((16,)),
        ],
        compiler_params=pltpu.CompilerParams(collective_id=0, has_side_effects=True, vmem_limit_bytes=MOST - CHUNKS - ROWS - SUMS - 24 * 1024),
        cost_estimate=pl.CostEstimate(flops=0, bytes_accessed=60_000_000, transcendentals=0),
        name="gather_keys",
    )(key_input, value_input, key_gain, order, frame, cross, query_input, output_grad, query_gain)


def attention_kernel(
    per_group, blocks, list_ref, query_ref, grad_ref, gain_ref, kv_ref, qn_ref, qt_ref, clear_ref,
    out_ref, gain_out, acc,
    dop, dot_t, s_ref, w_ref, m_ref, l_ref, o_ref,
):
    dim = 128
    rows = SEGMENT * per_group
    log_scale = LOG2E / math.sqrt(dim)
    scale = 1.0 / math.sqrt(dim)
    is_text = list_ref[3, 3] == 1
    gain = gain_ref[...]

    def one_block(b, parts):
        query_part, all_part = parts
        base = pl.multiple_of(b * SEGMENT, SEGMENT)
        count = list_ref[3, b] - 1
        wide = lax.div(count, WIDE)
        small = lax.div(lax.rem(count, WIDE), NARROW)
        rest = lax.rem(count, NARROW)
        qn, qt = qn_ref.at[b], qt_ref.at[b]
        m_ref[...] = jnp.full_like(m_ref, NEGATIVE)
        l_ref[...] = jnp.zeros_like(l_ref)
        o_ref[...] = jnp.zeros_like(o_ref)

        def starts(first, size):
            return [pl.multiple_of(list_ref[b, first + j], SEGMENT) for j in range(size)]

        def first(step):
            def at(size):
                ps = [0] + [jnp.where(j <= rest, j, 0) for j in range(1, size)]
                return [pl.multiple_of(list_ref[b, p], SEGMENT) for p in ps]

            @pl.when(rest < SMALL)
            def _():
                step(0, at(SMALL))

            @pl.when(rest >= SMALL)
            def _():
                step(0, at(NARROW))

        def tile(at, offset):
            return jnp.concatenate([kv_ref[pl.ds(s + offset, SEGMENT), :] for s in at], axis=0)

        def number(start):
            return lax.div(start, 384) * 3 + lax.div(lax.rem(start, 384), SEGMENT)

        def logits(slot, at, masked):
            width = len(at) * SEGMENT
            s = dot(qn[...], tile(at, 0), 1, 1) * log_scale
            if masked:
                lane = lax.broadcasted_iota(I32, (rows, width), 1)
                row = lax.broadcasted_iota(I32, (rows, width), 0)
                limit = lax.rem(row, SEGMENT) + jnp.where(is_text, 0, SEGMENT)
                ok = (lane < (rest + 1) * SEGMENT) & ((lane >= SEGMENT) | (lane <= limit))
                s = jnp.where(ok, s, NEGATIVE)
            top = m_ref[...]
            for t in range(width // 128):
                top = jnp.maximum(top, s[:, t * 128 : (t + 1) * 128])
            m_ref[...] = top
            for t in range(width // LANES):
                s_ref[slot + t] = s[:, t * LANES : (t + 1) * LANES]

        def weights(slot, at):
            top = m_ref[...]
            total = l_ref[...]
            out = o_ref[...]
            tiles = len(at) * SEGMENT // LANES
            each = LANES // SEGMENT
            values = [tile(at[u * each : (u + 1) * each], 192).T for u in range(tiles)]
            ready = []
            for u in range(tiles + 1):
                if u < tiles:
                    parts = []
                    for t in range(LANES // 128):
                        w = jnp.exp2(s_ref[slot + u, :, t * 128 : (t + 1) * 128] - top)
                        total = total + w
                        parts.append(w.astype(BF16))
                    w = jnp.concatenate(parts, axis=1)
                    w_ref[slot + u] = w
                    ready.append(w)
                if u > 0:
                    out = out + dot(values[u - 1], ready[u - 1], 1, 1)
            l_ref[...] = total
            o_ref[...] = out

        def slopes(slot, at):
            delta = m_ref[...]
            low = lax.broadcasted_iota(I32, (dim, 128), 1) < SEGMENT
            tiles = len(at) * SEGMENT // LANES
            each = LANES // SEGMENT
            here = [at[u * each : (u + 1) * each] for u in range(tiles)]
            keys = [tile(h, 0).T for h in here]
            pushes, ds, done = {}, {}, {}
            grad_q = o_ref[...]
            for step in range(tiles + 2):
                if step < tiles:
                    pushes[step] = dot(dop[...], tile(here[step], 192), 1, 1)
                u = step - 1
                if 0 <= u < tiles:
                    w = w_ref[slot + u]
                    parts = []
                    for t in range(LANES // 128):
                        sl = slice(t * 128, (t + 1) * 128)
                        parts.append((w[:, sl].astype(F32) * (pushes[u][:, sl] - delta)).astype(BF16))
                    d = jnp.concatenate(parts, axis=1)
                    grad_q = grad_q + dot(keys[u], d, 1, 1)
                    done[u] = dot(qt[...], d, 1, 0), dot(dot_t[...], w, 1, 0)
                u = step - 2
                if 0 <= u < tiles:
                    dk, dv = done[u]
                    for t in range(LANES // 128):
                        sl = slice(t * 128, (t + 1) * 128)
                        k2, v2 = dk[:, sl], dv[:, sl]
                        acc[number(here[u][2 * t])] += jnp.where(low, k2, pltpu.roll(v2, SEGMENT, 1))
                        acc[number(here[u][2 * t + 1])] += jnp.where(low, pltpu.roll(k2, SEGMENT, 1), v2)
            o_ref[...] = grad_q

        def over(step):
            def narrow(g, _):
                step((1 + g) * (NARROW * SEGMENT // LANES), starts(1 + rest + g * NARROW, NARROW))
                return 0

            def broad(g, _):
                step(
                    (1 + small) * (NARROW * SEGMENT // LANES) + g * (WIDE * SEGMENT // LANES),
                    starts(1 + rest + small * NARROW + g * WIDE, WIDE),
                )
                return 0

            lax.fori_loop(0, small, narrow, 0)
            lax.fori_loop(0, wide, broad, 0)

        first(lambda slot, at: logits(slot, at, True))
        over(lambda slot, at: logits(slot, at, False))
        m_ref[...] = jnp.broadcast_to(jnp.max(m_ref[...], axis=-1, keepdims=True), m_ref.shape)
        first(weights)
        over(weights)
        total = jnp.sum(l_ref[...], axis=-1, keepdims=True)
        over_total = 1.0 / total
        output = (o_ref[...].T / total).astype(BF16).astype(F32)
        o_ref[...] = jnp.zeros_like(o_ref)
        for h in range(per_group):
            sl = slice(h * SEGMENT, (h + 1) * SEGMENT)
            g = grad_ref[pl.ds(base, SEGMENT), h * dim : (h + 1) * dim].astype(F32)
            g = (g * over_total[sl]).astype(BF16)
            dop[sl, :] = g
            delta = jnp.sum(g.astype(F32) * output[sl], axis=-1, keepdims=True)
            m_ref[sl, :] = jnp.broadcast_to(delta, (SEGMENT, 128))
        dot_t[...] = dop[...].astype(F32).T.astype(BF16)
        first(slopes)
        over(slopes)
        raw = o_ref[...].T
        for h in range(per_group):
            sl = slice(h * SEGMENT, (h + 1) * SEGMENT)
            q = query_ref[pl.ds(base, SEGMENT), h * dim : (h + 1) * dim].astype(F32)
            inverse = lax.rsqrt(jnp.mean(q * q, axis=-1, keepdims=True) + EPSILON)
            unit = q * inverse
            grad = raw[sl] * scale
            e = grad * gain
            dq = inverse * (e - unit * jnp.mean(e * unit, axis=-1, keepdims=True))
            out_ref[pl.ds(base, SEGMENT), h * dim : (h + 1) * dim] = dq.astype(BF16)
            query_part = query_part + jnp.sum((grad * unit).reshape(SEGMENT // 8, 8, dim), axis=0)
            terms = raw[sl] * qn[sl, :].astype(F32)
            all_part = all_part + jnp.sum(terms.reshape(SEGMENT // 8, 8, dim), axis=0)
        return query_part, all_part

    none = jnp.zeros((8, dim), F32)
    query_part, all_part = lax.fori_loop(0, blocks, one_block, (none, none))

    query_sum = jnp.sum(query_part, axis=0, keepdims=True)
    row = lax.broadcasted_iota(I32, (8, dim), 0)
    filled = jnp.where(row == jnp.where(is_text, 0, 1), query_sum, 0.0)
    gain_out[...] = jnp.where(row == 2, jnp.sum(all_part, axis=0, keepdims=True), filled)


def attention(lists, query_input, output_grad, query_gain, kv, qn, qt, sums):
    rows, columns = query_input.shape
    per_group = columns // 128
    stacked = SEGMENT * per_group
    segments = kv.shape[0] * 3
    slots = (segments + NARROW) * SEGMENT // LANES
    flat = kv.shape[0] * 384
    whole = pl.BlockSpec(memory_space=VMEM)
    return pl.pallas_call(
        functools.partial(attention_kernel, per_group, rows // SEGMENT),
        out_shape=(
            jax.ShapeDtypeStruct((rows, columns), BF16),
            VMEM((8, 128), F32),
            VMEM(sums.shape, F32),
        ),
        in_specs=[pl.BlockSpec(memory_space=pltpu.SMEM)] + [whole] * 7,
        out_specs=(whole,) * 3,
        input_output_aliases={7: 2},
        scratch_shapes=[
            VMEM((stacked, 128), BF16), VMEM((128, stacked), BF16),
            VMEM((slots, stacked, LANES), F32), VMEM((slots, stacked, LANES), BF16),
            VMEM((stacked, 128), F32), VMEM((stacked, 128), F32), VMEM((128, stacked), F32),
        ],
        compiler_params=pltpu.CompilerParams(vmem_limit_bytes=40 * MIB),
        name="attention",
    )(lists, query_input, output_grad, query_gain, kv.reshape(flat, 128), qn, qt, sums)


def reduce_kernel(
    part_ref, kv_ref, gain_part, key_hbm, gain_hbm, key_out, value_out, gain_out,
    key_ref, gain_ref, load_sem, sent, sib, work, half_b, full_b, half_a, full_a, sums,
    send_s, recv_s, send_hb, recv_hb, send_fb, recv_fb, send_a, recv_a, send_g, recv_g,
):
    y, x, z, core = position()
    scale = 1.0 / math.sqrt(128)

    def target(first, second):
        nx, nz = shifted(x, z, core, first, second)
        return device(y, nx, nz, core)

    sibling = device(y, x, z, 1 - core)
    ring_a = (target(1, 0), target(3, 0))
    ring_b = (target(0, 1), target(0, 3))
    lines = (
        (y * 2 + core, 8, lambda n: device(lax.div(n, 2), x, z, lax.rem(n, 2))),
        (x * 4 + z, 16, lambda n: device(y, lax.div(n, 4), lax.rem(n, 4), core)),
    )
    far_a, far_b = target(2, 0), target(0, 2)
    peers = [of(lax.rem(at + o, size)) for at, size, of in lines for o in range(1, size)]
    loads = [
        pltpu.make_async_copy(key_hbm, key_ref, load_sem.at[0]), pltpu.make_async_copy(gain_hbm, gain_ref, load_sem.at[1])
    ]
    for load in loads:
        load.start()
    wait_all = meet(peers)
    visit = [(first, second) for second in (2, 1, 3, 0) for first in (2, 1, 3, 0)]

    def chunk(first, second, on):
        nx, nz = shifted(x, z, on, first, second)
        return part_ref[pl.ds(place_of(nx, nz, on) * 3, 3)].reshape(2, 192, 128)

    for first, second in visit:
        sent[first, second] = chunk(first, second, 1 - core).astype(BF16)
    wait_all()
    started = []

    def send(src, dst, send_sem, recv_sem, to):
        copy = remote(src, dst, send_sem, recv_sem, to)
        copy.start()
        started.append(copy)

    def arrived(dst, recv_sem):
        remote(dst, dst, send_s.at[0], recv_sem, sibling).wait_recv()

    def gain_send(stage, value):
        at, size, of = lines[stage]
        sums[stage, at] = value
        for o in range(1, size):
            send(sums.at[stage, at], sums.at[stage, at], send_g.at[stage, o], recv_g.at[stage, at], of(lax.rem(at + o, size)))

    def gain_sum(stage):
        at, size, of = lines[stage]
        for o in range(1, size):
            n = lax.rem(at + o, size)
            arrived(sums.at[stage, n], recv_g.at[stage, n])
        total = sums[stage, 0]
        for n in range(1, size):
            total = total + sums[stage, n]
        return total

    for first, second in visit:
        n = first * 4 + second
        send(sent.at[first, second], sib.at[first, second], send_s.at[n], recv_s.at[n], sibling)

    def text_terms(i, part):
        mine, keys = [], []
        for j in range(3):
            mine.append(part_ref[i * 3 + j].astype(BF16))
            keys.append(kv_ref[i, 0, j * SEGMENT : (j + 1) * SEGMENT, :])
            keys.append(jnp.zeros_like(keys[-1]))
        return part + dot(jnp.concatenate(mine, axis=1), jnp.concatenate(keys, axis=0), 1, 0)

    text = lax.fori_loop(0, 16, text_terms, jnp.zeros((128, 128), F32), unroll=4)
    diagonal = lax.broadcasted_iota(I32, (128, 128), 0) == lax.broadcasted_iota(I32, (128, 128), 1)
    text_sum = jnp.sum(jnp.where(diagonal, text, 0.0), axis=0, keepdims=True)
    given = gain_part[...]
    slot = lax.broadcasted_iota(I32, (8, 128), 0)
    gain_send(0, jnp.where(slot == 2, text_sum, jnp.where(slot == 3, given[2:3] - text_sum, given)))

    def combine(first, second):
        n = first * 4 + second
        arrived(sib.at[first, second], recv_s.at[n])
        return chunk(first, second, core) + sib[first, second].astype(F32)

    for first in (2, 1, 3, 0):
        work[first, 2] = combine(first, 2).astype(BF16)
        if first in SUM_B:
            send(work.at[first, 2], half_b.at[first], send_hb.at[first, 0], recv_hb.at[first, 0], far_b)
        else:
            for half in (0, 1):
                send(work.at[first, 2, half], half_b.at[first, half], send_hb.at[first, half], recv_hb.at[first, half], ring_b[half])
    for first in (2, 1, 3, 0):
        for half, second in ((0, 1), (1, 3)):
            mine = combine(first, second)
            work[first, second] = mine.astype(BF16)
            if first not in SUM_B:
                arrived(half_b.at[first, half], recv_hb.at[first, half])
                work[first, second, half] = (mine[half] + half_b[first, half].astype(F32)).astype(BF16)
            send(work.at[first, second], full_b.at[first, half], send_fb.at[first, half], recv_fb.at[first, half], ring_b[half])

    def settled(first):
        mine = combine(first, 0)
        if first in SUM_B:
            arrived(half_b.at[first], recv_hb.at[first, 0])
            mine = mine + half_b[first].astype(F32)
        for half in (0, 1):
            arrived(full_b.at[first, half], recv_fb.at[first, half])
            mine = mine + full_b[first, half].astype(F32)
        return mine

    gain_send(1, gain_sum(0))
    work[2, 0] = settled(2).astype(BF16)
    if SUM_A:
        send(work.at[2, 0], half_a, send_a.at[0], recv_a.at[0], far_a)
    else:
        for half in (0, 1):
            send(work.at[2, 0, half], half_a.at[half], send_a.at[half], recv_a.at[half], ring_a[half])
    for half, first in ((0, 1), (1, 3)):
        mine = settled(first)
        work[first, 0] = mine.astype(BF16)
        if not SUM_A:
            arrived(half_a.at[half], recv_a.at[half])
            work[first, 0, half] = (mine[half] + half_a[half].astype(F32)).astype(BF16)
        send(work.at[first, 0], full_a.at[half], send_a.at[2 + half], recv_a.at[2 + half], ring_a[half])
    mine = settled(0)
    totals = gain_sum(1)
    for load in loads:
        load.wait()
    gain = gain_ref[...]
    tower = lax.rem(z, 2)
    row = lax.broadcasted_iota(I32, (8, 128), 0)
    query_sum = jnp.sum(jnp.where(row == tower, totals, 0.0), axis=0, keepdims=True)
    key_sum = jnp.sum(jnp.where(row == 2 + tower, totals, 0.0), axis=0, keepdims=True)
    gain_out[0:1, :] = query_sum
    gain_out[1:2, :] = key_sum * scale / gain
    if SUM_A:
        arrived(half_a, recv_a.at[0])
        mine = mine + half_a[...].astype(F32)
    for half in (0, 1):
        arrived(full_a.at[half], recv_a.at[2 + half])
        mine = mine + full_a[half].astype(F32)
    blocks = jnp.concatenate([mine[0], mine[1]], axis=0)
    blocks = [blocks[j * 128 : (j + 1) * 128].T for j in range(3)]
    grad_keys = jnp.concatenate([block[:SEGMENT] for block in blocks], axis=0)
    grad_values = jnp.concatenate([block[SEGMENT:] for block in blocks], axis=0)
    value_out[...] = grad_values.astype(BF16)
    keys = key_ref[...].astype(F32)
    inverse = lax.rsqrt(jnp.mean(keys * keys, axis=-1, keepdims=True) + EPSILON)
    unit = keys * inverse
    e = grad_keys * scale * gain
    key_out[...] = (inverse * (e - unit * jnp.mean(e * unit, axis=-1, keepdims=True))).astype(BF16)
    for copy in started:
        copy.wait_send()


def reduced(part, kv, gain_part, key_input, key_gain):
    rows, dim = key_input.shape
    whole = pl.BlockSpec(memory_space=VMEM)
    one = (2, rows, dim)
    return pl.pallas_call(
        reduce_kernel,
        out_shape=(
            VMEM((rows, dim), BF16),
            VMEM((rows, dim), BF16),
            VMEM((2, dim), F32),
        ),
        in_specs=[whole, whole, whole, HBM, HBM],
        out_specs=(whole,) * 3,
        scratch_shapes=[
            VMEM((rows, dim), BF16), VMEM((1, dim), F32), DMA((2,)), VMEM((4, 4, *one), BF16),
            VMEM((4, 4, *one), BF16), VMEM((4, 4, *one), BF16), VMEM((4, *one), BF16), VMEM((4, 2, *one), BF16),
            VMEM(one, BF16), VMEM((2, *one), BF16), VMEM((2, 16, 8, dim), F32),
            DMA((16,)), DMA((16,)), DMA((4, 2)), DMA((4, 2)), DMA((4, 2)), DMA((4, 2)), DMA((4,)), DMA((4,)),
            DMA((2, 16)), DMA((2, 16)),
        ],
        compiler_params=pltpu.CompilerParams(collective_id=1, has_side_effects=True, vmem_limit_bytes=16 * MIB),
        name="reduce_keys",
    )(part, kv, gain_part, key_input, key_gain)


def shards(
    query_input, key_input, value_input, output_grad, query_gain, key_gain, stripe_order, frame_index, cross_blocks
):
    kv, lists, queries, grads, gain, qn, qt, sums = gathered(
        key_input, value_input, key_gain, stripe_order[None], frame_index[None], cross_blocks,
        query_input, output_grad, query_gain,
    )
    query_grad, gain_part, part = attention(lists, queries, grads, gain, kv, qn, qt, sums)
    key_grad, value_grad, gain_grads = reduced(part, kv, gain_part, key_input, key_gain)
    return query_grad, key_grad, value_grad, gain_grads[:, None, :]


def solution(mesh):
    split = Mesh(mesh.devices.reshape(mesh.shape["heads"], mesh.shape["tower"], 2, 4, 2), AXES)
    in_specs = (
        P(TOWER_BLK, "heads"),
        P(TOWER_BLK, "heads"),
        P(TOWER_BLK, "heads"),
        P(TOWER_BLK, "heads"),
        P("tower", None),
        P("tower", None),
        P(),
        P(),
        P(),
    )
    out_specs = (
        P(TOWER_BLK, "heads"),
        P(TOWER_BLK, "heads"),
        P(TOWER_BLK, "heads"),
        P(None, "tower", None),
    )
    return jax.shard_map(shards, mesh=split, in_specs=in_specs, out_specs=out_specs, check_vma=False)
```

```python
import functools
import math

import jax
import jax.numpy as jnp
from jax import lax
from jax.experimental import pallas as pl
from jax.experimental.pallas import tpu as pltpu
from jax.sharding import Mesh
from jax.sharding import PartitionSpec as P

SEGMENT = 64
AXES = ("heads", "tower", "blk_0", "blk_1", "blk_2")
TOWER_BLK = ("tower", "blk_0", "blk_1", "blk_2")
EPSILON = 1e-06
NEGATIVE = -1e30
LOG2E = 1.4426950408889634
WIDE, NARROW, SMALL, LANES = 24, 12, 4, 256
MESH = pl.DeviceIdType.MESH
HBM = pl.BlockSpec(memory_space=pltpu.HBM)
MIB = 1024 * 1024
DIRECT_A, DIRECT_B, LATE = True, (2,), False
SUM_A, SUM_B = True, ()
STACKED = 448
MOST, CHUNKS, ROWS, SUMS = 67_043_328, 32 * 2 * 192 * 128 * 2, 3 * 192 * 896 * 2 + 3 * 128 * 512 * 2, 96 * 128 * 128 * 4
VMEM = pltpu.VMEM
DMA = pltpu.SemaphoreType.DMA
F32, BF16, I32 = jnp.float32, jnp.bfloat16, jnp.int32


def dot(a, b, left, right):
    return lax.dot_general(a, b, (((left,), (right,)), ((), ())), preferred_element_type=F32)


def position():
    z = lax.axis_index("blk_0") * 2 + lax.axis_index("tower")
    return lax.axis_index("heads"), lax.axis_index("blk_1"), z, lax.axis_index("blk_2")


def device(y, x, z, core):
    return (y, lax.rem(z, 2), lax.div(z, 2), x, core)


def place_of(x, z, core):
    return lax.rem(z, 2) * 16 + lax.div(z, 2) * 8 + x * 2 + core


def shifted(x, z, core, first, second):
    nx = lax.rem(x + (1 - core) * first + core * second, 4)
    nz = lax.rem(z + core * first + (1 - core) * second, 4)
    return nx, nz


def remote(src, dst, send, recv, target):
    return pltpu.make_async_remote_copy(
        src_ref=src, dst_ref=dst, send_sem=send, recv_sem=recv, device_id=target, device_id_type=MESH
    )


def meet(targets):
    barrier = pltpu.get_barrier_semaphore()
    for target in targets:
        pl.semaphore_signal(barrier, inc=1, device_id=target, device_id_type=MESH)
    return lambda: pl.semaphore_wait(barrier, len(targets))


def gather_kernel(
    key_hbm, value_hbm, gain_hbm, order_hbm, frame_hbm, cross_hbm, query_hbm, grad_hbm, query_gain_hbm,
    all_ref, list_ref, query_out, grad_out, query_gain_out, qn_out, qt_out, acc_out,
    key_ref, gain_ref, order_ref, frame_ref, cross_ref, mine, load_sem, own_sem, send_a, recv_a, send_b, recv_b, send_s, recv_s,
):
    y, x, z, core = position()

    def target(first, second):
        nx, nz = shifted(x, z, core, first, second)
        return device(y, nx, nz, core)

    def chunk(first, second):
        nx, nz = shifted(x, z, core, first, second)
        return place_of(nx, nz, core)

    loads = [
        pltpu.make_async_copy(src, dst, load_sem.at[n])
        for n, (src, dst) in enumerate((
            (key_hbm, key_ref),
            (gain_hbm, gain_ref),
            (value_hbm, mine.at[1]),
            (order_hbm, order_ref),
            (frame_hbm, frame_ref),
            (cross_hbm, cross_ref),
            (query_hbm, query_out),
            (grad_hbm, grad_out),
            (query_gain_hbm, query_gain_out),
        ))
    ]
    for load in loads:
        load.start()
    sibling = device(y, x, z, 1 - core)
    ring_a = (target(1, 0), target(3, 0))
    ring_b = (target(0, 1), target(0, 3))
    far_a, far_b = target(2, 0), target(0, 2)
    wait_all = meet((*ring_a, *ring_b, far_a, far_b, sibling))
    loads[0].wait()
    loads[1].wait()
    keys = key_ref[...].astype(F32)
    inverse = lax.rsqrt(jnp.mean(keys * keys, axis=-1, keepdims=True) + EPSILON)
    mine[0] = (keys * inverse * gain_ref[...]).astype(BF16)
    me = place_of(x, z, core)
    own = pltpu.make_async_copy(mine, all_ref.at[me], own_sem)
    started = []

    def send(src, dst, send_sem, recv_sem, to):
        copy = remote(src, dst, send_sem, recv_sem, to)
        copy.start()
        started.append(copy)

    def arrived(dst, recv_sem):
        remote(dst, dst, send_s.at[0], recv_sem, sibling).wait_recv()

    def spread(first, src):
        at = all_ref.at[chunk(first, 0)]
        send(src, at, send_b.at[first, 0], recv_b.at[first, 1], ring_b[0])
        send(src, at, send_b.at[first, 1], recv_b.at[first, 0], ring_b[1])
        if first in DIRECT_B:
            send(src, at, send_b.at[first, 2], recv_b.at[first, 2], far_b)

    def share(first, second, src):
        n = first * 4 + second
        send(src, all_ref.at[chunk(first, second)], send_s.at[n], recv_s.at[n], sibling)

    loads[2].wait()
    wait_all()
    own.start()
    send(mine, all_ref.at[me], send_a.at[0], recv_a.at[1], ring_a[0])
    send(mine, all_ref.at[me], send_a.at[1], recv_a.at[0], ring_a[1])
    if DIRECT_A:
        send(mine, all_ref.at[me], send_a.at[2], recv_a.at[2], far_a)
    if not LATE:
        spread(0, mine)
    share(0, 0, mine)

    lane = lax.broadcasted_iota(I32, (1, 128), 1)
    down = lax.broadcasted_iota(I32, (128, 128), 0)
    across = lax.broadcasted_iota(I32, (128, 128), 1)
    for load in loads[3:6]:
        load.wait()
    order = jnp.concatenate([order_ref[...], jnp.zeros((1, 32), I32)], axis=1)
    frame = jnp.concatenate([frame_ref[...], jnp.zeros((1, 80), I32)], axis=1)
    frame = jnp.where((lane >= 48) & (lane < 96), pltpu.roll(frame, 48, 1), -1)
    below = (across < down).astype(F32)
    start_of = (lax.shift_right_logical(down * 171, 9) * 384 + (down - 3 * lax.shift_right_logical(down * 171, 9)) * 64)
    image = me >= 16
    list_ref[...] = jnp.zeros_like(list_ref)
    counts = jnp.where(lane == 3, jnp.where(image, 0, 1), 0)
    for b in range(3):
        block = me * 3 + b
        here = lane == block
        slot = jnp.sum(jnp.where(here, order, 0), axis=-1, keepdims=True)
        seen = jnp.sum(jnp.where(here, frame, 0), axis=-1, keepdims=True)
        same = (lane >= 48) == image
        near = (order <= slot) | ((frame == seen) & (seen >= 0))
        crossing = jnp.concatenate([cross_ref[pl.ds(block, 1), :], jnp.zeros((1, 32), I32)], axis=1)
        opened = same | (crossing == 1)
        others = (near & opened & (lane < 96) & (lane != block)).astype(F32)
        column = jnp.broadcast_to(others, (128, 128)).T
        at = dot(below, column, 1, 0).astype(I32) + 1
        chosen = (column > 0.5) & (at == across)
        listed = jnp.sum(jnp.where(chosen, start_of, 0), axis=0, keepdims=True)
        first_start = me * 384 + b * 64
        list_ref[b : b + 1, :] = jnp.where(lane == 0, first_start, listed)
        count = 1 + jnp.sum(others, axis=-1, keepdims=True).astype(I32)
        counts = jnp.where(lane == b, count, counts)
    list_ref[3:4, :] = counts

    for load in loads[6:]:
        load.wait()
    query_gain = query_gain_out[...]
    per_group = query_out.shape[1] // 128
    for b in range(3):
        for h in range(per_group):
            q = query_out[b * SEGMENT : (b + 1) * SEGMENT, h * 128 : (h + 1) * 128].astype(F32)
            inverse = lax.rsqrt(jnp.mean(q * q, axis=-1, keepdims=True) + EPSILON)
            qn_out[b, h * SEGMENT : (h + 1) * SEGMENT, :] = (q * inverse * query_gain).astype(BF16)
        qt_out[b] = qn_out[b].astype(F32).T.astype(BF16)

    def clear(i, _):
        acc_out[i] = jnp.zeros((128, 128), F32)
        return 0

    lax.fori_loop(0, acc_out.shape[0], clear, 0)

    def from_a(slot, first, half, to, forward_recv):
        at = all_ref.at[chunk(first, 0)]
        arrived(at, recv_a.at[slot])
        if not DIRECT_A:
            send(at.at[half], at.at[half], send_a.at[2 + half], recv_a.at[forward_recv], to)
        spread(first, at)
        share(first, 0, at)

    def from_b(first, slot, second, half, to):
        at = all_ref.at[chunk(first, second)]
        arrived(at, recv_b.at[first, slot])
        if first not in DIRECT_B:
            send(at.at[half], at.at[half], send_b.at[first, 2 + half], recv_b.at[first, 2 + half], to)
        share(first, second, at)

    def both_b(first):
        from_b(first, 0, 1, 0, ring_b[1])
        from_b(first, 1, 3, 1, ring_b[0])

    from_a(0, 1, 0, ring_a[1], 2)
    from_a(1, 3, 1, ring_a[0], 3)
    if LATE:
        spread(0, mine)
    if not DIRECT_A:
        both_b(0)
    at = all_ref.at[chunk(2, 0)]
    if DIRECT_A:
        arrived(at, recv_a.at[2])
    else:
        arrived(at.at[0], recv_a.at[2])
        arrived(at.at[1], recv_a.at[3])
    spread(2, at)
    share(2, 0, at)
    if DIRECT_A:
        both_b(0)
    both_b(1)
    both_b(3)
    both_b(2)
    for first in (0, 1, 3, 2):
        at = all_ref.at[chunk(first, 2)]
        if first in DIRECT_B:
            arrived(at, recv_b.at[first, 2])
        else:
            arrived(at.at[0], recv_b.at[first, 2])
            arrived(at.at[1], recv_b.at[first, 3])
        share(first, 2, at)
    own.wait()
    for copy in started:
        copy.wait_send()
    for n in range(16):
        nx, nz = shifted(x, z, 1 - core, n // 4, n % 4)
        arrived(all_ref.at[place_of(nx, nz, 1 - core)], recv_s.at[n])


def gathered(key_input, value_input, key_gain, order, frame, cross, query_input, output_grad, query_gain):
    rows, dim = key_input.shape
    whole = pl.BlockSpec(memory_space=VMEM)
    return pl.pallas_call(
        gather_kernel,
        out_shape=(
            VMEM((32, 2, rows, dim), BF16), VMEM((8, 128), I32), VMEM(query_input.shape, BF16), VMEM(query_input.shape, BF16),
            VMEM((1, dim), F32), VMEM((3, STACKED, dim), BF16), VMEM((3, dim, STACKED), BF16), VMEM((96, dim, 128), F32),
        ),
        in_specs=[HBM] * 9,
        out_specs=(pl.BlockSpec(memory_space=pl.ANY), whole, *(whole,) * 6),
        scratch_shapes=[
            VMEM((rows, dim), BF16), VMEM((1, dim), F32), VMEM(order.shape, I32), VMEM(frame.shape, I32),
            VMEM(cross.shape, I32), VMEM((2, rows, dim), BF16), DMA((9,)), DMA, DMA((4,)), DMA((4,)), DMA((4, 4)), DMA((4, 4)), DMA((16,)), DMA((16,)),
        ],
        compiler_params=pltpu.CompilerParams(collective_id=0, has_side_effects=True, vmem_limit_bytes=MOST - CHUNKS - ROWS - SUMS - 24 * 1024),
        cost_estimate=pl.CostEstimate(flops=0, bytes_accessed=60_000_000, transcendentals=0),
        name="gather_keys",
    )(key_input, value_input, key_gain, order, frame, cross, query_input, output_grad, query_gain)


def attention_kernel(
    per_group, blocks, list_ref, query_ref, grad_ref, gain_ref, kv_ref, qn_ref, qt_ref, clear_ref,
    out_ref, gain_out, acc,
    dop, dot_t, s_ref, w_ref, m_ref, l_ref, o_ref,
):
    dim = 128
    rows = SEGMENT * per_group
    log_scale = LOG2E / math.sqrt(dim)
    scale = 1.0 / math.sqrt(dim)
    is_text = list_ref[3, 3] == 1
    gain = gain_ref[...]

    def one_block(b, parts):
        query_part, all_part = parts
        base = pl.multiple_of(b * SEGMENT, SEGMENT)
        count = list_ref[3, b] - 1
        wide = lax.div(count, WIDE)
        small = lax.div(lax.rem(count, WIDE), NARROW)
        rest = lax.rem(count, NARROW)
        qn, qt = qn_ref.at[b], qt_ref.at[b]
        m_ref[...] = jnp.full_like(m_ref, NEGATIVE)
        l_ref[...] = jnp.zeros_like(l_ref)
        o_ref[...] = jnp.zeros_like(o_ref)

        def starts(first, size):
            return [pl.multiple_of(list_ref[b, first + j], SEGMENT) for j in range(size)]

        def first(step):
            def at(size):
                ps = [0] + [jnp.where(j <= rest, j, 0) for j in range(1, size)]
                return [pl.multiple_of(list_ref[b, p], SEGMENT) for p in ps]

            @pl.when(rest < SMALL)
            def _():
                step(0, at(SMALL))

            @pl.when(rest >= SMALL)
            def _():
                step(0, at(NARROW))

        def tile(at, offset):
            return jnp.concatenate([kv_ref[pl.ds(s + offset, SEGMENT), :] for s in at], axis=0)

        def number(start):
            return lax.div(start, 384) * 3 + lax.div(lax.rem(start, 384), SEGMENT)

        def logits(slot, at, masked):
            width = len(at) * SEGMENT
            s = dot(qn[...], tile(at, 0), 1, 1) * log_scale
            if masked:
                lane = lax.broadcasted_iota(I32, (rows, width), 1)
                row = lax.broadcasted_iota(I32, (rows, width), 0)
                limit = lax.rem(row, SEGMENT) + jnp.where(is_text, 0, SEGMENT)
                ok = (lane < (rest + 1) * SEGMENT) & ((lane >= SEGMENT) | (lane <= limit))
                s = jnp.where(ok, s, NEGATIVE)
            top = m_ref[...]
            for t in range(width // 128):
                top = jnp.maximum(top, s[:, t * 128 : (t + 1) * 128])
            m_ref[...] = top
            for t in range(width // LANES):
                s_ref[slot + t] = s[:, t * LANES : (t + 1) * LANES]

        def weights(slot, at):
            top = m_ref[...]
            total = l_ref[...]
            out = o_ref[...]
            tiles = len(at) * SEGMENT // LANES
            each = LANES // SEGMENT
            values = [tile(at[u * each : (u + 1) * each], 192).T for u in range(tiles)]
            ready = []
            for u in range(tiles + 1):
                if u < tiles:
                    parts = []
                    for t in range(LANES // 128):
                        w = jnp.exp2(s_ref[slot + u, :, t * 128 : (t + 1) * 128] - top)
                        total = total + w
                        parts.append(w.astype(BF16))
                    w = jnp.concatenate(parts, axis=1)
                    w_ref[slot + u] = w
                    ready.append(w)
                if u > 0:
                    out = out + dot(values[u - 1], ready[u - 1], 1, 1)
            l_ref[...] = total
            o_ref[...] = out

        def slopes(slot, at):
            delta = m_ref[...]
            low = lax.broadcasted_iota(I32, (dim, 128), 1) < SEGMENT
            tiles = len(at) * SEGMENT // LANES
            each = LANES // SEGMENT
            here = [at[u * each : (u + 1) * each] for u in range(tiles)]
            pushes, dvs, done = {}, {}, {}
            grad_q = o_ref[...]
            for step in range(tiles + 2):
                if step < tiles:
                    pushes[step] = dot(dop[...], tile(here[step], 192), 1, 1)
                    dvs[step] = dot(dot_t[...], w_ref[slot + step], 1, 0)
                u = step - 1
                if 0 <= u < tiles:
                    w = w_ref[slot + u]
                    parts = []
                    for t in range(LANES // 128):
                        sl = slice(t * 128, (t + 1) * 128)
                        parts.append((w[:, sl].astype(F32) * (pushes[u][:, sl] - delta)).astype(BF16))
                    d = jnp.concatenate(parts, axis=1)
                    grad_q = grad_q + dot(tile(here[u], 0).T, d, 1, 1)
                    done[u] = dot(qt[...], d, 1, 0), dvs[u]
                u = step - 2
                if 0 <= u < tiles:
                    dk, dv = done[u]
                    for t in range(LANES // 128):
                        sl = slice(t * 128, (t + 1) * 128)
                        k2, v2 = dk[:, sl], dv[:, sl]
                        acc[number(here[u][2 * t])] += jnp.where(low, k2, pltpu.roll(v2, SEGMENT, 1))
                        acc[number(here[u][2 * t + 1])] += jnp.where(low, pltpu.roll(k2, SEGMENT, 1), v2)
            o_ref[...] = grad_q

        def over(step):
            def narrow(g, _):
                step((1 + g) * (NARROW * SEGMENT // LANES), starts(1 + rest + g * NARROW, NARROW))
                return 0

            def broad(g, _):
                step(
                    (1 + small) * (NARROW * SEGMENT // LANES) + g * (WIDE * SEGMENT // LANES),
                    starts(1 + rest + small * NARROW + g * WIDE, WIDE),
                )
                return 0

            lax.fori_loop(0, small, narrow, 0)
            lax.fori_loop(0, wide, broad, 0)

        first(lambda slot, at: logits(slot, at, True))
        over(lambda slot, at: logits(slot, at, False))
        m_ref[...] = jnp.broadcast_to(jnp.max(m_ref[...], axis=-1, keepdims=True), m_ref.shape)
        first(weights)
        over(weights)
        total = jnp.sum(l_ref[...], axis=-1, keepdims=True)
        over_total = 1.0 / total
        output = (o_ref[...].T / total).astype(BF16).astype(F32)
        o_ref[...] = jnp.zeros_like(o_ref)
        for h in range(per_group):
            sl = slice(h * SEGMENT, (h + 1) * SEGMENT)
            g = grad_ref[pl.ds(base, SEGMENT), h * dim : (h + 1) * dim].astype(F32)
            g = (g * over_total[sl]).astype(BF16)
            dop[sl, :] = g
            delta = jnp.sum(g.astype(F32) * output[sl], axis=-1, keepdims=True)
            m_ref[sl, :] = jnp.broadcast_to(delta, (SEGMENT, 128))
        dot_t[...] = dop[...].astype(F32).T.astype(BF16)
        first(slopes)
        over(slopes)
        raw = o_ref[...].T
        for h in range(per_group):
            sl = slice(h * SEGMENT, (h + 1) * SEGMENT)
            q = query_ref[pl.ds(base, SEGMENT), h * dim : (h + 1) * dim].astype(F32)
            inverse = lax.rsqrt(jnp.mean(q * q, axis=-1, keepdims=True) + EPSILON)
            unit = q * inverse
            grad = raw[sl] * scale
            e = grad * gain
            dq = inverse * (e - unit * jnp.mean(e * unit, axis=-1, keepdims=True))
            out_ref[pl.ds(base, SEGMENT), h * dim : (h + 1) * dim] = dq.astype(BF16)
            query_part = query_part + jnp.sum((grad * unit).reshape(SEGMENT // 8, 8, dim), axis=0)
            terms = raw[sl] * qn[sl, :].astype(F32)
            all_part = all_part + jnp.sum(terms.reshape(SEGMENT // 8, 8, dim), axis=0)
        return query_part, all_part

    none = jnp.zeros((8, dim), F32)
    query_part, all_part = lax.fori_loop(0, blocks, one_block, (none, none))

    query_sum = jnp.sum(query_part, axis=0, keepdims=True)
    row = lax.broadcasted_iota(I32, (8, dim), 0)
    filled = jnp.where(row == jnp.where(is_text, 0, 1), query_sum, 0.0)
    gain_out[...] = jnp.where(row == 2, jnp.sum(all_part, axis=0, keepdims=True), filled)


def attention(lists, query_input, output_grad, query_gain, kv, qn, qt, sums):
    rows, columns = query_input.shape
    per_group = columns // 128
    stacked = SEGMENT * per_group
    segments = kv.shape[0] * 3
    slots = (segments + NARROW) * SEGMENT // LANES
    flat = kv.shape[0] * 384
    whole = pl.BlockSpec(memory_space=VMEM)
    return pl.pallas_call(
        functools.partial(attention_kernel, per_group, rows // SEGMENT),
        out_shape=(
            jax.ShapeDtypeStruct((rows, columns), BF16),
            VMEM((8, 128), F32),
            VMEM(sums.shape, F32),
        ),
        in_specs=[pl.BlockSpec(memory_space=pltpu.SMEM)] + [whole] * 7,
        out_specs=(whole,) * 3,
        input_output_aliases={7: 2},
        scratch_shapes=[
            VMEM((stacked, 128), BF16), VMEM((128, stacked), BF16),
            VMEM((slots, stacked, LANES), F32), VMEM((slots, stacked, LANES), BF16),
            VMEM((stacked, 128), F32), VMEM((stacked, 128), F32), VMEM((128, stacked), F32),
        ],
        compiler_params=pltpu.CompilerParams(vmem_limit_bytes=40 * MIB),
        name="attention",
    )(lists, query_input, output_grad, query_gain, kv.reshape(flat, 128), qn, qt, sums)


def reduce_kernel(
    part_ref, kv_ref, gain_part, key_hbm, gain_hbm, key_out, value_out, gain_out,
    key_ref, gain_ref, load_sem, sent, sib, work, half_b, full_b, half_a, full_a, sums,
    send_s, recv_s, send_hb, recv_hb, send_fb, recv_fb, send_a, recv_a, send_g, recv_g,
):
    y, x, z, core = position()
    scale = 1.0 / math.sqrt(128)

    def target(first, second):
        nx, nz = shifted(x, z, core, first, second)
        return device(y, nx, nz, core)

    sibling = device(y, x, z, 1 - core)
    ring_a = (target(1, 0), target(3, 0))
    ring_b = (target(0, 1), target(0, 3))
    lines = (
        (y * 2 + core, 8, lambda n: device(lax.div(n, 2), x, z, lax.rem(n, 2))),
        (x * 4 + z, 16, lambda n: device(y, lax.div(n, 4), lax.rem(n, 4), core)),
    )
    far_a, far_b = target(2, 0), target(0, 2)
    peers = [of(lax.rem(at + o, size)) for at, size, of in lines for o in range(1, size)]
    loads = [
        pltpu.make_async_copy(key_hbm, key_ref, load_sem.at[0]), pltpu.make_async_copy(gain_hbm, gain_ref, load_sem.at[1])
    ]
    for load in loads:
        load.start()
    wait_all = meet(peers)
    visit = [(first, second) for second in (2, 1, 3, 0) for first in (2, 1, 3, 0)]

    def chunk(first, second, on):
        nx, nz = shifted(x, z, on, first, second)
        return part_ref[pl.ds(place_of(nx, nz, on) * 3, 3)].reshape(2, 192, 128)

    for first, second in visit:
        sent[first, second] = chunk(first, second, 1 - core).astype(BF16)
    wait_all()
    started = []

    def send(src, dst, send_sem, recv_sem, to):
        copy = remote(src, dst, send_sem, recv_sem, to)
        copy.start()
        started.append(copy)

    def arrived(dst, recv_sem):
        remote(dst, dst, send_s.at[0], recv_sem, sibling).wait_recv()

    def gain_send(stage, value):
        at, size, of = lines[stage]
        sums[stage, at] = value
        for o in range(1, size):
            send(sums.at[stage, at], sums.at[stage, at], send_g.at[stage, o], recv_g.at[stage, at], of(lax.rem(at + o, size)))

    def gain_sum(stage):
        at, size, of = lines[stage]
        for o in range(1, size):
            n = lax.rem(at + o, size)
            arrived(sums.at[stage, n], recv_g.at[stage, n])
        total = sums[stage, 0]
        for n in range(1, size):
            total = total + sums[stage, n]
        return total

    for first, second in visit:
        n = first * 4 + second
        send(sent.at[first, second], sib.at[first, second], send_s.at[n], recv_s.at[n], sibling)

    def text_terms(i, part):
        mine, keys = [], []
        for j in range(3):
            mine.append(part_ref[i * 3 + j].astype(BF16))
            keys.append(kv_ref[i, 0, j * SEGMENT : (j + 1) * SEGMENT, :])
            keys.append(jnp.zeros_like(keys[-1]))
        return part + dot(jnp.concatenate(mine, axis=1), jnp.concatenate(keys, axis=0), 1, 0)

    text = lax.fori_loop(0, 16, text_terms, jnp.zeros((128, 128), F32), unroll=4)
    diagonal = lax.broadcasted_iota(I32, (128, 128), 0) == lax.broadcasted_iota(I32, (128, 128), 1)
    text_sum = jnp.sum(jnp.where(diagonal, text, 0.0), axis=0, keepdims=True)
    given = gain_part[...]
    slot = lax.broadcasted_iota(I32, (8, 128), 0)
    gain_send(0, jnp.where(slot == 2, text_sum, jnp.where(slot == 3, given[2:3] - text_sum, given)))

    def combine(first, second):
        n = first * 4 + second
        arrived(sib.at[first, second], recv_s.at[n])
        return chunk(first, second, core) + sib[first, second].astype(F32)

    for first in (2, 1, 3, 0):
        work[first, 2] = combine(first, 2).astype(BF16)
        if first in SUM_B:
            send(work.at[first, 2], half_b.at[first], send_hb.at[first, 0], recv_hb.at[first, 0], far_b)
        else:
            for half in (0, 1):
                send(work.at[first, 2, half], half_b.at[first, half], send_hb.at[first, half], recv_hb.at[first, half], ring_b[half])
    for first in (2, 1, 3, 0):
        for half, second in ((0, 1), (1, 3)):
            mine = combine(first, second)
            work[first, second] = mine.astype(BF16)
            if first not in SUM_B:
                arrived(half_b.at[first, half], recv_hb.at[first, half])
                work[first, second, half] = (mine[half] + half_b[first, half].astype(F32)).astype(BF16)
            send(work.at[first, second], full_b.at[first, half], send_fb.at[first, half], recv_fb.at[first, half], ring_b[half])

    def settled(first):
        mine = combine(first, 0)
        if first in SUM_B:
            arrived(half_b.at[first], recv_hb.at[first, 0])
            mine = mine + half_b[first].astype(F32)
        for half in (0, 1):
            arrived(full_b.at[first, half], recv_fb.at[first, half])
            mine = mine + full_b[first, half].astype(F32)
        return mine

    gain_send(1, gain_sum(0))
    work[2, 0] = settled(2).astype(BF16)
    if SUM_A:
        send(work.at[2, 0], half_a, send_a.at[0], recv_a.at[0], far_a)
    else:
        for half in (0, 1):
            send(work.at[2, 0, half], half_a.at[half], send_a.at[half], recv_a.at[half], ring_a[half])
    for half, first in ((0, 1), (1, 3)):
        mine = settled(first)
        work[first, 0] = mine.astype(BF16)
        if not SUM_A:
            arrived(half_a.at[half], recv_a.at[half])
            work[first, 0, half] = (mine[half] + half_a[half].astype(F32)).astype(BF16)
        send(work.at[first, 0], full_a.at[half], send_a.at[2 + half], recv_a.at[2 + half], ring_a[half])
    mine = settled(0)
    totals = gain_sum(1)
    for load in loads:
        load.wait()
    gain = gain_ref[...]
    tower = lax.rem(z, 2)
    row = lax.broadcasted_iota(I32, (8, 128), 0)
    query_sum = jnp.sum(jnp.where(row == tower, totals, 0.0), axis=0, keepdims=True)
    key_sum = jnp.sum(jnp.where(row == 2 + tower, totals, 0.0), axis=0, keepdims=True)
    gain_out[0:1, :] = query_sum
    gain_out[1:2, :] = key_sum * scale / gain
    if SUM_A:
        arrived(half_a, recv_a.at[0])
        mine = mine + half_a[...].astype(F32)
    for half in (0, 1):
        arrived(full_a.at[half], recv_a.at[2 + half])
        mine = mine + full_a[half].astype(F32)
    blocks = jnp.concatenate([mine[0], mine[1]], axis=0)
    blocks = [blocks[j * 128 : (j + 1) * 128].T for j in range(3)]
    grad_keys = jnp.concatenate([block[:SEGMENT] for block in blocks], axis=0)
    grad_values = jnp.concatenate([block[SEGMENT:] for block in blocks], axis=0)
    value_out[...] = grad_values.astype(BF16)
    keys = key_ref[...].astype(F32)
    inverse = lax.rsqrt(jnp.mean(keys * keys, axis=-1, keepdims=True) + EPSILON)
    unit = keys * inverse
    e = grad_keys * scale * gain
    key_out[...] = (inverse * (e - unit * jnp.mean(e * unit, axis=-1, keepdims=True))).astype(BF16)
    for copy in started:
        copy.wait_send()


def reduced(part, kv, gain_part, key_input, key_gain):
    rows, dim = key_input.shape
    whole = pl.BlockSpec(memory_space=VMEM)
    one = (2, rows, dim)
    return pl.pallas_call(
        reduce_kernel,
        out_shape=(
            VMEM((rows, dim), BF16),
            VMEM((rows, dim), BF16),
            VMEM((2, dim), F32),
        ),
        in_specs=[whole, whole, whole, HBM, HBM],
        out_specs=(whole,) * 3,
        scratch_shapes=[
            VMEM((rows, dim), BF16), VMEM((1, dim), F32), DMA((2,)), VMEM((4, 4, *one), BF16),
            VMEM((4, 4, *one), BF16), VMEM((4, 4, *one), BF16), VMEM((4, *one), BF16), VMEM((4, 2, *one), BF16),
            VMEM(one, BF16), VMEM((2, *one), BF16), VMEM((2, 16, 8, dim), F32),
            DMA((16,)), DMA((16,)), DMA((4, 2)), DMA((4, 2)), DMA((4, 2)), DMA((4, 2)), DMA((4,)), DMA((4,)),
            DMA((2, 16)), DMA((2, 16)),
        ],
        compiler_params=pltpu.CompilerParams(collective_id=1, has_side_effects=True, vmem_limit_bytes=16 * MIB),
        name="reduce_keys",
    )(part, kv, gain_part, key_input, key_gain)


def shards(
    query_input, key_input, value_input, output_grad, query_gain, key_gain, stripe_order, frame_index, cross_blocks
):
    kv, lists, queries, grads, gain, qn, qt, sums = gathered(
        key_input, value_input, key_gain, stripe_order[None], frame_index[None], cross_blocks,
        query_input, output_grad, query_gain,
    )
    query_grad, gain_part, part = attention(lists, queries, grads, gain, kv, qn, qt, sums)
    key_grad, value_grad, gain_grads = reduced(part, kv, gain_part, key_input, key_gain)
    return query_grad, key_grad, value_grad, gain_grads[:, None, :]


def solution(mesh):
    split = Mesh(mesh.devices.reshape(mesh.shape["heads"], mesh.shape["tower"], 2, 4, 2), AXES)
    in_specs = (
        P(TOWER_BLK, "heads"),
        P(TOWER_BLK, "heads"),
        P(TOWER_BLK, "heads"),
        P(TOWER_BLK, "heads"),
        P("tower", None),
        P("tower", None),
        P(),
        P(),
        P(),
    )
    out_specs = (
        P(TOWER_BLK, "heads"),
        P(TOWER_BLK, "heads"),
        P(TOWER_BLK, "heads"),
        P(None, "tower", None),
    )
    return jax.shard_map(shards, mesh=split, in_specs=in_specs, out_specs=out_specs, check_vma=False)
```

```python
import functools
import math

import jax
import jax.numpy as jnp
from jax import lax
from jax.experimental import pallas as pl
from jax.experimental.pallas import tpu as pltpu
from jax.sharding import Mesh
from jax.sharding import PartitionSpec as P

SEGMENT = 64
AXES = ("heads", "tower", "blk_0", "blk_1", "blk_2")
TOWER_BLK = ("tower", "blk_0", "blk_1", "blk_2")
EPSILON = 1e-06
NEGATIVE = -1e30
LOG2E = 1.4426950408889634
WIDE, NARROW, SMALL, LANES = 24, 12, 4, 256
MESH = pl.DeviceIdType.MESH
HBM = pl.BlockSpec(memory_space=pltpu.HBM)
MIB = 1024 * 1024
DIRECT_A, DIRECT_B, LATE = True, (2,), False
SUM_A, SUM_B = True, ()
STACKED = 448
MOST, CHUNKS, ROWS, SUMS = 67_043_328, 32 * 2 * 192 * 128 * 2, 3 * 192 * 896 * 2 + 3 * 128 * 512 * 2, 96 * 128 * 128 * 4
VMEM = pltpu.VMEM
DMA = pltpu.SemaphoreType.DMA
F32, BF16, I32 = jnp.float32, jnp.bfloat16, jnp.int32


def dot(a, b, left, right):
    return lax.dot_general(a, b, (((left,), (right,)), ((), ())), preferred_element_type=F32)


def position():
    z = lax.axis_index("blk_0") * 2 + lax.axis_index("tower")
    return lax.axis_index("heads"), lax.axis_index("blk_1"), z, lax.axis_index("blk_2")


def device(y, x, z, core):
    return (y, lax.rem(z, 2), lax.div(z, 2), x, core)


def place_of(x, z, core):
    return lax.rem(z, 2) * 16 + lax.div(z, 2) * 8 + x * 2 + core


def shifted(x, z, core, first, second):
    nx = lax.rem(x + (1 - core) * first + core * second, 4)
    nz = lax.rem(z + core * first + (1 - core) * second, 4)
    return nx, nz


def remote(src, dst, send, recv, target):
    return pltpu.make_async_remote_copy(
        src_ref=src, dst_ref=dst, send_sem=send, recv_sem=recv, device_id=target, device_id_type=MESH
    )


def meet(targets):
    barrier = pltpu.get_barrier_semaphore()
    for target in targets:
        pl.semaphore_signal(barrier, inc=1, device_id=target, device_id_type=MESH)
    return lambda: pl.semaphore_wait(barrier, len(targets))


def gather_kernel(
    key_hbm, value_hbm, gain_hbm, order_hbm, frame_hbm, cross_hbm, query_hbm, grad_hbm, query_gain_hbm,
    all_ref, list_ref, query_out, grad_out, query_gain_out, qn_out, qt_out, acc_out,
    key_ref, gain_ref, order_ref, frame_ref, cross_ref, mine, load_sem, own_sem, send_a, recv_a, send_b, recv_b, send_s, recv_s,
):
    y, x, z, core = position()

    def target(first, second):
        nx, nz = shifted(x, z, core, first, second)
        return device(y, nx, nz, core)

    def chunk(first, second):
        nx, nz = shifted(x, z, core, first, second)
        return place_of(nx, nz, core)

    loads = [
        pltpu.make_async_copy(src, dst, load_sem.at[n])
        for n, (src, dst) in enumerate((
            (key_hbm, key_ref),
            (gain_hbm, gain_ref),
            (value_hbm, mine.at[1]),
            (order_hbm, order_ref),
            (frame_hbm, frame_ref),
            (cross_hbm, cross_ref),
            (query_hbm, query_out),
            (grad_hbm, grad_out),
            (query_gain_hbm, query_gain_out),
        ))
    ]
    for load in loads:
        load.start()
    sibling = device(y, x, z, 1 - core)
    ring_a = (target(1, 0), target(3, 0))
    ring_b = (target(0, 1), target(0, 3))
    far_a, far_b = target(2, 0), target(0, 2)
    wait_all = meet((*ring_a, *ring_b, far_a, far_b, sibling))
    loads[0].wait()
    loads[1].wait()
    keys = key_ref[...].astype(F32)
    inverse = lax.rsqrt(jnp.mean(keys * keys, axis=-1, keepdims=True) + EPSILON)
    mine[0] = (keys * inverse * gain_ref[...]).astype(BF16)
    me = place_of(x, z, core)
    own = pltpu.make_async_copy(mine, all_ref.at[me], own_sem)
    started = []

    def send(src, dst, send_sem, recv_sem, to):
        copy = remote(src, dst, send_sem, recv_sem, to)
        copy.start()
        started.append(copy)

    def arrived(dst, recv_sem):
        remote(dst, dst, send_s.at[0], recv_sem, sibling).wait_recv()

    def spread(first, src):
        at = all_ref.at[chunk(first, 0)]
        send(src, at, send_b.at[first, 0], recv_b.at[first, 1], ring_b[0])
        send(src, at, send_b.at[first, 1], recv_b.at[first, 0], ring_b[1])
        if first in DIRECT_B:
            send(src, at, send_b.at[first, 2], recv_b.at[first, 2], far_b)

    def share(first, second, src):
        n = first * 4 + second
        send(src, all_ref.at[chunk(first, second)], send_s.at[n], recv_s.at[n], sibling)

    loads[2].wait()
    wait_all()
    own.start()
    send(mine, all_ref.at[me], send_a.at[0], recv_a.at[1], ring_a[0])
    send(mine, all_ref.at[me], send_a.at[1], recv_a.at[0], ring_a[1])
    if DIRECT_A:
        send(mine, all_ref.at[me], send_a.at[2], recv_a.at[2], far_a)
    if not LATE:
        spread(0, mine)
    share(0, 0, mine)

    lane = lax.broadcasted_iota(I32, (1, 128), 1)
    down = lax.broadcasted_iota(I32, (128, 128), 0)
    across = lax.broadcasted_iota(I32, (128, 128), 1)
    for load in loads[3:6]:
        load.wait()
    order = jnp.concatenate([order_ref[...], jnp.zeros((1, 32), I32)], axis=1)
    frame = jnp.concatenate([frame_ref[...], jnp.zeros((1, 80), I32)], axis=1)
    frame = jnp.where((lane >= 48) & (lane < 96), pltpu.roll(frame, 48, 1), -1)
    below = (across < down).astype(F32)
    start_of = (lax.shift_right_logical(down * 171, 9) * 384 + (down - 3 * lax.shift_right_logical(down * 171, 9)) * 64)
    image = me >= 16
    list_ref[...] = jnp.zeros_like(list_ref)
    counts = jnp.where(lane == 3, jnp.where(image, 0, 1), 0)
    for b in range(3):
        block = me * 3 + b
        here = lane == block
        slot = jnp.sum(jnp.where(here, order, 0), axis=-1, keepdims=True)
        seen = jnp.sum(jnp.where(here, frame, 0), axis=-1, keepdims=True)
        same = (lane >= 48) == image
        near = (order <= slot) | ((frame == seen) & (seen >= 0))
        crossing = jnp.concatenate([cross_ref[pl.ds(block, 1), :], jnp.zeros((1, 32), I32)], axis=1)
        opened = same | (crossing == 1)
        others = (near & opened & (lane < 96) & (lane != block)).astype(F32)
        column = jnp.broadcast_to(others, (128, 128)).T
        at = dot(below, column, 1, 0).astype(I32) + 1
        chosen = (column > 0.5) & (at == across)
        listed = jnp.sum(jnp.where(chosen, start_of, 0), axis=0, keepdims=True)
        first_start = me * 384 + b * 64
        list_ref[b : b + 1, :] = jnp.where(lane == 0, first_start, listed)
        count = 1 + jnp.sum(others, axis=-1, keepdims=True).astype(I32)
        counts = jnp.where(lane == b, count, counts)
    list_ref[3:4, :] = counts

    for load in loads[6:]:
        load.wait()
    query_gain = query_gain_out[...]
    per_group = query_out.shape[1] // 128
    for b in range(3):
        for h in range(per_group):
            q = query_out[b * SEGMENT : (b + 1) * SEGMENT, h * 128 : (h + 1) * 128].astype(F32)
            inverse = lax.rsqrt(jnp.mean(q * q, axis=-1, keepdims=True) + EPSILON)
            qn_out[b, h * SEGMENT : (h + 1) * SEGMENT, :] = (q * inverse * query_gain).astype(BF16)
        qt_out[b] = qn_out[b].astype(F32).T.astype(BF16)

    def clear(i, _):
        acc_out[i] = jnp.zeros((128, 128), F32)
        return 0

    lax.fori_loop(0, acc_out.shape[0], clear, 0)

    def from_a(slot, first, half, to, forward_recv):
        at = all_ref.at[chunk(first, 0)]
        arrived(at, recv_a.at[slot])
        if not DIRECT_A:
            send(at.at[half], at.at[half], send_a.at[2 + half], recv_a.at[forward_recv], to)
        spread(first, at)
        share(first, 0, at)

    def from_b(first, slot, second, half, to):
        at = all_ref.at[chunk(first, second)]
        arrived(at, recv_b.at[first, slot])
        if first not in DIRECT_B:
            send(at.at[half], at.at[half], send_b.at[first, 2 + half], recv_b.at[first, 2 + half], to)
        share(first, second, at)

    def both_b(first):
        from_b(first, 0, 1, 0, ring_b[1])
        from_b(first, 1, 3, 1, ring_b[0])

    from_a(0, 1, 0, ring_a[1], 2)
    from_a(1, 3, 1, ring_a[0], 3)
    if LATE:
        spread(0, mine)
    if not DIRECT_A:
        both_b(0)
    at = all_ref.at[chunk(2, 0)]
    if DIRECT_A:
        arrived(at, recv_a.at[2])
    else:
        arrived(at.at[0], recv_a.at[2])
        arrived(at.at[1], recv_a.at[3])
    spread(2, at)
    share(2, 0, at)
    if DIRECT_A:
        both_b(0)
    both_b(1)
    both_b(3)
    both_b(2)
    for first in (0, 1, 3, 2):
        at = all_ref.at[chunk(first, 2)]
        if first in DIRECT_B:
            arrived(at, recv_b.at[first, 2])
        else:
            arrived(at.at[0], recv_b.at[first, 2])
            arrived(at.at[1], recv_b.at[first, 3])
        share(first, 2, at)
    own.wait()
    for copy in started:
        copy.wait_send()
    for n in range(16):
        nx, nz = shifted(x, z, 1 - core, n // 4, n % 4)
        arrived(all_ref.at[place_of(nx, nz, 1 - core)], recv_s.at[n])


def gathered(key_input, value_input, key_gain, order, frame, cross, query_input, output_grad, query_gain):
    rows, dim = key_input.shape
    whole = pl.BlockSpec(memory_space=VMEM)
    return pl.pallas_call(
        gather_kernel,
        out_shape=(
            VMEM((32, 2, rows, dim), BF16), VMEM((8, 128), I32), VMEM(query_input.shape, BF16), VMEM(query_input.shape, BF16),
            VMEM((1, dim), F32), VMEM((3, STACKED, dim), BF16), VMEM((3, dim, STACKED), BF16), VMEM((96, dim, 128), F32),
        ),
        in_specs=[HBM] * 9,
        out_specs=(pl.BlockSpec(memory_space=pl.ANY), whole, *(whole,) * 6),
        scratch_shapes=[
            VMEM((rows, dim), BF16), VMEM((1, dim), F32), VMEM(order.shape, I32), VMEM(frame.shape, I32),
            VMEM(cross.shape, I32), VMEM((2, rows, dim), BF16), DMA((9,)), DMA, DMA((4,)), DMA((4,)), DMA((4, 4)), DMA((4, 4)), DMA((16,)), DMA((16,)),
        ],
        compiler_params=pltpu.CompilerParams(collective_id=0, has_side_effects=True, vmem_limit_bytes=MOST - CHUNKS - ROWS - SUMS - 24 * 1024),
        cost_estimate=pl.CostEstimate(flops=0, bytes_accessed=60_000_000, transcendentals=0),
        name="gather_keys",
    )(key_input, value_input, key_gain, order, frame, cross, query_input, output_grad, query_gain)


def attention_kernel(
    per_group, blocks, list_ref, query_ref, grad_ref, gain_ref, kv_ref, qn_ref, qt_ref, clear_ref,
    out_ref, gain_out, acc,
    dop, dot_t, s_ref, w_ref, m_ref, l_ref, o_ref,
):
    dim = 128
    rows = SEGMENT * per_group
    log_scale = LOG2E / math.sqrt(dim)
    scale = 1.0 / math.sqrt(dim)
    is_text = list_ref[3, 3] == 1
    gain = gain_ref[...]

    def one_block(b, parts):
        query_part, all_part = parts
        base = pl.multiple_of(b * SEGMENT, SEGMENT)
        count = list_ref[3, b] - 1
        wide = lax.div(count, WIDE)
        small = lax.div(lax.rem(count, WIDE), NARROW)
        rest = lax.rem(count, NARROW)
        qn, qt = qn_ref.at[b], qt_ref.at[b]
        m_ref[...] = jnp.full_like(m_ref, NEGATIVE)
        l_ref[...] = jnp.zeros_like(l_ref)
        o_ref[...] = jnp.zeros_like(o_ref)

        def starts(first, size):
            return [pl.multiple_of(list_ref[b, first + j], SEGMENT) for j in range(size)]

        def first(step):
            def at(size):
                ps = [0] + [jnp.where(j <= rest, j, 0) for j in range(1, size)]
                return [pl.multiple_of(list_ref[b, p], SEGMENT) for p in ps]

            @pl.when(rest < SMALL)
            def _():
                step(0, at(SMALL))

            @pl.when(rest >= SMALL)
            def _():
                step(0, at(NARROW))

        def tile(at, offset):
            return jnp.concatenate([kv_ref[pl.ds(s + offset, SEGMENT), :] for s in at], axis=0)

        def number(start):
            return lax.div(start, 384) * 3 + lax.div(lax.rem(start, 384), SEGMENT)

        def logits(slot, at, masked):
            width = len(at) * SEGMENT
            s = dot(qn[...], tile(at, 0), 1, 1) * log_scale
            if masked:
                lane = lax.broadcasted_iota(I32, (rows, width), 1)
                row = lax.broadcasted_iota(I32, (rows, width), 0)
                limit = lax.rem(row, SEGMENT) + jnp.where(is_text, 0, SEGMENT)
                ok = (lane < (rest + 1) * SEGMENT) & ((lane >= SEGMENT) | (lane <= limit))
                s = jnp.where(ok, s, NEGATIVE)
            top = m_ref[...]
            for t in range(width // 128):
                top = jnp.maximum(top, s[:, t * 128 : (t + 1) * 128])
            m_ref[...] = top
            for t in range(width // LANES):
                s_ref[slot + t] = s[:, t * LANES : (t + 1) * LANES]

        def weights(slot, at):
            top = m_ref[...]
            total = l_ref[...]
            out = o_ref[...]
            tiles = len(at) * SEGMENT // LANES
            each = LANES // SEGMENT
            values = [tile(at[u * each : (u + 1) * each], 192).T for u in range(tiles)]
            ready = []
            for u in range(tiles + 1):
                if u < tiles:
                    parts = []
                    for t in range(LANES // 128):
                        w = jnp.exp2(s_ref[slot + u, :, t * 128 : (t + 1) * 128] - top)
                        total = total + w
                        parts.append(w.astype(BF16))
                    w = jnp.concatenate(parts, axis=1)
                    w_ref[slot + u] = w
                    ready.append(w)
                if u > 0:
                    out = out + dot(values[u - 1], ready[u - 1], 1, 1)
            l_ref[...] = total
            o_ref[...] = out

        def slopes(slot, at):
            delta = m_ref[...]
            low = lax.broadcasted_iota(I32, (dim, 128), 1) < SEGMENT
            tiles = len(at) * SEGMENT // LANES
            each = LANES // SEGMENT
            here = [at[u * each : (u + 1) * each] for u in range(tiles)]
            pushes, dvs, done = {}, {}, {}
            grad_q = o_ref[...]
            for step in range(tiles + 2):
                if step < tiles:
                    pushes[step] = dot(dop[...], tile(here[step], 192), 1, 1)
                    dvs[step] = dot(dot_t[...], w_ref[slot + step], 1, 0)
                u = step - 1
                if 0 <= u < tiles:
                    w = w_ref[slot + u]
                    parts = []
                    for t in range(LANES // 128):
                        sl = slice(t * 128, (t + 1) * 128)
                        parts.append((w[:, sl].astype(F32) * (pushes[u][:, sl] - delta)).astype(BF16))
                    d = jnp.concatenate(parts, axis=1)
                    grad_q = grad_q + dot(tile(here[u], 0).T, d, 1, 1)
                    done[u] = dot(qt[...], d, 1, 0), dvs[u]
                u = step - 2
                if 0 <= u < tiles:
                    dk, dv = done[u]
                    for t in range(LANES // 128):
                        sl = slice(t * 128, (t + 1) * 128)
                        k2, v2 = dk[:, sl], dv[:, sl]
                        acc[number(here[u][2 * t])] += jnp.where(low, k2, pltpu.roll(v2, SEGMENT, 1))
                        acc[number(here[u][2 * t + 1])] += jnp.where(low, pltpu.roll(k2, SEGMENT, 1), v2)
            o_ref[...] = grad_q

        def over(step):
            def narrow(g, _):
                step((1 + g) * (NARROW * SEGMENT // LANES), starts(1 + rest + g * NARROW, NARROW))
                return 0

            def broad(g, _):
                step(
                    (1 + small) * (NARROW * SEGMENT // LANES) + g * (WIDE * SEGMENT // LANES),
                    starts(1 + rest + small * NARROW + g * WIDE, WIDE),
                )
                return 0

            lax.fori_loop(0, small, narrow, 0)
            lax.fori_loop(0, wide, broad, 0)

        first(lambda slot, at: logits(slot, at, True))
        over(lambda slot, at: logits(slot, at, False))
        m_ref[...] = jnp.broadcast_to(jnp.max(m_ref[...], axis=-1, keepdims=True), m_ref.shape)
        first(weights)
        over(weights)
        total = jnp.sum(l_ref[...], axis=-1, keepdims=True)
        over_total = 1.0 / total
        output = (o_ref[...].T / total).astype(BF16).astype(F32)
        o_ref[...] = jnp.zeros_like(o_ref)
        for h in range(per_group):
            sl = slice(h * SEGMENT, (h + 1) * SEGMENT)
            g = grad_ref[pl.ds(base, SEGMENT), h * dim : (h + 1) * dim].astype(F32)
            g = (g * over_total[sl]).astype(BF16)
            dop[sl, :] = g
            delta = jnp.sum(g.astype(F32) * output[sl], axis=-1, keepdims=True)
            m_ref[sl, :] = jnp.broadcast_to(delta, (SEGMENT, 128))
        dot_t[...] = dop[...].astype(F32).T.astype(BF16)
        first(slopes)
        over(slopes)
        raw = o_ref[...].T
        for h in range(per_group):
            sl = slice(h * SEGMENT, (h + 1) * SEGMENT)
            q = query_ref[pl.ds(base, SEGMENT), h * dim : (h + 1) * dim].astype(F32)
            inverse = lax.rsqrt(jnp.mean(q * q, axis=-1, keepdims=True) + EPSILON)
            unit = q * inverse
            grad = raw[sl] * scale
            e = grad * gain
            dq = inverse * (e - unit * jnp.mean(e * unit, axis=-1, keepdims=True))
            out_ref[pl.ds(base, SEGMENT), h * dim : (h + 1) * dim] = dq.astype(BF16)
            query_part = query_part + jnp.sum((grad * unit).reshape(SEGMENT // 8, 8, dim), axis=0)
            terms = raw[sl] * qn[sl, :].astype(F32)
            all_part = all_part + jnp.sum(terms.reshape(SEGMENT // 8, 8, dim), axis=0)
        return query_part, all_part

    none = jnp.zeros((8, dim), F32)
    query_part, all_part = lax.fori_loop(0, blocks, one_block, (none, none))

    query_sum = jnp.sum(query_part, axis=0, keepdims=True)
    row = lax.broadcasted_iota(I32, (8, dim), 0)
    filled = jnp.where(row == jnp.where(is_text, 0, 1), query_sum, 0.0)
    gain_out[...] = jnp.where(row == 2, jnp.sum(all_part, axis=0, keepdims=True), filled)


def attention(lists, query_input, output_grad, query_gain, kv, qn, qt, sums):
    rows, columns = query_input.shape
    per_group = columns // 128
    stacked = SEGMENT * per_group
    segments = kv.shape[0] * 3
    slots = (segments + NARROW) * SEGMENT // LANES
    flat = kv.shape[0] * 384
    whole = pl.BlockSpec(memory_space=VMEM)
    return pl.pallas_call(
        functools.partial(attention_kernel, per_group, rows // SEGMENT),
        out_shape=(
            jax.ShapeDtypeStruct((rows, columns), BF16),
            VMEM((8, 128), F32),
            VMEM(sums.shape, F32),
        ),
        in_specs=[pl.BlockSpec(memory_space=pltpu.SMEM)] + [whole] * 7,
        out_specs=(whole,) * 3,
        input_output_aliases={7: 2},
        scratch_shapes=[
            VMEM((stacked, 128), BF16), VMEM((128, stacked), BF16),
            VMEM((slots, stacked, LANES), F32), VMEM((slots, stacked, LANES), BF16),
            VMEM((stacked, 128), F32), VMEM((stacked, 128), F32), VMEM((128, stacked), F32),
        ],
        compiler_params=pltpu.CompilerParams(vmem_limit_bytes=40 * MIB),
        name="attention",
    )(lists, query_input, output_grad, query_gain, kv.reshape(flat, 128), qn, qt, sums)


def reduce_kernel(
    part_ref, kv_ref, gain_part, key_hbm, gain_hbm, key_out, value_out, gain_out,
    key_ref, gain_ref, load_sem, sent, sib, work, half_b, full_b, half_a, full_a, sums,
    send_s, recv_s, send_hb, recv_hb, send_fb, recv_fb, send_a, recv_a, send_g, recv_g,
):
    y, x, z, core = position()
    scale = 1.0 / math.sqrt(128)

    def target(first, second):
        nx, nz = shifted(x, z, core, first, second)
        return device(y, nx, nz, core)

    sibling = device(y, x, z, 1 - core)
    ring_a = (target(1, 0), target(3, 0))
    ring_b = (target(0, 1), target(0, 3))
    lines = (
        (y * 2 + core, 8, lambda n: device(lax.div(n, 2), x, z, lax.rem(n, 2))),
        (x * 4 + z, 16, lambda n: device(y, lax.div(n, 4), lax.rem(n, 4), core)),
    )
    far_a, far_b = target(2, 0), target(0, 2)
    peers = [of(lax.rem(at + o, size)) for at, size, of in lines for o in range(1, size)]
    loads = [
        pltpu.make_async_copy(key_hbm, key_ref, load_sem.at[0]), pltpu.make_async_copy(gain_hbm, gain_ref, load_sem.at[1])
    ]
    for load in loads:
        load.start()
    wait_all = meet(peers)
    visit = [(first, second) for second in (2, 1, 3, 0) for first in (2, 1, 3, 0)]

    def chunk(first, second, on):
        nx, nz = shifted(x, z, on, first, second)
        return part_ref[pl.ds(place_of(nx, nz, on) * 3, 3)].reshape(2, 192, 128)

    def round_down(part):
        for first, second in part:
            sent[first, second] = chunk(first, second, 1 - core).astype(BF16)

    round_down(visit[:4])
    wait_all()
    started = []

    def send(src, dst, send_sem, recv_sem, to):
        copy = remote(src, dst, send_sem, recv_sem, to)
        copy.start()
        started.append(copy)

    def arrived(dst, recv_sem):
        remote(dst, dst, send_s.at[0], recv_sem, sibling).wait_recv()

    def gain_send(stage, value):
        at, size, of = lines[stage]
        sums[stage, at] = value
        for o in range(1, size):
            send(sums.at[stage, at], sums.at[stage, at], send_g.at[stage, o], recv_g.at[stage, at], of(lax.rem(at + o, size)))

    def gain_sum(stage):
        at, size, of = lines[stage]
        for o in range(1, size):
            n = lax.rem(at + o, size)
            arrived(sums.at[stage, n], recv_g.at[stage, n])
        total = sums[stage, 0]
        for n in range(1, size):
            total = total + sums[stage, n]
        return total

    def share(part):
        for first, second in part:
            n = first * 4 + second
            send(sent.at[first, second], sib.at[first, second], send_s.at[n], recv_s.at[n], sibling)

    share(visit[:4])
    round_down(visit[4:12])
    share(visit[4:8])
    round_down(visit[12:])
    share(visit[8:])

    def text_terms(i, part):
        mine, keys = [], []
        for j in range(3):
            mine.append(part_ref[i * 3 + j].astype(BF16))
            keys.append(kv_ref[i, 0, j * SEGMENT : (j + 1) * SEGMENT, :])
            keys.append(jnp.zeros_like(keys[-1]))
        return part + dot(jnp.concatenate(mine, axis=1), jnp.concatenate(keys, axis=0), 1, 0)

    text = lax.fori_loop(0, 16, text_terms, jnp.zeros((128, 128), F32), unroll=4)
    diagonal = lax.broadcasted_iota(I32, (128, 128), 0) == lax.broadcasted_iota(I32, (128, 128), 1)
    text_sum = jnp.sum(jnp.where(diagonal, text, 0.0), axis=0, keepdims=True)
    given = gain_part[...]
    slot = lax.broadcasted_iota(I32, (8, 128), 0)
    gain_send(0, jnp.where(slot == 2, text_sum, jnp.where(slot == 3, given[2:3] - text_sum, given)))

    def combine(first, second):
        n = first * 4 + second
        arrived(sib.at[first, second], recv_s.at[n])
        return chunk(first, second, core) + sib[first, second].astype(F32)

    for first in (2, 1, 3, 0):
        work[first, 2] = combine(first, 2).astype(BF16)
        if first in SUM_B:
            send(work.at[first, 2], half_b.at[first], send_hb.at[first, 0], recv_hb.at[first, 0], far_b)
        else:
            for half in (0, 1):
                send(work.at[first, 2, half], half_b.at[first, half], send_hb.at[first, half], recv_hb.at[first, half], ring_b[half])
    for first in (2, 1, 3, 0):
        for half, second in ((0, 1), (1, 3)):
            mine = combine(first, second)
            work[first, second] = mine.astype(BF16)
            if first not in SUM_B:
                arrived(half_b.at[first, half], recv_hb.at[first, half])
                work[first, second, half] = (mine[half] + half_b[first, half].astype(F32)).astype(BF16)
            send(work.at[first, second], full_b.at[first, half], send_fb.at[first, half], recv_fb.at[first, half], ring_b[half])

    def settled(first):
        mine = combine(first, 0)
        if first in SUM_B:
            arrived(half_b.at[first], recv_hb.at[first, 0])
            mine = mine + half_b[first].astype(F32)
        for half in (0, 1):
            arrived(full_b.at[first, half], recv_fb.at[first, half])
            mine = mine + full_b[first, half].astype(F32)
        return mine

    gain_send(1, gain_sum(0))
    work[2, 0] = settled(2).astype(BF16)
    if SUM_A:
        send(work.at[2, 0], half_a, send_a.at[0], recv_a.at[0], far_a)
    else:
        for half in (0, 1):
            send(work.at[2, 0, half], half_a.at[half], send_a.at[half], recv_a.at[half], ring_a[half])
    for half, first in ((0, 1), (1, 3)):
        mine = settled(first)
        work[first, 0] = mine.astype(BF16)
        if not SUM_A:
            arrived(half_a.at[half], recv_a.at[half])
            work[first, 0, half] = (mine[half] + half_a[half].astype(F32)).astype(BF16)
        send(work.at[first, 0], full_a.at[half], send_a.at[2 + half], recv_a.at[2 + half], ring_a[half])
    mine = settled(0)
    totals = gain_sum(1)
    for load in loads:
        load.wait()
    gain = gain_ref[...]
    tower = lax.rem(z, 2)
    row = lax.broadcasted_iota(I32, (8, 128), 0)
    query_sum = jnp.sum(jnp.where(row == tower, totals, 0.0), axis=0, keepdims=True)
    key_sum = jnp.sum(jnp.where(row == 2 + tower, totals, 0.0), axis=0, keepdims=True)
    gain_out[0:1, :] = query_sum
    gain_out[1:2, :] = key_sum * scale / gain
    if SUM_A:
        arrived(half_a, recv_a.at[0])
        mine = mine + half_a[...].astype(F32)
    for half in (0, 1):
        arrived(full_a.at[half], recv_a.at[2 + half])
        mine = mine + full_a[half].astype(F32)
    blocks = jnp.concatenate([mine[0], mine[1]], axis=0)
    blocks = [blocks[j * 128 : (j + 1) * 128].T for j in range(3)]
    grad_keys = jnp.concatenate([block[:SEGMENT] for block in blocks], axis=0)
    grad_values = jnp.concatenate([block[SEGMENT:] for block in blocks], axis=0)
    value_out[...] = grad_values.astype(BF16)
    keys = key_ref[...].astype(F32)
    inverse = lax.rsqrt(jnp.mean(keys * keys, axis=-1, keepdims=True) + EPSILON)
    unit = keys * inverse
    e = grad_keys * scale * gain
    key_out[...] = (inverse * (e - unit * jnp.mean(e * unit, axis=-1, keepdims=True))).astype(BF16)
    for copy in started:
        copy.wait_send()


def reduced(part, kv, gain_part, key_input, key_gain):
    rows, dim = key_input.shape
    whole = pl.BlockSpec(memory_space=VMEM)
    one = (2, rows, dim)
    return pl.pallas_call(
        reduce_kernel,
        out_shape=(
            VMEM((rows, dim), BF16),
            VMEM((rows, dim), BF16),
            VMEM((2, dim), F32),
        ),
        in_specs=[whole, whole, whole, HBM, HBM],
        out_specs=(whole,) * 3,
        scratch_shapes=[
            VMEM((rows, dim), BF16), VMEM((1, dim), F32), DMA((2,)), VMEM((4, 4, *one), BF16),
            VMEM((4, 4, *one), BF16), VMEM((4, 4, *one), BF16), VMEM((4, *one), BF16), VMEM((4, 2, *one), BF16),
            VMEM(one, BF16), VMEM((2, *one), BF16), VMEM((2, 16, 8, dim), F32),
            DMA((16,)), DMA((16,)), DMA((4, 2)), DMA((4, 2)), DMA((4, 2)), DMA((4, 2)), DMA((4,)), DMA((4,)),
            DMA((2, 16)), DMA((2, 16)),
        ],
        compiler_params=pltpu.CompilerParams(collective_id=1, has_side_effects=True, vmem_limit_bytes=16 * MIB),
        name="reduce_keys",
    )(part, kv, gain_part, key_input, key_gain)


def shards(
    query_input, key_input, value_input, output_grad, query_gain, key_gain, stripe_order, frame_index, cross_blocks
):
    kv, lists, queries, grads, gain, qn, qt, sums = gathered(
        key_input, value_input, key_gain, stripe_order[None], frame_index[None], cross_blocks,
        query_input, output_grad, query_gain,
    )
    query_grad, gain_part, part = attention(lists, queries, grads, gain, kv, qn, qt, sums)
    key_grad, value_grad, gain_grads = reduced(part, kv, gain_part, key_input, key_gain)
    return query_grad, key_grad, value_grad, gain_grads[:, None, :]


def solution(mesh):
    split = Mesh(mesh.devices.reshape(mesh.shape["heads"], mesh.shape["tower"], 2, 4, 2), AXES)
    in_specs = (
        P(TOWER_BLK, "heads"),
        P(TOWER_BLK, "heads"),
        P(TOWER_BLK, "heads"),
        P(TOWER_BLK, "heads"),
        P("tower", None),
        P("tower", None),
        P(),
        P(),
        P(),
    )
    out_specs = (
        P(TOWER_BLK, "heads"),
        P(TOWER_BLK, "heads"),
        P(TOWER_BLK, "heads"),
        P(None, "tower", None),
    )
    return jax.shard_map(shards, mesh=split, in_specs=in_specs, out_specs=out_specs, check_vma=False)
```
